128 devices in a mesh: wide: 64 (over y, z, x_hi, core), narrow: 2 (over x_lo).
Axes of the slice: x: 4 (x_hi: 2, x_lo: 2; x = x_hi * 2 + x_lo), y: 4, z: 4, core: 2. Of those that a mesh axis runs over, the one named last changes fastest.
Arguments:
- tokens: bfloat16 [16384, 1152], P(('wide', 'narrow')), may hold values from -6 to 6
- doc_ids: int32 [16384], P(('wide', 'narrow')), may hold values from 0 to 127, never falling along the last dimension, each value on 1 to 256 neighbouring positions
- keep: int32 [16384], P(('wide', 'narrow')), may hold values from 0 to 1
- attention_gain: bfloat16 [1152], P(('wide', 'narrow')), may hold values from 0.5 to 1.5
- query_weight: bfloat16 [1152, 1152], P(('wide', 'narrow')), may hold values from -0.1875 to 0.1875
- key_weight: bfloat16 [1152, 384], P(('wide', 'narrow')), may hold values from -0.1875 to 0.1875
- value_weight: bfloat16 [1152, 384], P(('wide', 'narrow')), may hold values from -0.1875 to 0.1875
- out_weight: bfloat16 [1152, 1152], P(('wide', 'narrow')), may hold values from -0.5 to 0.5
- feed_gain: bfloat16 [1152], P(('wide', 'narrow')), may hold values from 0.5 to 1.5
- gate_weight: bfloat16 [1152, 3072], P(('wide', 'narrow')), may hold values from -0.1875 to 0.1875
- up_weight: bfloat16 [1152, 3072], P(('wide', 'narrow')), may hold values from -0.1875 to 0.1875
- down_weight: bfloat16 [3072, 1152], P(('wide', 'narrow')), may hold values from -0.21875 to 0.21875
- cotangent: float32 [16384, 1152], P(('wide', 'narrow')), may hold values from -6 to 6
Outputs:
- mixed: bfloat16 [16384, 1152], P(('wide', 'narrow'))
- back_tokens: float32 [16384, 1152], P(('wide', 'narrow'))
- back_attention_gain: float32 [1152], P(('wide', 'narrow'))
- back_query: float32 [1152, 1152], P(('wide', 'narrow'))
- back_key: float32 [1152, 384], P(('wide', 'narrow'))
- back_value: float32 [1152, 384], P(('wide', 'narrow'))
- back_out: float32 [1152, 1152], P(('wide', 'narrow'))
- back_feed_gain: float32 [1152], P(('wide', 'narrow'))
- back_gate: float32 [1152, 3072], P(('wide', 'narrow'))
- back_up: float32 [1152, 3072], P(('wide', 'narrow'))
- back_down: float32 [3072, 1152], P(('wide', 'narrow'))
The draws below stay inside these ranges and needn't reach their ends.
Inputs may be any that keep to these rules, and one draw needn't show every extreme that they name: `doc_ids`: ids never fall along the rows; each document covers 1 to 256 rows, one exactly 256.
All inputs are finite; a program needn't handle non-finite values.
Results may differ from the reference program's by a relative error of at most 0.019.
Values may be sent and summed in bfloat16 or wider, within the bound.
No kernel may reach another device: no remote copies, remote signals or barrier semaphores. Data moves between devices by JAX's collectives and lax.ppermute only.
A program may use at most 256 MiB of HBM per device.

```python
import math
import jax
import jax.numpy as jnp
import numpy as np
from jax import lax

D = 1152
H = 18
KV = 6
HD = 64
FF = 3072
TOK_DEV = 128
LEN = 256
TOKENS = 16384


def draw_keep(key, part):
    first, second = jax.random.split(jax.random.fold_in(key, 17))
    blocks = TOKENS // TOK_DEV
    rates = jax.random.randint(first, (blocks, 1), 0, 5)
    rolls = jax.random.randint(second, (blocks, TOK_DEV), 0, 4)
    return (rolls < rates).astype(jnp.int32).reshape(TOKENS)


def level_of(stream_key, dims, pieces, low, high):
    loudness, own = 1.0, jax.random.fold_in(stream_key, 6)
    for dim, blocks in pieces:
        heights = jnp.exp(jax.random.uniform(jax.random.fold_in(own, dim), (blocks,), jnp.float32, low / len(pieces), high / len(pieces)))
        loudness = loudness * jnp.repeat(heights, dims[dim] // blocks).reshape([-1 if axis == dim else 1 for axis in range(len(dims))])
    return loudness


def split_up(count, total, reach, skew):
    loads = [(1 << 20) // math.isqrt(standing ** skew) + 1 for standing in range(2, count + 1)]
    spare, given = total - reach - (count - 1), [1] * (count - 1)
    while spare > 0:
        candidates = [i for i in range(count - 1) if given[i] < reach]
        pool, remaining = sum([loads[i] for i in candidates]), spare
        for i in candidates:
            extra = min(reach - given[i], max(1, remaining * loads[i] // pool), spare)
            given[i] = given[i] + extra
            spare = spare - extra
    return np.array([reach] + given)


def ragged_sizes(stream_key, amount, total, bound, skew):
    if amount == 2:
        one = jax.random.randint(stream_key, (), max(1, total - bound), min(bound, total - 1) + 1)
        return jnp.stack([one, total - one])
    sizes = jnp.asarray(split_up(amount, total, bound, skew), jnp.int32)
    pairs = (amount - 1) // 2
    giver, receiver = sizes[1:1 + 2 * pairs:2], sizes[2:2 + 2 * pairs:2]
    margin = jnp.minimum(giver - 1, bound - receiver)
    shifted = jax.random.randint(jax.random.fold_in(stream_key, 1), (pairs,), 0, 1 << 20) % (margin + 1)
    sizes = sizes.at[1:1 + 2 * pairs:2].set(giver - shifted).at[2:2 + 2 * pairs:2].set(receiver + shifted)
    return sizes[jax.random.permutation(jax.random.fold_in(stream_key, 2), amount)]


def scatter_about(stream_key, dims, width, most, cuts=(), dtype=jnp.bfloat16):
    entries = jax.random.normal(stream_key, dims, jnp.float32) * width
    if len(cuts) > 0:
        entries = level_of(stream_key, dims, cuts, -0.22, 0.18) * entries
    return jnp.clip(entries, min=-most, max=most).astype(dtype)


def setup_inputs(seed: int = 0) -> dict:
    streams_of = jax.random.split(jax.random.key(seed), 14)
    tokens = scatter_about(streams_of[0], (TOKENS, D), 1.0, 6.0, ((0, 128),))
    doc_ids = jnp.searchsorted(jnp.cumsum(ragged_sizes(streams_of[1], 2 * TOKENS // LEN, TOKENS, LEN, 1)), jnp.arange(TOKENS), side="right").astype(jnp.int32)
    keep = draw_keep(jax.random.fold_in(streams_of[13], 71), 0)
    attention_gain = jnp.clip(1.0 + 0.1 * jax.random.normal(streams_of[3], (D,), jnp.float32), 0.5, 1.5).astype(jnp.bfloat16)
    query_weight = scatter_about(streams_of[4], (D, H * HD), D ** -0.5, 0.1875, ((0, 128),))
    key_weight = scatter_about(streams_of[5], (D, KV * HD), D ** -0.5, 0.1875, ((0, 128),))
    value_weight = scatter_about(streams_of[6], (D, KV * HD), D ** -0.5, 0.1875, ((0, 128),))
    out_weight = scatter_about(streams_of[7], (H * HD, D), (H * HD // 8) ** -0.5, 0.5, ((0, 128),))
    feed_gain = jnp.clip(1.0 + 0.1 * jax.random.normal(streams_of[8], (D,), jnp.float32), 0.5, 1.5).astype(jnp.bfloat16)
    gate_weight = scatter_about(streams_of[9], (D, FF), D ** -0.5, 0.1875, ((0, 128),))
    up_weight = scatter_about(streams_of[10], (D, FF), D ** -0.5, 0.1875, ((0, 128),))
    down_weight = scatter_about(streams_of[11], (FF, D), (FF // 4) ** -0.5, 0.21875, ((0, 128),))
    cotangent = scatter_about(streams_of[12], (TOKENS, D), 1.0, 6.0, ((0, 128),), jnp.float32)
    return {"tokens": tokens, "doc_ids": doc_ids, "keep": keep, "attention_gain": attention_gain, "query_weight": query_weight, "key_weight": key_weight, "value_weight": value_weight, "out_weight": out_weight, "feed_gain": feed_gain, "gate_weight": gate_weight, "up_weight": up_weight, "down_weight": down_weight, "cotangent": cotangent}


@jax.custom_vjp
def low(v):
    return lax.optimization_barrier(v.astype(jnp.bfloat16)).astype(jnp.float32)

@jax.custom_vjp
def low_back(v):
    return v

def low_keep(v):
    return (low(v), None)

def low_pass(kept, grad):
    return (grad,)

def back_keep(v):
    return (v, None)

def back_low(kept, grad):
    return (low(grad),)
low.defvjp(low_keep, low_pass)
low_back.defvjp(back_keep, back_low)
NEGATIVE = -1e+30
EPSILON = 1e-05

def matmul(left, right):
    return jnp.dot(left, right, precision=lax.Precision.HIGHEST, preferred_element_type=jnp.float32)

def rms_scale(values, gain):
    meansq = lax.optimization_barrier(jnp.mean(values * values, axis=-1, keepdims=True))
    return values * lax.rsqrt(meansq + EPSILON) * gain

def rotate(values, position, heads):
    half = HD // 2
    freqs = 10000.0 ** (-(jnp.arange(half).astype(jnp.float32) * 2.0 / HD))
    angle = position.astype(jnp.float32)[:, None] * freqs[None, :]
    cosine = jnp.cos(angle)[:, None, :]
    sine = jnp.sin(angle)[:, None, :]
    shaped = values.reshape(values.shape[0], heads, HD)
    first = shaped[:, :, :half]
    second = shaped[:, :, half:]
    turned = jnp.concatenate([first * cosine - second * sine, second * cosine + first * sine], axis=-1)
    return turned.reshape(values.shape)

def attend(query, keys, values, docs):
    length = query.shape[0]
    spots = jnp.arange(length)
    allowed = (spots[None, :] <= spots[:, None]) & (docs[None, :] == docs[:, None])
    query_heads = query.reshape(length, KV, H // KV, HD)
    key_heads = keys.reshape(length, KV, HD)
    value_heads = values.reshape(length, KV, HD)
    products = jnp.einsum('qkgd,tkd->kgqt', query_heads, key_heads, precision=lax.Precision.HIGHEST) * (1.0 / math.sqrt(HD))
    scores = jnp.where(allowed[None, None], low_back(products), NEGATIVE)
    highest = lax.optimization_barrier(jnp.max(scores, axis=-1, keepdims=True))
    weights = jnp.exp(scores - highest)
    probs = low(weights / lax.optimization_barrier(jnp.sum(weights, axis=-1, keepdims=True)))
    result = jnp.einsum('kgqt,tkd->qkgd', probs, value_heads, precision=lax.Precision.HIGHEST)
    return result.reshape(length, H * HD)

def layer(inputs, gain_one, query_weight, key_weight, value_weight, out_weight, gain_two, gate_weight, up_weight, down_weight, doc_ids, keep_rows):
    position = jnp.arange(TOKENS) % LEN
    normed = low(rms_scale(inputs, gain_one))
    query = low(rotate(low_back(matmul(normed, query_weight)), position, H))
    keys = low(rotate(low_back(matmul(normed, key_weight)), position, KV))
    values = low(low_back(matmul(normed, value_weight)))
    sequences = TOKENS // LEN
    checked = jax.checkpoint(attend)
    attended = lax.map(lambda parts: checked(parts[0], parts[1], parts[2], parts[3]), (query.reshape(sequences, LEN, H * HD), keys.reshape(sequences, LEN, KV * HD), values.reshape(sequences, LEN, KV * HD), doc_ids.reshape(sequences, LEN)))
    attended = low(low_back(attended.reshape(TOKENS, H * HD)))
    middle = inputs + keep_rows * low_back(matmul(attended, out_weight))
    normed_two = low(rms_scale(middle, gain_two))
    gate = low_back(matmul(normed_two, gate_weight))
    upward = low_back(matmul(normed_two, up_weight))
    active = low(jax.nn.sigmoid(gate) * gate * upward)
    return middle + keep_rows * low_back(matmul(active, down_weight))

def reference(tokens, doc_ids, keep, attention_gain, query_weight, key_weight, value_weight, out_weight, feed_gain, gate_weight, up_weight, down_weight, cotangent):
    keep_rows = keep.astype(jnp.float32)[:, None]
    floats = [a.astype(jnp.float32) for a in (tokens, attention_gain, query_weight, key_weight, value_weight, out_weight, feed_gain, gate_weight, up_weight, down_weight)]

    def forward(*weights):
        return layer(*weights, doc_ids, keep_rows)
    output, pull = jax.vjp(forward, *floats)
    grads = pull(cotangent.astype(jnp.float32))
    return (output.astype(jnp.bfloat16), grads[0], grads[1], grads[2], grads[3], grads[4], grads[5], grads[6], grads[7], grads[8], grads[9])
```

```python
import math

import jax
import jax.numpy as jnp
from jax import lax
from jax.sharding import Mesh, PartitionSpec as P

H = 18
KV = 6
HD = 64
D = 1152
FF = 3072
ROWS = 128
EPSILON = 1e-05
NEGATIVE = -1e30
AXES = ("y", "z", "xh", "c", "xl")
SIZES = {"y": 4, "z": 4, "xh": 2, "c": 2, "xl": 2}
BF = jnp.bfloat16
F32 = jnp.float32
HQ = H // 2
HK = KV // 2
GROUP = H // KV
QKV = (HQ + 2 * HK) * HD
A_SPLIT = 1024
A_COLS = 1664
HALF = FF // 2


def places():
    for y in range(4):
        for z in range(4):
            for xh in range(2):
                for c in range(2):
                    for xl in range(2):
                        yield {"y": y, "z": z, "xh": xh, "c": c, "xl": xl}


def index_of(place):
    total = 0
    for name in AXES:
        total = total * SIZES[name] + place[name]
    return total


def shift_pairs(axis, step):
    pairs = []
    for place in places():
        other = dict(place)
        if axis == "x":
            spot = (place["xh"] * 2 + place["xl"] + step) % 4
            other["xh"], other["xl"] = spot // 2, spot % 2
        elif axis == "c":
            other["c"] = 1 - place["c"]
        else:
            other[axis] = (place[axis] + step) % 4
        pairs.append((index_of(place), index_of(other)))
    return pairs


PAIRS = {(axis, step): shift_pairs(axis, step) for axis in "xyz" for step in (1, -1, 2)}
PAIRS["c"] = shift_pairs("c", 1)
PAIRS["late"] = [
    (index_of(place), index_of({**place, "xl": 1})) for place in places() if place["xl"] == 0
]
PAIRS["early"] = [
    (index_of(place), index_of({**place, "xl": 0})) for place in places() if place["xl"] == 1
]


def send(value, key):
    return lax.ppermute(value, AXES, PAIRS[key])


def mm(left, right):
    return jnp.dot(left, right, preferred_element_type=F32)


def mm_t(left, right):
    return lax.dot_general(left, right, (((1,), (1,)), ((), ())), preferred_element_type=F32)


def put(full, block, axis, index):
    starts = [0] * full.ndim
    starts[axis] = index
    return lax.dynamic_update_slice(full, jnp.expand_dims(block, axis), starts)


def pick(array, axis, index):
    return lax.dynamic_index_in_dim(array, index, axis, keepdims=False)


def wrap(spot, step):
    return lax.rem(spot + step + 4, 4)


def gather_direct(block, axis, spot, dim):
    shape = list(block.shape)
    shape.insert(dim, 4)
    full = jnp.zeros(shape, block.dtype)
    full = put(full, block, dim, spot)
    full = put(full, send(block, (axis, 1)), dim, wrap(spot, -1))
    full = put(full, send(block, (axis, -1)), dim, wrap(spot, 1))
    return put(full, send(block, (axis, 2)), dim, wrap(spot, 2))


def gather_ring(block, axis, spot, dim):
    half = block.shape[-2] // 2
    shape = list(block.shape)
    shape.insert(dim, 4)
    left = send(block, (axis, 1))
    right = send(block, (axis, -1))
    low = send(left[..., :half, :], (axis, 1))
    high = send(right[..., half:, :], (axis, -1))
    full = jnp.zeros(shape, block.dtype)
    full = put(full, block, dim, spot)
    full = put(full, left, dim, wrap(spot, -1))
    full = put(full, right, dim, wrap(spot, 1))
    far = jnp.concatenate([low, high], axis=-2)
    return put(full, far, dim, wrap(spot, 2))


def reduce_ring(chunk, axis):
    far = chunk(2).astype(BF)
    half = far.shape[-2] // 2
    low = send(far[..., :half, :], (axis, 1))
    high = send(far[..., half:, :], (axis, -1))
    ahead = chunk(1)
    ahead = jnp.concatenate([ahead[..., :half, :] + low, ahead[..., half:, :]], axis=-2)
    behind = chunk(-1)
    behind = jnp.concatenate([behind[..., :half, :], behind[..., half:, :] + high], axis=-2)
    first = send(ahead.astype(BF), (axis, 1))
    second = send(behind.astype(BF), (axis, -1))
    return chunk(0) + first + second


def reduce_direct(parts, axis, spot, dim):
    low = parts.astype(BF)
    first = send(pick(low, dim, wrap(spot, 1)), (axis, 1))
    second = send(pick(low, dim, wrap(spot, -1)), (axis, -1))
    third = send(pick(low, dim, wrap(spot, 2)), (axis, 2))
    return pick(parts, dim, spot) + first + second + third


def normal(values):
    scale = lax.rsqrt(jnp.mean(values * values, axis=-1, keepdims=True) + EPSILON)
    return values * scale, scale


def normal_pull(hat, scale, grad):
    return scale * (grad - hat * jnp.mean(grad * hat, axis=-1, keepdims=True))


def turn(values, cosine, sine):
    first, second = values[..., : HD // 2], values[..., HD // 2 :]
    return jnp.concatenate(
        [first * cosine - second * sine, second * cosine + first * sine], axis=-1
    )


def on_device(
    tokens, doc_ids, keep, gain_one, wq, wk, wv, wo, gain_two, wg, wu, wd, cotangent
):
    y, z, c = lax.axis_index("y"), lax.axis_index("z"), lax.axis_index("c")
    xl = lax.axis_index("xl")
    x = lax.axis_index("xh") * 2 + xl
    first_core = c == 0

    def both(own, other):
        return jnp.where(first_core, jnp.stack([own, other]), jnp.stack([other, own]))

    def attention_half(h):
        return jnp.concatenate(
            [
                wq[:, h * 576 : h * 576 + 576],
                wk[:, h * 192 : h * 192 + 192],
                wv[:, h * 192 : h * 192 + 192],
                gain_one[:, None],
                gain_two[:, None],
                jnp.zeros((9, A_SPLIT - QKV - 2), BF),
                wo[:, h * 576 : h * 576 + 576],
                jnp.zeros((9, A_COLS - A_SPLIT - 576), BF),
            ],
            axis=1,
        )

    def own_other(zero, one):
        return jnp.where(first_core, zero, one), jnp.where(first_core, one, zero)

    def hidden_half(w, h):
        return w.reshape(9, 32, 2, 48)[:, :, h, :].reshape(9, HALF)

    r = lax.broadcasted_iota(jnp.int32, (72, 96), 0)
    s = lax.broadcasted_iota(jnp.int32, (72, 96), 1)
    xh_r, rest = r // 36, r % 36
    c_r, rest = rest // 18, rest % 18
    xl_r, i_r = rest // 9, rest % 9
    k_r = lax.rem(xh_r * 2 + xl_r - x + 4, 4)
    select = (s == k_r * 24 + jnp.where(c_r == c, 0, 9) + i_r).astype(BF)

    def rows72(zero, one):
        own, other = own_other(zero, one)
        got = send(other, "c")
        block = jnp.concatenate([own, got, jnp.zeros((6, own.shape[1]), BF)], axis=0)
        stacked = jnp.concatenate(
            [block, send(block, ("x", -1)), send(block, ("x", 2)), send(block, ("x", 1))], axis=0
        )
        return mm(select, stacked).astype(BF)

    def gather_zy(block):
        return gather_ring(
            gather_direct(block, "z", z, 0).reshape(1, 288, -1), "y", y, 1
        ).reshape(D, -1)

    def gather_yz(block):
        return gather_ring(gather_direct(block, "y", y, 0), "z", z, 1).reshape(D, -1)

    x_all = both(tokens, send(tokens, "c")).reshape(2 * ROWS, D).astype(F32)
    marks = jnp.stack([doc_ids, keep])
    marks = both(marks, send(marks, "c"))
    docs, kf = marks[:, 0], marks[:, 1].astype(F32).reshape(2 * ROWS, 1)
    docs_early = send(docs, "late")
    cot = both(cotangent, send(cotangent, "c")).reshape(2 * ROWS, D)

    a72 = rows72(attention_half(0), attention_half(1))
    qkv_w = jnp.concatenate([gather_zy(a72[:, :512]), gather_yz(a72[:, 512:A_SPLIT])], axis=1)
    out_w = gather_yz(a72[:, A_SPLIT:])
    g72 = rows72(hidden_half(wg, 0), hidden_half(wg, 1))
    u72 = rows72(hidden_half(wu, 0), hidden_half(wu, 1))
    gate_w = gather_zy(g72)
    up_w = gather_yz(u72)
    d_block = gather_direct(gather_direct(wd, "y", y, 0), "z", z, 1)
    down_w = gather_ring(d_block.reshape(16, 24, D), "x", x, 1).reshape(HALF, D)

    unit = (
        lax.broadcasted_iota(jnp.int32, (8, 128), 1)
        == lax.broadcasted_iota(jnp.int32, (8, 128), 0) + (QKV - 896)
    ).astype(BF)
    gains = mm_t(unit, qkv_w[:, 896:A_SPLIT])
    g1, g2 = gains[0:1], gains[1:2]

    half = HD // 2
    freqs = 10000.0 ** (-(jnp.arange(half).astype(F32) * 2.0 / HD))
    position = xl * ROWS + jnp.arange(ROWS, dtype=jnp.int32)
    angle = position.astype(F32)[:, None] * freqs[None, :]
    cosine = jnp.cos(angle)[None, :, None, :]
    sine = jnp.sin(angle)[None, :, None, :]

    hat, hat_scale = normal(x_all)
    n1 = (hat * g1).astype(BF)
    qkv = mm(n1, qkv_w)
    q = turn(qkv[:, : HQ * HD].reshape(2, ROWS, HQ, HD), cosine, sine).astype(BF)
    k = turn(
        qkv[:, HQ * HD : (HQ + HK) * HD].reshape(2, ROWS, HK, HD), cosine, sine
    ).astype(BF)
    v = qkv[:, (HQ + HK) * HD : QKV].reshape(2, ROWS, HK, HD).astype(BF)
    kv = jnp.concatenate([k, v], axis=2)
    kv_early = send(kv, "late")
    kv_all = jnp.concatenate([kv_early, kv], axis=1)
    keys, vals = kv_all[:, :, :HK], kv_all[:, :, HK:]
    spots = jnp.arange(ROWS)
    causal = spots[None, :] <= spots[:, None]
    allowed = jnp.concatenate(
        [
            (docs_early[:, None, :] == docs[:, :, None]) & (xl == 1),
            (docs[:, None, :] == docs[:, :, None]) & causal[None],
        ],
        axis=2,
    )
    qg = q.reshape(2, ROWS, HK, GROUP, HD)
    scores = jnp.einsum("sqkgd,stkd->skgqt", qg, keys, preferred_element_type=F32) * (
        1.0 / math.sqrt(HD)
    )
    scores = jnp.where(allowed[:, None, None], scores, NEGATIVE)
    weights = jnp.exp(scores - jnp.max(scores, axis=-1, keepdims=True))
    probs = weights / jnp.sum(weights, axis=-1, keepdims=True)
    probs_low = probs.astype(BF)
    o = jnp.einsum("skgqt,stkd->sqkgd", probs_low, vals, preferred_element_type=F32)
    o = o.reshape(2 * ROWS, HQ * HD).astype(BF)
    o_got = send(o, "c")
    o_all = jnp.where(
        first_core, jnp.concatenate([o, o_got], axis=1), jnp.concatenate([o_got, o], axis=1)
    )

    part = kf * mm(o_all, out_w)[:, :576]
    part_got = send(part, "c")
    middle = x_all + jnp.where(
        first_core,
        jnp.concatenate([part, part_got], axis=1),
        jnp.concatenate([part_got, part], axis=1),
    )
    hat2, hat2_scale = normal(middle)
    n2 = (hat2 * g2).astype(BF)
    gate = mm(n2, gate_w)
    up = mm(n2, up_w)
    sig = jax.nn.sigmoid(gate)
    silu = gate * sig
    act = (silu * up).astype(BF)
    down = mm(act, down_w).reshape(2, ROWS, D)
    down_got = send(pick(down, 0, 1 - c).astype(BF), "c")
    own_kf = pick(kf.reshape(2, ROWS, 1), 0, c)
    mixed = pick(middle.reshape(2, ROWS, D), 0, c) + own_kf * (pick(down, 0, c) + down_got)

    bm = (kf * cot).astype(BF)
    dact = mm_t(bm, down_w)
    dgate = (dact * up * (sig * (1.0 + gate * (1.0 - sig)))).astype(BF)
    dup = (dact * silu).astype(BF)
    act_t = act.T.reshape(16, 4, 24, 2 * ROWS)
    d_first = reduce_ring(
        lambda step: mm(pick(act_t, 1, wrap(x, step)).reshape(384, 2 * ROWS), bm).reshape(
            16, 24, D
        ),
        "x",
    )
    n2_t = n2.T

    def reduce_yz_first(lhs_t, rhs):
        by_y = lhs_t.reshape(4, 288, 2 * ROWS)
        total = reduce_ring(lambda step: mm(pick(by_y, 0, wrap(y, step)), rhs), "y")
        return reduce_direct(total.reshape(4, 72, -1), "z", z, 0)

    def reduce_zy_first(lhs_t, rhs):
        by_z = lhs_t.reshape(4, 4, 72, 2 * ROWS)
        total = reduce_ring(
            lambda step: mm(pick(by_z, 1, wrap(z, step)).reshape(288, 2 * ROWS), rhs).reshape(
                4, 72, -1
            ),
            "z",
        )
        return reduce_direct(total, "y", y, 0)

    dg72 = reduce_yz_first(n2_t, dgate)
    du72 = reduce_zy_first(n2_t, dup)

    dn2_part = mm_t(dgate, gate_w) + mm_t(dup, up_w)
    dn2 = dn2_part + send(dn2_part.astype(BF), "c")
    dmiddle = cot + normal_pull(hat2, hat2_scale, dn2 * g2)
    ba = (kf * dmiddle).astype(BF)
    ba_own = jnp.where(first_core, ba[:, :576], ba[:, 576:])
    ba_own = jnp.concatenate([ba_own, jnp.zeros((2 * ROWS, 64), BF)], axis=1)
    do_part = mm_t(ba_own, out_w).reshape(2 * ROWS, 2, 576)
    do = pick(do_part, 1, c) + send(pick(do_part, 1, 1 - c).astype(BF), "c")
    do = do.astype(BF).reshape(2, ROWS, HK, GROUP, HD)
    do72 = reduce_zy_first(o_all.T, ba_own)

    dp = jnp.einsum("sqkgd,stkd->skgqt", do, vals, preferred_element_type=F32)
    ds = (probs * (dp - jnp.sum(probs * dp, axis=-1, keepdims=True))).astype(BF)
    scale = 1.0 / math.sqrt(HD)
    dq = jnp.einsum("skgqt,stkd->sqkgd", ds, keys, preferred_element_type=F32) * scale
    dk = jnp.einsum("skgqt,sqkgd->stkd", ds, qg, preferred_element_type=F32) * scale
    dv = jnp.einsum("skgqt,sqkgd->stkd", probs_low, do, preferred_element_type=F32)
    dkv = jnp.concatenate([dk, dv], axis=2)
    dkv = dkv[:, ROWS:] + send(dkv[:, :ROWS].astype(BF), "early")
    dq = turn(dq.reshape(2, ROWS, HQ, HD), cosine, -sine)
    dk = turn(dkv[:, :, :HK], cosine, -sine)
    dqkv = jnp.concatenate([dq, dk, dkv[:, :, HK:]], axis=2).astype(BF).reshape(2 * ROWS, QKV)
    dqkv = jnp.concatenate([dqkv, jnp.zeros((2 * ROWS, A_SPLIT - QKV), BF)], axis=1)
    n1_t = n1.T
    da72 = jnp.concatenate(
        [reduce_yz_first(n1_t, dqkv[:, :512]), reduce_zy_first(n1_t, dqkv[:, 512:]), do72], axis=1
    )
    dn1_part = mm_t(dqkv, qkv_w).reshape(2, ROWS, D)
    dn1 = pick(dn1_part, 0, c) + send(pick(dn1_part, 0, 1 - c).astype(BF), "c")
    hat_own = pick(hat.reshape(2, ROWS, D), 0, c)
    scale_own = pick(hat_scale.reshape(2, ROWS, 1), 0, c)
    back_tokens = pick(dmiddle.reshape(2, ROWS, D), 0, c) + normal_pull(
        hat_own, scale_own, dn1 * g1
    )

    def rows9(rows):
        low = rows.astype(BF)
        chunks = lax.dot_general(
            select, low, (((0,), (0,)), ((), ())), preferred_element_type=F32
        )
        chunks_low = chunks.astype(BF)
        total = (
            chunks[0:24]
            + send(chunks_low[24:48], ("x", 1))
            + send(chunks_low[48:72], ("x", 2))
            + send(chunks_low[72:96], ("x", -1))
        )
        got = send(total[9:18].astype(BF), "c").astype(F32)
        own = total[0:9]
        return jnp.where(first_core, own, got), jnp.where(first_core, got, own)

    def hidden_join(zero, one):
        return jnp.stack([zero.reshape(9, 32, 48), one.reshape(9, 32, 48)], axis=2).reshape(9, FF)

    back_down = reduce_direct(
        reduce_direct(d_first.reshape(4, 4, 24, D), "z", z, 1), "y", y, 0
    )
    back_gate = hidden_join(*rows9(dg72))
    back_up = hidden_join(*rows9(du72))
    a0, a1 = rows9(da72)
    join = lambda low, high: jnp.concatenate([a0[:, low:high], a1[:, low:high]], axis=1)
    back_query = join(0, 576)
    back_key = join(576, 768)
    back_value = join(768, 960)
    back_out = join(A_SPLIT, A_SPLIT + 576)
    dots = lambda weight, grad: jnp.sum(weight.astype(F32) * grad, axis=1)
    back_one = (
        dots(wq, back_query) + dots(wk, back_key) + dots(wv, back_value)
    ) / gain_one.astype(F32)
    back_two = (dots(wg, back_gate) + dots(wu, back_up)) / gain_two.astype(F32)
    return (
        mixed.astype(BF),
        back_tokens,
        back_one,
        back_query,
        back_key,
        back_value,
        back_out,
        back_two,
        back_gate,
        back_up,
        back_down,
    )


def solution(mesh):
    fine = Mesh(mesh.devices.reshape([SIZES[name] for name in AXES]), AXES)
    row, rows = P(AXES), P(AXES, None)
    in_specs = (rows, row, row, row, rows, rows, rows, rows, row, rows, rows, rows, rows)
    out_specs = (rows, rows, row, rows, rows, rows, rows, row, rows, rows, rows)
    return jax.shard_map(
        on_device, mesh=fine, in_specs=in_specs, out_specs=out_specs, check_vma=False
    )
```

```python
import math

import jax
import jax.numpy as jnp
from jax import lax
from jax.sharding import Mesh, PartitionSpec as P

H = 18
KV = 6
HD = 64
D = 1152
FF = 3072
ROWS = 128
EPSILON = 1e-05
NEGATIVE = -1e30
AXES = ("y", "z", "xh", "c", "xl")
SIZES = {"y": 4, "z": 4, "xh": 2, "c": 2, "xl": 2}
BF = jnp.bfloat16
F32 = jnp.float32
HQ = H // 2
HK = KV // 2
GROUP = H // KV
PART = 832
VPAD = 256
HALF = FF // 2
SLOTS = 1536
WIDE = FF + D
CHIPS = ("y", "z", "xh", "xl")


def places():
    for y in range(4):
        for z in range(4):
            for xh in range(2):
                for c in range(2):
                    for xl in range(2):
                        yield {"y": y, "z": z, "xh": xh, "c": c, "xl": xl}


def index_of(place):
    total = 0
    for name in AXES:
        total = total * SIZES[name] + place[name]
    return total


def shift_pairs(axis, step):
    pairs = []
    for place in places():
        other = dict(place)
        if axis == "x":
            spot = (place["xh"] * 2 + place["xl"] + step) % 4
            other["xh"], other["xl"] = spot // 2, spot % 2
        elif axis == "c":
            other["c"] = 1 - place["c"]
        else:
            other[axis] = (place[axis] + step) % 4
        pairs.append((index_of(place), index_of(other)))
    return pairs


PAIRS = {(axis, step): shift_pairs(axis, step) for axis in "xyz" for step in (1, -1, 2)}
PAIRS["c"] = shift_pairs("c", 1)
PAIRS["late"] = [
    (index_of(place), index_of({**place, "xl": 1})) for place in places() if place["xl"] == 0
]
PAIRS["early"] = [
    (index_of(place), index_of({**place, "xl": 0})) for place in places() if place["xl"] == 1
]


def send(value, key):
    return lax.ppermute(value, AXES, PAIRS[key])


def mm(left, right):
    return jnp.dot(left, right, preferred_element_type=F32)


def mm_t(left, right):
    return lax.dot_general(left, right, (((1,), (1,)), ((), ())), preferred_element_type=F32)


def inner(left, right):
    return lax.dot_general(left, right, (((0,), (0,)), ((), ())), preferred_element_type=F32)


def put(full, block, axis, index):
    starts = [0] * full.ndim
    starts[axis] = index
    return lax.dynamic_update_slice(full, jnp.expand_dims(block, axis), starts)


def pick(array, axis, index):
    return lax.dynamic_index_in_dim(array, index, axis, keepdims=False)


def wrap(spot, step):
    return lax.rem(spot + step + 4, 4)


def gather_direct(block, axis, spot, dim):
    shape = list(block.shape)
    shape.insert(dim, 4)
    full = jnp.zeros(shape, block.dtype)
    full = put(full, block, dim, spot)
    full = put(full, send(block, (axis, 1)), dim, wrap(spot, -1))
    full = put(full, send(block, (axis, -1)), dim, wrap(spot, 1))
    return put(full, send(block, (axis, 2)), dim, wrap(spot, 2))


def reduce_first(chunk, axis):
    first = send(chunk(1).astype(BF), (axis, 1))
    second = send(chunk(-1).astype(BF), (axis, -1))
    third = send(chunk(2).astype(BF), (axis, 2))
    return chunk(0) + first + second + third


def reduce_direct(parts, axis, spot, dim):
    low = parts.astype(BF)
    first = send(pick(low, dim, wrap(spot, 1)), (axis, 1))
    second = send(pick(low, dim, wrap(spot, -1)), (axis, -1))
    third = send(pick(low, dim, wrap(spot, 2)), (axis, 2))
    return pick(parts, dim, spot) + first + second + third


def normal(values):
    scale = lax.rsqrt(jnp.mean(values * values, axis=-1, keepdims=True) + EPSILON)
    return values * scale, scale


def normal_pull(hat, scale, grad):
    return scale * (grad - hat * jnp.mean(grad * hat, axis=-1, keepdims=True))


def turn(values, cosine, sine):
    first, second = values[..., : HD // 2], values[..., HD // 2 :]
    return jnp.concatenate(
        [first * cosine - second * sine, second * cosine + first * sine], axis=-1
    )


def on_device(
    tokens, doc_ids, keep, gain_one, wq, wk, wv, wo, gain_two, wg, wu, wd, cotangent
):
    y, z, c = lax.axis_index("y"), lax.axis_index("z"), lax.axis_index("c")
    xl = lax.axis_index("xl")
    x = lax.axis_index("xh") * 2 + xl
    first_core = c == 0

    def both(own, other):
        return jnp.where(first_core, jnp.stack([own, other]), jnp.stack([other, own]))

    def attention_half(h):
        return jnp.concatenate(
            [
                wq[:, h * 576 : h * 576 + 576],
                wk[:, h * 192 : h * 192 + 192],
                gain_one[:, None],
                gain_two[:, None],
                jnp.zeros((9, PART - 770), BF),
                wv[:, h * 192 : h * 192 + 192],
                jnp.zeros((9, VPAD - 192), BF),
                wo[:, h * 576 : h * 576 + 576],
            ],
            axis=1,
        )

    def own_other(zero, one):
        return jnp.where(first_core, zero, one), jnp.where(first_core, one, zero)

    def hidden_half(w, h):
        return w.reshape(9, 32, 2, 48)[:, :, h, :].reshape(9, HALF)

    r = lax.broadcasted_iota(jnp.int32, (72, 96), 0)
    s = lax.broadcasted_iota(jnp.int32, (72, 96), 1)
    xh_r, rest = r // 36, r % 36
    c_r, rest = rest // 18, rest % 18
    xl_r, i_r = rest // 9, rest % 9
    k_r = lax.rem(xh_r * 2 + xl_r - x + 4, 4)
    select = (s == k_r * 24 + jnp.where(c_r == c, 0, 9) + i_r).astype(BF)

    def rows72(zero, one):
        own, other = own_other(zero, one)
        got = send(other, "c")
        block = jnp.concatenate([own, got, jnp.zeros((6, own.shape[1]), BF)], axis=0)
        stacked = jnp.concatenate(
            [block, send(block, ("x", -1)), send(block, ("x", 2)), send(block, ("x", 1))], axis=0
        )
        return mm(select, stacked).astype(BF)

    def gather_zy(block):
        return gather_direct(
            gather_direct(block, "z", z, 0).reshape(288, -1), "y", y, 0
        ).reshape(D, -1)

    def gather_yz(block):
        return gather_direct(gather_direct(block, "y", y, 0), "z", z, 1).reshape(D, -1)

    x_all = both(tokens, send(tokens, "c")).reshape(2 * ROWS, D).astype(F32)
    marks = jnp.stack([doc_ids, keep])
    marks = both(marks, send(marks, "c"))
    docs, kf = marks[:, 0], marks[:, 1].astype(F32).reshape(2 * ROWS, 1)
    docs_early = send(docs, "late")
    cot = both(cotangent, send(cotangent, "c")).reshape(2 * ROWS, D)

    zero_half = jnp.concatenate([hidden_half(wg, 0), hidden_half(wu, 0)], axis=1)
    one_half = jnp.concatenate([hidden_half(wg, 1), hidden_half(wu, 1)], axis=1)
    own, other = own_other(zero_half, one_half)
    got = send(other, "c")
    feed_block = jnp.concatenate(
        [jnp.where(first_core, own, got), jnp.where(first_core, got, own), jnp.zeros((6, FF), BF)]
    )
    feed_w = lax.all_gather(
        jnp.concatenate([feed_block, wd], axis=1), CHIPS, axis=0, tiled=True
    )
    gu_w, down_w = feed_w[:, :FF], feed_w[:, FF:]
    slot = lax.broadcasted_iota(jnp.int32, (D, SLOTS), 1)
    feature = lax.broadcasted_iota(jnp.int32, (D, SLOTS), 0)
    chip, inside = slot // 24, slot % 24
    source = (chip // 2) * 36 + (inside // 9) * 18 + (chip % 2) * 9 + inside % 9
    to_slots = ((source == feature) & (inside < 18)).astype(BF)

    a72 = rows72(attention_half(0), attention_half(1))
    qk_w = gather_zy(a72[:, :PART])
    vo_w = gather_yz(a72[:, PART:])
    v_w, out_w = vo_w[:, :VPAD], vo_w[:, VPAD:]

    unit = (
        lax.broadcasted_iota(jnp.int32, (8, 64), 1)
        == lax.broadcasted_iota(jnp.int32, (8, 64), 0)
    ).astype(BF)
    gains = mm_t(unit, qk_w[:, 768:])
    g1, g2 = gains[0:1], gains[1:2]

    half = HD // 2
    freqs = 10000.0 ** (-(jnp.arange(half).astype(F32) * 2.0 / HD))
    position = xl * ROWS + jnp.arange(ROWS, dtype=jnp.int32)
    angle = position.astype(F32)[:, None] * freqs[None, :]
    cosine = jnp.cos(angle)[None, :, None, :]
    sine = jnp.sin(angle)[None, :, None, :]

    hat, hat_scale = normal(x_all)
    n1 = (hat * g1).astype(BF)
    qk = mm(n1, qk_w)
    qk = turn(qk[:, :768].reshape(2, ROWS, HQ + HK, HD), cosine, sine).astype(BF)
    q, k = qk[:, :, :HQ], qk[:, :, HQ:]
    v = mm(n1, v_w)[:, :192].reshape(2, ROWS, HK, HD).astype(BF)
    kv = jnp.concatenate([k, v], axis=2)
    kv_early = send(kv, "late")
    kv_all = jnp.concatenate([kv_early, kv], axis=1)
    keys, vals = kv_all[:, :, :HK], kv_all[:, :, HK:]
    spots = jnp.arange(ROWS)
    causal = spots[None, :] <= spots[:, None]
    allowed = jnp.concatenate(
        [
            (docs_early[:, None, :] == docs[:, :, None]) & (xl == 1),
            (docs[:, None, :] == docs[:, :, None]) & causal[None],
        ],
        axis=2,
    )
    qg = q.reshape(2, ROWS, HK, GROUP, HD)
    scores = jnp.einsum("sqkgd,stkd->skgqt", qg, keys, preferred_element_type=F32) * (
        1.0 / math.sqrt(HD)
    )
    scores = jnp.where(allowed[:, None, None], scores, NEGATIVE)
    weights = jnp.exp(scores - jnp.max(scores, axis=-1, keepdims=True))
    probs = weights / jnp.sum(weights, axis=-1, keepdims=True)
    probs_low = probs.astype(BF)
    o = jnp.einsum("skgqt,stkd->sqkgd", probs_low, vals, preferred_element_type=F32)
    o = o.reshape(2 * ROWS, HQ * HD).astype(BF)
    o_got = send(o, "c")
    o_all = jnp.where(
        first_core, jnp.concatenate([o, o_got], axis=1), jnp.concatenate([o_got, o], axis=1)
    )

    part = kf * mm(o_all, out_w)
    part_got = send(part, "c")
    middle = x_all + jnp.where(
        first_core,
        jnp.concatenate([part, part_got], axis=1),
        jnp.concatenate([part_got, part], axis=1),
    )
    hat2, hat2_scale = normal(middle)
    n2 = (hat2 * g2).astype(BF)
    n2 = mm(n2, to_slots).astype(BF)
    gu = mm(n2, gu_w)
    gate, up = gu[:, :HALF], gu[:, HALF:]
    sig = jax.nn.sigmoid(gate)
    silu = gate * sig
    act = (silu * up).astype(BF)
    down = mm(act, down_w).reshape(2, ROWS, D)
    down_got = send(pick(down, 0, 1 - c).astype(BF), "c")
    own_kf = pick(kf.reshape(2, ROWS, 1), 0, c)
    mixed = pick(middle.reshape(2, ROWS, D), 0, c) + own_kf * (pick(down, 0, c) + down_got)

    bm = (kf * cot).astype(BF)
    dact = mm_t(bm, down_w)
    dgate = dact * up * (sig * (1.0 + gate * (1.0 - sig)))
    dgu = jnp.concatenate([dgate, dact * silu], axis=1).astype(BF)
    feed_grad = jnp.concatenate(
        [inner(n2, dgu).astype(BF), inner(act, bm).astype(BF)], axis=1
    )
    feed_sum = lax.psum_scatter(feed_grad, ("y", "z"), scatter_dimension=0, tiled=True)

    dn2_part = mm_t(mm_t(dgu, gu_w).astype(BF), to_slots)
    dn2 = dn2_part + send(dn2_part.astype(BF), "c")
    dmiddle = cot + normal_pull(hat2, hat2_scale, dn2 * g2)
    ba = (kf * dmiddle).astype(BF)
    ba_own = jnp.where(first_core, ba[:, :576], ba[:, 576:])
    do_part = mm_t(ba_own, out_w).reshape(2 * ROWS, 2, 576)
    do = pick(do_part, 1, c) + send(pick(do_part, 1, 1 - c).astype(BF), "c")
    do = do.astype(BF).reshape(2, ROWS, HK, GROUP, HD)
    dp = jnp.einsum("sqkgd,stkd->skgqt", do, vals, preferred_element_type=F32)
    ds = (probs * (dp - jnp.sum(probs * dp, axis=-1, keepdims=True))).astype(BF)
    scale = 1.0 / math.sqrt(HD)
    dq = jnp.einsum("skgqt,stkd->sqkgd", ds, keys, preferred_element_type=F32) * scale
    dk = jnp.einsum("skgqt,sqkgd->stkd", ds, qg, preferred_element_type=F32) * scale
    dv = jnp.einsum("skgqt,sqkgd->stkd", probs_low, do, preferred_element_type=F32)
    dkv = jnp.concatenate([dk, dv], axis=2)
    dkv = dkv[:, ROWS:] + send(dkv[:, :ROWS].astype(BF), "early")
    dq = turn(dq.reshape(2, ROWS, HQ, HD), cosine, -sine)
    dk = turn(dkv[:, :, :HK], cosine, -sine)
    dqk = jnp.concatenate([dq, dk], axis=2).astype(BF).reshape(2 * ROWS, 768)
    dqk = jnp.concatenate([dqk, jnp.zeros((2 * ROWS, PART - 768), BF)], axis=1)
    dv = dkv[:, :, HK:].astype(BF).reshape(2 * ROWS, 192)
    dv = jnp.concatenate([dv, jnp.zeros((2 * ROWS, VPAD - 192), BF)], axis=1)
    n1_t = n1.T
    n1_y = n1_t.reshape(4, 288, 2 * ROWS)
    n1_z = n1_t.reshape(4, 4, 72, 2 * ROWS)
    o_z = o_all.T.reshape(4, 4, 72, 2 * ROWS)
    qk_sum = reduce_first(lambda step: mm(pick(n1_y, 0, wrap(y, step)), dqk), "y")
    vo_sum = reduce_first(
        lambda step: jnp.concatenate(
            [
                mm(pick(n1_z, 1, wrap(z, step)).reshape(288, 2 * ROWS), dv),
                mm(pick(o_z, 1, wrap(z, step)).reshape(288, 2 * ROWS), ba_own),
            ],
            axis=1,
        ),
        "z",
    )
    da72 = jnp.concatenate(
        [
            reduce_direct(qk_sum.reshape(4, 72, PART), "z", z, 0),
            reduce_direct(vo_sum.reshape(4, 72, PART), "y", y, 0),
        ],
        axis=1,
    )
    dn1_part = (mm_t(dqk, qk_w) + mm_t(dv, v_w)).reshape(2, ROWS, D)
    dn1 = pick(dn1_part, 0, c) + send(pick(dn1_part, 0, 1 - c).astype(BF), "c")
    hat_own = pick(hat.reshape(2, ROWS, D), 0, c)
    scale_own = pick(hat_scale.reshape(2, ROWS, 1), 0, c)
    back_tokens = pick(dmiddle.reshape(2, ROWS, D), 0, c) + normal_pull(
        hat_own, scale_own, dn1 * g1
    )

    def chunks_over_x(rows):
        return lax.dot_general(select, rows, (((0,), (0,)), ((), ())), preferred_element_type=F32)

    def swap(own, other):
        got = send(other.astype(BF), "c").astype(F32)
        return jnp.where(first_core, own, got), jnp.where(first_core, got, own)

    def hidden_join(zero, one):
        return jnp.stack([zero.reshape(9, 32, 48), one.reshape(9, 32, 48)], axis=2).reshape(9, FF)

    feed24 = reduce_direct(feed_sum.astype(F32).reshape(4, 24, WIDE), "x", x, 0)
    back_down = feed24[:, FF:]
    core0, core1 = feed24[:9, :FF], feed24[9:18, :FF]
    f0, f1 = swap(jnp.where(first_core, core0, core1), jnp.where(first_core, core1, core0))
    back_gate = hidden_join(f0[:, :HALF], f1[:, :HALF])
    back_up = hidden_join(f0[:, HALF:], f1[:, HALF:])
    chunks = chunks_over_x(da72.astype(BF))
    chunks_low = chunks.astype(BF)
    a24 = (
        chunks[0:24]
        + send(chunks_low[24:48], ("x", 1))
        + send(chunks_low[48:72], ("x", 2))
        + send(chunks_low[72:96], ("x", -1))
    )
    a0, a1 = swap(a24[0:9], a24[9:18])
    join = lambda low, high: jnp.concatenate([a0[:, low:high], a1[:, low:high]], axis=1)
    back_query = join(0, 576)
    back_key = join(576, 768)
    back_value = join(PART, PART + 192)
    back_out = join(PART + VPAD, 2 * PART)
    dots = lambda weight, grad: jnp.sum(weight.astype(F32) * grad, axis=1)
    back_one = (
        dots(wq, back_query) + dots(wk, back_key) + dots(wv, back_value)
    ) / gain_one.astype(F32)
    back_two = (dots(wg, back_gate) + dots(wu, back_up)) / gain_two.astype(F32)
    return (
        mixed.astype(BF),
        back_tokens,
        back_one,
        back_query,
        back_key,
        back_value,
        back_out,
        back_two,
        back_gate,
        back_up,
        back_down,
    )


def solution(mesh):
    fine = Mesh(mesh.devices.reshape([SIZES[name] for name in AXES]), AXES)
    row, rows = P(AXES), P(AXES, None)
    in_specs = (rows, row, row, row, rows, rows, rows, rows, row, rows, rows, rows, rows)
    out_specs = (rows, rows, row, rows, rows, rows, rows, row, rows, rows, rows)
    return jax.shard_map(
        on_device, mesh=fine, in_specs=in_specs, out_specs=out_specs, check_vma=False
    )
```

```python
import math

import jax
import jax.numpy as jnp
from jax import lax
from jax.experimental import pallas as pl
from jax.experimental.pallas import tpu as pltpu
from jax.sharding import Mesh, PartitionSpec as P

H = 18
KV = 6
HD = 64
D = 1152
FF = 3072
ROWS = 128
EPSILON = 1e-05
NEGATIVE = -1e30
AXES = ("y", "z", "xh", "c", "xl")
SIZES = {"y": 4, "z": 4, "xh": 2, "c": 2, "xl": 2}
BF = jnp.bfloat16
F32 = jnp.float32
HQ = H // 2
HK = KV // 2
GROUP = H // KV
PART = 832
VPAD = 256
OWN = 576
LANES = 640
HALF = FF // 2
SLOTS = 1536
WIDE = FF + D
CHIPS = ("y", "z", "xh", "xl")


def places():
    for y in range(4):
        for z in range(4):
            for xh in range(2):
                for c in range(2):
                    for xl in range(2):
                        yield {"y": y, "z": z, "xh": xh, "c": c, "xl": xl}


def index_of(place):
    total = 0
    for name in AXES:
        total = total * SIZES[name] + place[name]
    return total


def shift_pairs(axis, step):
    pairs = []
    for place in places():
        other = dict(place)
        if axis == "x":
            spot = (place["xh"] * 2 + place["xl"] + step) % 4
            other["xh"], other["xl"] = spot // 2, spot % 2
        elif axis == "c":
            other["c"] = 1 - place["c"]
        else:
            other[axis] = (place[axis] + step) % 4
        pairs.append((index_of(place), index_of(other)))
    return pairs


PAIRS = {(axis, step): shift_pairs(axis, step) for axis in "xyz" for step in (1, -1, 2)}
PAIRS["c"] = shift_pairs("c", 1)
PAIRS["late"] = [
    (index_of(place), index_of({**place, "xl": 1})) for place in places() if place["xl"] == 0
]
PAIRS["early"] = [
    (index_of(place), index_of({**place, "xl": 0})) for place in places() if place["xl"] == 1
]


def send(value, key):
    return lax.ppermute(value, AXES, PAIRS[key])


def mm(left, right):
    return jnp.dot(left, right, preferred_element_type=F32)


def mm_t(left, right):
    return lax.dot_general(left, right, (((1,), (1,)), ((), ())), preferred_element_type=F32)


def inner(left, right):
    return lax.dot_general(left, right, (((0,), (0,)), ((), ())), preferred_element_type=F32)


def put(full, block, axis, index):
    starts = [0] * full.ndim
    starts[axis] = index
    return lax.dynamic_update_slice(full, jnp.expand_dims(block, axis), starts)


def pick(array, axis, index):
    return lax.dynamic_index_in_dim(array, index, axis, keepdims=False)


def wrap(spot, step):
    return lax.rem(spot + step + 4, 4)


def gather_direct(block, axis, spot, dim):
    shape = list(block.shape)
    shape.insert(dim, 4)
    full = jnp.zeros(shape, block.dtype)
    full = put(full, block, dim, spot)
    full = put(full, send(block, (axis, 1)), dim, wrap(spot, -1))
    full = put(full, send(block, (axis, -1)), dim, wrap(spot, 1))
    return put(full, send(block, (axis, 2)), dim, wrap(spot, 2))


def reduce_ring(chunk, axis):
    far = chunk(2).astype(BF)
    half = far.shape[0] // 2
    low = send(far[:half], (axis, 1))
    high = send(far[half:], (axis, -1))
    ahead = chunk(1) + jnp.pad(low, ((0, half), (0, 0)))
    behind = chunk(-1) + jnp.pad(high, ((half, 0), (0, 0)))
    first = send(ahead.astype(BF), (axis, 1))
    second = send(behind.astype(BF), (axis, -1))
    return chunk(0) + first + second


def reduce_direct(parts, axis, spot, dim):
    low = parts.astype(BF)
    first = send(pick(low, dim, wrap(spot, 1)), (axis, 1))
    second = send(pick(low, dim, wrap(spot, -1)), (axis, -1))
    third = send(pick(low, dim, wrap(spot, 2)), (axis, 2))
    return pick(parts, dim, spot) + first + second + third


def normal(values):
    scale = lax.rsqrt(jnp.mean(values * values, axis=-1, keepdims=True) + EPSILON)
    return values * scale, scale


def normal_pull(hat, scale, grad):
    return scale * (grad - hat * jnp.mean(grad * hat, axis=-1, keepdims=True))


def halves_swapped(values):
    lane = lax.broadcasted_iota(jnp.int32, values.shape, 1)
    return jnp.where(
        lane % HD < HD // 2, pltpu.roll(values, 96, 1), pltpu.roll(values, 32, 1)
    )


SMEM = pl.BlockSpec(memory_space=pltpu.SMEM)
HERE = pl.BlockSpec(memory_space=pltpu.HBM)
FAR = "far"


def call(body, outs, args, flops, scratch=(), places=None, megabytes=24):
    total = sum(math.prod(a.shape) * a.dtype.itemsize for a in args)
    total += sum(math.prod(shape) * jnp.dtype(kind).itemsize for shape, kind in outs)
    places = places or {}

    def spec(index, shape):
        if places.get(index, FAR) is not FAR:
            return places[index]
        return pl.BlockSpec(
            shape, lambda i: (0,) * len(shape), pipeline_mode=pl.Buffered(1)
        )

    in_specs = [spec(i, a.shape) for i, a in enumerate(args)]
    out_specs = [spec(len(args) + i, shape) for i, (shape, _) in enumerate(outs)]
    return pl.pallas_call(
        body,
        grid=(1,),
        out_shape=[
            pltpu.HBM(shape, kind)
            if places.get(len(args) + i) in (HERE, FAR)
            else jax.ShapeDtypeStruct(shape, kind)
            for i, (shape, kind) in enumerate(outs)
        ],
        in_specs=in_specs,
        out_specs=out_specs,
        scratch_shapes=list(scratch),
        compiler_params=pltpu.CompilerParams(vmem_limit_bytes=megabytes << 20),
        cost_estimate=pl.CostEstimate(flops=flops, bytes_accessed=total, transcendentals=0),
    )(
        *[
            pltpu.with_memory_space_constraint(a, pltpu.HBM)
            if places.get(i) in (HERE, FAR)
            else a
            for i, a in enumerate(args)
        ]
    )


TOK = 2 * ROWS
SCALE = 1.0 / math.sqrt(HD)


def project_kernel(x_ref, g_ref, wqk_ref, wvo_ref, cos_ref, sin_ref, n1_ref, qk_ref, kv_ref):
    hat, _ = normal(x_ref[...].astype(F32))
    n1 = (hat * g_ref[...]).astype(BF)
    n1_ref[...] = n1
    raw = mm(n1, wqk_ref[:, :768])
    v = mm(n1, wvo_ref[:, :VPAD]).astype(BF)
    cosine, sine = cos_ref[...], sin_ref[...]
    for s in range(2):
        rows = slice(s * ROWS, s * ROWS + ROWS)
        for j in range(6):
            tile = raw[rows, j * 128 : j * 128 + 128]
            turned = (tile * cosine + halves_swapped(tile) * sine).astype(BF)
            qk_ref[rows, j * 128 : j * 128 + 128] = turned
            if j == 0:
                kv_ref[rows, 0:128] = turned
            if j == 1:
                lane = lax.broadcasted_iota(jnp.int32, turned.shape, 1)
                kv_ref[rows, 128:256] = jnp.where(lane < 64, turned, v[rows, 0:128])
        kv_ref[rows, 256:384] = v[rows, 128:256]


def head_data(s, h, qk, kv, early):
    rows = slice(s * ROWS, s * ROWS + ROWS)
    base = 192 + h * 192
    q = jnp.concatenate(
        [qk[rows, base + 64 * g : base + 64 * g + 64] for g in range(GROUP)], axis=0
    )
    ke, ko = early[rows, 64 * h : 64 * h + 64], kv[rows, 64 * h : 64 * h + 64]
    ve, vo = (
        early[rows, 192 + 64 * h : 256 + 64 * h],
        kv[rows, 192 + 64 * h : 256 + 64 * h],
    )
    return rows, q, ke, ko, ve, vo


def masks(s, dcol_ref, drow_ref, derow_ref):
    rows = slice(s * ROWS, s * ROWS + ROWS)
    col = dcol_ref[rows, :]
    at = lax.broadcasted_iota(jnp.int32, (ROWS, ROWS), 0)
    to = lax.broadcasted_iota(jnp.int32, (ROWS, ROWS), 1)
    mask_o = (to <= at) & (col == drow_ref[s : s + 1, :])
    mask_e = col == derow_ref[s : s + 1, :]
    wide = lambda m: jnp.concatenate([jnp.where(m, 0.0, NEGATIVE)] * GROUP, axis=0)
    return wide(mask_e), wide(mask_o)


def softmax(q, ke, ko, mask_e, mask_o):
    se = jnp.where(mask_e == 0.0, mm_t(q, ke) * SCALE, NEGATIVE)
    so = jnp.where(mask_o == 0.0, mm_t(q, ko) * SCALE, NEGATIVE)
    top = jnp.maximum(
        jnp.max(se, axis=-1, keepdims=True), jnp.max(so, axis=-1, keepdims=True)
    )
    ee, eo = jnp.exp(se - top), jnp.exp(so - top)
    total = jnp.sum(ee, axis=-1, keepdims=True) + jnp.sum(eo, axis=-1, keepdims=True)
    return ee / total, eo / total


def attend_kernel(qk_ref, kv_ref, early_ref, dcol_ref, drow_ref, derow_ref, o_ref):
    qk, kv, early = qk_ref[...], kv_ref[...], early_ref[...]
    for s in range(2):
        mask_e, mask_o = masks(s, dcol_ref, drow_ref, derow_ref)
        pieces = []
        for h in range(HK):
            rows, q, ke, ko, ve, vo = head_data(s, h, qk, kv, early)
            pe, po = softmax(q, ke, ko, mask_e, mask_o)
            o = mm(pe.astype(BF), ve) + mm(po.astype(BF), vo)
            pieces += [o[g * ROWS : g * ROWS + ROWS] for g in range(GROUP)]
        pieces.append(jnp.zeros((ROWS, LANES - OWN), F32))
        o_ref[rows, :] = jnp.concatenate(pieces, axis=1).astype(BF)


def attend_back_kernel(
    qk_ref, kv_ref, early_ref, dcol_ref, drow_ref, derow_ref, do_ref, got_ref,
    dqk_ref, dv_ref, de_ref,
):
    qk, kv, early = qk_ref[...], kv_ref[...], early_ref[...]
    do_all = (do_ref[...] + got_ref[:, :OWN].astype(F32)).astype(BF)
    for s in range(2):
        mask_e, mask_o = masks(s, dcol_ref, drow_ref, derow_ref)
        dqs, dke, dko, dve, dvo = [], [], [], [], []
        for h in range(HK):
            rows, q, ke, ko, ve, vo = head_data(s, h, qk, kv, early)
            pe, po = softmax(q, ke, ko, mask_e, mask_o)
            do = jnp.concatenate(
                [
                    do_all[rows, (GROUP * h + g) * 64 : (GROUP * h + g) * 64 + 64]
                    for g in range(GROUP)
                ],
                axis=0,
            )
            dpe, dpo = mm_t(do, ve), mm_t(do, vo)
            centre = jnp.sum(pe * dpe, axis=-1, keepdims=True) + jnp.sum(
                po * dpo, axis=-1, keepdims=True
            )
            dse = (pe * (dpe - centre)).astype(BF)
            dso = (po * (dpo - centre)).astype(BF)
            dq = (mm(dse, ke) + mm(dso, ko)) * SCALE
            dqs += [dq[g * ROWS : g * ROWS + ROWS] for g in range(GROUP)]
            dke.append(inner(dse, q) * SCALE)
            dko.append(inner(dso, q) * SCALE)
            dve.append(inner(pe.astype(BF), do))
            dvo.append(inner(po.astype(BF), do))
        dqk_ref[rows, :] = jnp.concatenate(dko + dqs, axis=1)
        dv_ref[rows, :] = jnp.concatenate([jnp.zeros((ROWS, 64), F32)] + dvo, axis=1)
        de_ref[rows, :] = jnp.concatenate(dke + dve, axis=1).astype(BF)


def project_back_kernel(
    dqk_ref, dv_ref, got_ref, cos_ref, sin_ref, wqk_ref, wvo_ref, low_ref, dvlow_ref, dn1_ref
):
    got = got_ref[...].astype(F32)
    cosine, sine = cos_ref[...], sin_ref[...]
    lane = lax.broadcasted_iota(jnp.int32, (ROWS, 128), 1)
    for s in range(2):
        rows = slice(s * ROWS, s * ROWS + ROWS)
        for j in range(6):
            tile = dqk_ref[rows, j * 128 : j * 128 + 128]
            if j == 0:
                tile = tile + got[rows, 0:128]
            if j == 1:
                tile = tile + jnp.where(lane < 64, got[rows, 128:256], 0.0)
            turned = tile * cosine - halves_swapped(tile) * sine
            low_ref[rows, j * 128 : j * 128 + 128] = turned.astype(BF)
        dv0 = dv_ref[rows, 0:128] + jnp.where(lane < 64, 0.0, got[rows, 128:256])
        dvlow_ref[rows, 0:128] = dv0.astype(BF)
        dvlow_ref[rows, 128:256] = (dv_ref[rows, 128:256] + got[rows, 256:384]).astype(BF)
    dn1_ref[...] = mm_t(low_ref[...], wqk_ref[:, :768]) + mm_t(dvlow_ref[...], wvo_ref[:, :VPAD])


def out_rows(w_ref, c):
    return w_ref[pl.ds(pl.multiple_of(c * OWN, 64), OWN), VPAD:]


def out_kernel(c_ref, o_ref, got_ref, w_ref, kf_ref, part_ref):
    c = c_ref[0]
    total = mm(o_ref[:, :OWN], out_rows(w_ref, c)) + mm(
        got_ref[:, :OWN], out_rows(w_ref, 1 - c)
    )
    part_ref[:, :OWN] = kf_ref[...] * total
    part_ref[:, OWN:] = jnp.zeros((TOK, LANES - OWN), F32)


def feed_kernel(
    c_ref, x_ref, part_ref, got_ref, g_ref, fs_ref, bm_ref, w_ref,
    mid_ref, grad_ref, act_ref, dgu_ref,
    n2_ref, n2t_ref, wb, gb, in_sem, out_sem,
):
    tile = 512
    steps = HALF // tile

    def spots(t):
        at = pl.multiple_of(t * tile, tile)
        return (
            (slice(None), pl.ds(at, tile)),
            (slice(None), pl.ds(HALF + at, tile)),
            (pl.ds(at, tile), pl.ds(FF, D)),
        )

    def loads(t):
        return [
            pltpu.make_async_copy(w_ref.at[spot], wb.at[spot], in_sem.at[t, i])
            for i, spot in enumerate(spots(t))
        ]

    def stores(t):
        return [
            pltpu.make_async_copy(gb.at[spot], grad_ref.at[spot], out_sem.at[t, i])
            for i, spot in enumerate(spots(t))
        ]

    for t in range(steps):
        for copy in loads(t):
            copy.start()

    first = c_ref[0] == 0
    part, got = part_ref[:, :OWN], got_ref[:, :OWN]
    low = jnp.where(first, part, got)
    high = jnp.where(first, got, part)
    middle = x_ref[...].astype(F32) + jnp.concatenate([low, high], axis=1)
    mid_ref[...] = middle
    hat, _ = normal(middle)
    normed = (hat * g_ref[...]).astype(BF)
    n2_ref[...] = mm_t(normed, fs_ref[...]).astype(BF)
    n2t_ref[...] = n2_ref[...].T

    def step(t, carry):
        for copy in loads(t):
            copy.wait()
        gate_at, up_at, down_at = spots(t)
        n2, n2t, bm = n2_ref[...], n2t_ref[...], bm_ref[...]
        gate = mm(n2, wb[gate_at])
        up = mm(n2, wb[up_at])
        dact = mm_t(bm, wb[down_at])
        sig = jax.nn.sigmoid(gate)
        silu = gate * sig
        act = (silu * up).astype(BF)
        dgate = (dact * up * (sig * (1.0 + gate * (1.0 - sig)))).astype(BF)
        dup = (dact * silu).astype(BF)
        act_ref[gate_at] = act
        dgu_ref[gate_at] = dgate
        dgu_ref[up_at] = dup
        gb[gate_at] = mm(n2t, dgate).astype(BF)
        gb[up_at] = mm(n2t, dup).astype(BF)
        gb[down_at] = inner(act, bm).astype(BF)
        for copy in stores(t):
            copy.start()
        return carry

    lax.fori_loop(0, steps, step, 0)
    for t in range(steps):
        for copy in stores(t):
            copy.wait()


def feed_back_kernel(
    act_ref, dgu_ref, w_ref, fs_ref, down_ref, dn2_ref, wb, dgt_ref, slots_ref, sem
):
    tile = 256
    steps = SLOTS // tile

    def load(t):
        rows = pl.ds(pl.multiple_of(t * tile, tile), tile)
        return pltpu.make_async_copy(w_ref.at[rows, :], wb.at[rows, :], sem.at[t])

    for t in range(steps):
        load(t).start()
    down_ref[...] = jnp.zeros_like(down_ref)
    dgt_ref[...] = dgu_ref[...].T

    def step(t, carry):
        load(t).wait()
        rows = pl.ds(pl.multiple_of(t * tile, tile), tile)
        slots_ref[rows, :] = mm(wb[rows, :FF], dgt_ref[...]).astype(BF)
        down_ref[...] += mm(act_ref[:, rows], wb[rows, FF:])
        return carry

    lax.fori_loop(0, steps, step, 0)
    dn2_ref[...] = inner(slots_ref[...], fs_ref[...])


def middle_back_kernel(
    c_ref, part_ref, got_ref, mid_ref, cot_ref, g_ref, kf_ref, w_ref,
    dmid_ref, ba_ref, do_ref, other_ref,
):
    c = c_ref[0]
    dn2 = part_ref[...] + got_ref[...].astype(F32)
    hat, scale = normal(mid_ref[...])
    dmiddle = cot_ref[...] + normal_pull(hat, scale, dn2 * g_ref[...])
    dmid_ref[...] = dmiddle
    ba = kf_ref[...] * dmiddle
    half = jnp.where(c == 0, ba[:, :576], ba[:, 576:]).astype(BF)
    ba_ref[...] = half
    do_ref[...] = mm_t(half, out_rows(w_ref, c))
    other_ref[:, :OWN] = mm_t(half, out_rows(w_ref, 1 - c)).astype(BF)
    other_ref[:, OWN:] = jnp.zeros((TOK, LANES - OWN), BF)


def on_device(
    tokens, doc_ids, keep, gain_one, wq, wk, wv, wo, gain_two, wg, wu, wd, cotangent
):
    y, z, c = lax.axis_index("y"), lax.axis_index("z"), lax.axis_index("c")
    xl = lax.axis_index("xl")
    x = lax.axis_index("xh") * 2 + xl
    first_core = c == 0

    def both(own, other):
        return jnp.where(first_core, jnp.stack([own, other]), jnp.stack([other, own]))

    def attention_half(h):
        return jnp.concatenate(
            [
                wk[:, h * 192 : h * 192 + 192],
                wq[:, h * 576 : h * 576 + 576],
                gain_one[:, None],
                gain_two[:, None],
                jnp.zeros((9, PART - 770), BF),
                jnp.zeros((9, VPAD - 192), BF),
                wv[:, h * 192 : h * 192 + 192],
                wo[:, h * 576 : h * 576 + 576],
            ],
            axis=1,
        )

    def own_other(zero, one):
        return jnp.where(first_core, zero, one), jnp.where(first_core, one, zero)

    r = lax.broadcasted_iota(jnp.int32, (72, 96), 0)
    s = lax.broadcasted_iota(jnp.int32, (72, 96), 1)
    xh_r, rest = r // 36, r % 36
    c_r, rest = rest // 18, rest % 18
    xl_r, i_r = rest // 9, rest % 9
    k_r = lax.rem(xh_r * 2 + xl_r - x + 4, 4)
    select = (s == k_r * 24 + jnp.where(c_r == c, 0, 9) + i_r).astype(BF)

    def rows72(zero, one):
        own, other = own_other(zero, one)
        got = send(other, "c")
        block = jnp.concatenate([own, got, jnp.zeros((6, own.shape[1]), BF)], axis=0)
        stacked = jnp.concatenate(
            [block, send(block, ("x", -1)), send(block, ("x", 2)), send(block, ("x", 1))], axis=0
        )
        return mm(select, stacked).astype(BF)

    def gather_zy(block):
        return gather_direct(
            gather_direct(block, "z", z, 0).reshape(288, -1), "y", y, 0
        ).reshape(D, -1)

    def gather_yz(block):
        return gather_direct(gather_direct(block, "y", y, 0), "z", z, 1).reshape(D, -1)

    x_all = both(tokens, send(tokens, "c")).reshape(TOK, D)
    marks = jnp.stack([doc_ids, keep])
    marks = both(marks, send(marks, "c"))
    docs, kf = marks[:, 0], marks[:, 1].astype(F32).reshape(2 * ROWS, 1)
    docs_early = jnp.where(xl == 1, send(docs, "late"), -1)
    doc_args = (docs.reshape(TOK, 1), docs, docs_early)
    cot = both(cotangent, send(cotangent, "c")).reshape(2 * ROWS, D)

    by_core = jnp.concatenate([wg, wu]).reshape(18, 32, 2, 48)
    halves = [by_core[:, :, h, :].reshape(18, HALF) for h in range(2)]
    zero_half, one_half = [jnp.concatenate([h[:9], h[9:]], axis=1) for h in halves]
    own, other = own_other(zero_half, one_half)
    got = send(other, "c")
    feed_block = jnp.concatenate(
        [jnp.where(first_core, own, got), jnp.where(first_core, got, own), jnp.zeros((6, FF), BF)]
    )
    feed_w = lax.all_gather(
        jnp.concatenate([feed_block, wd], axis=1), CHIPS, axis=0, tiled=True
    )
    slot = lax.broadcasted_iota(jnp.int32, (SLOTS, D), 0)
    feature = lax.broadcasted_iota(jnp.int32, (SLOTS, D), 1)
    chip, inside = slot // 24, slot % 24
    source = (chip // 2) * 36 + (inside // 9) * 18 + (chip % 2) * 9 + inside % 9
    from_slots = ((source == feature) & (inside < 18)).astype(BF)

    a72 = rows72(attention_half(0), attention_half(1))
    qk_w = gather_zy(a72[:, :PART])
    vo_w = gather_yz(a72[:, PART:])

    unit = (
        lax.broadcasted_iota(jnp.int32, (8, 64), 1)
        == lax.broadcasted_iota(jnp.int32, (8, 64), 0)
    ).astype(BF)
    gains = mm_t(unit, qk_w[:, 768:])
    g1, g2 = gains[0:1], gains[1:2]

    half = HD // 2
    freqs = 10000.0 ** (-(jnp.arange(half).astype(F32) * 2.0 / HD))
    position = xl * ROWS + jnp.arange(ROWS, dtype=jnp.int32)
    angle = position.astype(F32)[:, None] * freqs[None, :]
    cosine = jnp.tile(jnp.cos(angle), (1, 4))
    sine = jnp.sin(angle)
    sine = jnp.concatenate([-sine, sine, -sine, sine], axis=1)
    core = c.astype(jnp.int32).reshape(1)
    bm = (kf * cot).astype(BF)
    early_work = (x_all, from_slots, bm, cosine, sine, kf, cot) + doc_args
    early_work, a_blocks = lax.optimization_barrier((early_work, (qk_w, vo_w)))
    x_all, from_slots, bm, cosine, sine, kf, cot = early_work[:7]
    doc_args = early_work[7:]
    qk_w, vo_w = a_blocks

    n1, qk, kv = call(
        project_kernel,
        [((TOK, D), BF), ((TOK, 768), BF), ((TOK, 384), BF)],
        (x_all, g1, qk_w, vo_w, cosine, sine),
        2 * TOK * D * 1024,
        places={0: FAR, 2: FAR, 3: FAR, 6: FAR, 7: FAR, 8: FAR},
    )
    n1_slots = mm_t(from_slots, n1).astype(BF).reshape(16, 4, 24, TOK)
    kv_early, n1_slots = lax.optimization_barrier((send(kv, "late"), n1_slots))
    (o,) = call(
        attend_kernel,
        [((TOK, LANES), BF)],
        (qk, kv, kv_early) + doc_args,
        4 * TOK * 576 * 256,
        places={0: FAR, 1: FAR, 2: FAR, 6: FAR},
    )
    o_got = send(o, "c")
    (part,) = call(
        out_kernel,
        [((TOK, LANES), F32)],
        (core, o, o_got, vo_w, kf),
        2 * TOK * D * 576,
        places={0: SMEM, 1: FAR, 2: FAR, 3: FAR, 5: FAR},
    )
    part_got = send(part, "c")
    middle, feed_grad, act, dgu = call(
        feed_kernel,
        [((TOK, D), F32), ((SLOTS, WIDE), BF), ((TOK, HALF), BF), ((TOK, FF), BF)],
        (core, x_all, part, part_got, g2, from_slots, bm, feed_w),
        4 * TOK * SLOTS * (WIDE + D),
        scratch=[
            pltpu.VMEM((TOK, SLOTS), BF),
            pltpu.VMEM((SLOTS, TOK), BF),
            pltpu.VMEM((SLOTS, WIDE), BF),
            pltpu.VMEM((SLOTS, WIDE), BF),
            pltpu.SemaphoreType.DMA((3, 3)),
            pltpu.SemaphoreType.DMA((3, 3)),
        ],
        places={0: SMEM, 7: HERE, 9: HERE} | {i: FAR for i in (1, 2, 3, 5, 6, 8, 10, 11)},
        megabytes=52,
    )
    feed_sum = lax.psum_scatter(feed_grad, ("y", "z"), scatter_dimension=0, tiled=True)
    down, dn2_part = call(
        feed_back_kernel,
        [((TOK, D), F32), ((TOK, D), F32)],
        (act, dgu, feed_w, from_slots),
        2 * TOK * SLOTS * (WIDE + D),
        scratch=[
            pltpu.VMEM((SLOTS, WIDE), BF),
            pltpu.VMEM((FF, TOK), BF),
            pltpu.VMEM((SLOTS, TOK), BF),
            pltpu.SemaphoreType.DMA((6,)),
        ],
        megabytes=40,
        places={0: FAR, 1: FAR, 2: HERE, 3: FAR},
    )
    down = down.reshape(2, ROWS, D)
    down_got = send(pick(down, 0, 1 - c).astype(BF), "c")
    own_kf = pick(kf.reshape(2, ROWS, 1), 0, c)
    mixed = pick(middle.reshape(2, ROWS, D), 0, c) + own_kf * (pick(down, 0, c) + down_got)

    dn2_got = send(dn2_part.astype(BF), "c")
    dmiddle, ba_own, do_part, do_other = call(
        middle_back_kernel,
        [((TOK, D), F32), ((TOK, OWN), BF), ((TOK, OWN), F32), ((TOK, LANES), BF)],
        (core, dn2_part, dn2_got, middle, cot, g2, kf, vo_w),
        4 * TOK * D * 576,
        places={0: SMEM, 3: FAR, 4: FAR, 7: FAR, 8: FAR},
    )
    do_got = send(do_other, "c")
    dqk_raw, dv_raw, de = call(
        attend_back_kernel,
        [((TOK, 768), F32), ((TOK, 256), F32), ((TOK, 384), BF)],
        (qk, kv, kv_early) + doc_args + (do_part, do_got),
        10 * TOK * 576 * 256,
        places={0: FAR, 1: FAR, 2: FAR},
    )
    d_got = send(de, "early")
    dqk, dv, dn1_part = call(
        project_back_kernel,
        [((TOK, 768), BF), ((TOK, 256), BF), ((TOK, D), F32)],
        (dqk_raw, dv_raw, d_got, cosine, sine, qk_w, vo_w),
        2 * TOK * D * 1024,
        places={5: FAR, 6: FAR},
    )
    dn1_part = dn1_part.reshape(2, ROWS, D)
    o_all = jnp.where(
        first_core,
        jnp.concatenate([o[:, :OWN], o_got[:, :OWN]], axis=1),
        jnp.concatenate([o_got[:, :OWN], o[:, :OWN]], axis=1),
    )
    o_slots = mm_t(from_slots, o_all).astype(BF).reshape(16, 4, 24, TOK)
    dqkv = jnp.concatenate([dqk, dv], axis=1)

    def over_x(lhs, rhs):
        return reduce_ring(
            lambda step: mm(pick(lhs, 1, wrap(x, step)).reshape(384, TOK), rhs), "x"
        )

    ba_wide = jnp.concatenate([ba_own, jnp.zeros((TOK, LANES - OWN), BF)], axis=1)
    attention_sum = jnp.concatenate([over_x(n1_slots, dqkv), over_x(o_slots, ba_wide)], axis=1)
    attention_sum = reduce_direct(attention_sum.reshape(4, 4, 24, 2 * PART), "z", z, 1)
    attention_sum, feed_sum = lax.optimization_barrier((attention_sum, feed_sum))
    a24 = reduce_direct(attention_sum, "y", y, 0)
    dn1 = pick(dn1_part, 0, c) + send(pick(dn1_part, 0, 1 - c).astype(BF), "c")
    hat_own, scale_own = normal(tokens.astype(F32))
    back_tokens = pick(dmiddle.reshape(2, ROWS, D), 0, c) + normal_pull(
        hat_own, scale_own, dn1 * g1
    )

    def swap(own, other):
        got = send(other.astype(BF), "c").astype(F32)
        return jnp.where(first_core, own, got), jnp.where(first_core, got, own)

    def hidden_join(zero, one):
        return jnp.stack([zero.reshape(9, 32, 48), one.reshape(9, 32, 48)], axis=2).reshape(9, FF)

    feed24 = reduce_direct(feed_sum.astype(F32).reshape(4, 24, WIDE), "x", x, 0)
    back_down = feed24[:, FF:]
    core0, core1 = feed24[:9, :FF], feed24[9:18, :FF]
    f0, f1 = swap(jnp.where(first_core, core0, core1), jnp.where(first_core, core1, core0))
    back_gate = hidden_join(f0[:, :HALF], f1[:, :HALF])
    back_up = hidden_join(f0[:, HALF:], f1[:, HALF:])
    core0, core1 = a24[:9], a24[9:18]
    a0, a1 = swap(jnp.where(first_core, core0, core1), jnp.where(first_core, core1, core0))
    join = lambda low, high: jnp.concatenate([a0[:, low:high], a1[:, low:high]], axis=1)
    back_query = join(192, 768)
    back_key = join(0, 192)
    back_value = join(832, 1024)
    back_out = join(1024, 1600)
    dots = lambda weight, grad: jnp.sum(weight.astype(F32) * grad, axis=1)
    back_one = (
        dots(wq, back_query) + dots(wk, back_key) + dots(wv, back_value)
    ) / gain_one.astype(F32)
    back_two = (dots(wg, back_gate) + dots(wu, back_up)) / gain_two.astype(F32)
    return (
        mixed.astype(BF),
        back_tokens,
        back_one,
        back_query,
        back_key,
        back_value,
        back_out,
        back_two,
        back_gate,
        back_up,
        back_down,
    )


def solution(mesh):
    fine = Mesh(mesh.devices.reshape([SIZES[name] for name in AXES]), AXES)
    row, rows = P(AXES), P(AXES, None)
    in_specs = (rows, row, row, row, rows, rows, rows, rows, row, rows, rows, rows, rows)
    out_specs = (rows, rows, row, rows, rows, rows, rows, row, rows, rows, rows)
    return jax.shard_map(
        on_device, mesh=fine, in_specs=in_specs, out_specs=out_specs, check_vma=False
    )
```

```python
import math

import jax
import jax.numpy as jnp
from jax import lax
from jax.experimental import pallas as pl
from jax.experimental.pallas import tpu as pltpu
from jax.sharding import Mesh, PartitionSpec as P

H = 18
KV = 6
HD = 64
D = 1152
FF = 3072
ROWS = 128
EPSILON = 1e-05
NEGATIVE = -1e30
AXES = ("y", "z", "xh", "c", "xl")
SIZES = {"y": 4, "z": 4, "xh": 2, "c": 2, "xl": 2}
BF = jnp.bfloat16
F32 = jnp.float32
HQ = H // 2
HK = KV // 2
GROUP = H // KV
PART = 832
VPAD = 256
OWN = 576
LANES = 640
TOK = 2 * ROWS
HALF = FF // 2
SLOTS = 1536
WIDE = FF + D
CHIPS = ("y", "z", "xh", "xl")


def places():
    for y in range(4):
        for z in range(4):
            for xh in range(2):
                for c in range(2):
                    for xl in range(2):
                        yield {"y": y, "z": z, "xh": xh, "c": c, "xl": xl}


def index_of(place):
    total = 0
    for name in AXES:
        total = total * SIZES[name] + place[name]
    return total


def shift_pairs(axis, step):
    pairs = []
    for place in places():
        other = dict(place)
        if axis == "x":
            spot = (place["xh"] * 2 + place["xl"] + step) % 4
            other["xh"], other["xl"] = spot // 2, spot % 2
        elif axis == "c":
            other["c"] = 1 - place["c"]
        else:
            other[axis] = (place[axis] + step) % 4
        pairs.append((index_of(place), index_of(other)))
    return pairs


PAIRS = {(axis, step): shift_pairs(axis, step) for axis in "xyz" for step in (1, -1, 2)}
PAIRS["c"] = shift_pairs("c", 1)
PAIRS["late"] = [
    (index_of(place), index_of({**place, "xl": 1})) for place in places() if place["xl"] == 0
]
PAIRS["early"] = [
    (index_of(place), index_of({**place, "xl": 0})) for place in places() if place["xl"] == 1
]


def send(value, key):
    return lax.ppermute(value, AXES, PAIRS[key])


def mm(left, right):
    return jnp.dot(left, right, preferred_element_type=F32)


def mm_t(left, right):
    return lax.dot_general(left, right, (((1,), (1,)), ((), ())), preferred_element_type=F32)


def inner(left, right):
    return lax.dot_general(left, right, (((0,), (0,)), ((), ())), preferred_element_type=F32)


def put(full, block, axis, index):
    starts = [0] * full.ndim
    starts[axis] = index
    return lax.dynamic_update_slice(full, jnp.expand_dims(block, axis), starts)


def pick(array, axis, index):
    return lax.dynamic_index_in_dim(array, index, axis, keepdims=False)


def wrap(spot, step):
    return lax.rem(spot + step + 4, 4)


def gather_direct(block, axis, spot, dim):
    shape = list(block.shape)
    shape.insert(dim, 4)
    full = jnp.zeros(shape, block.dtype)
    full = put(full, block, dim, spot)
    full = put(full, send(block, (axis, 1)), dim, wrap(spot, -1))
    full = put(full, send(block, (axis, -1)), dim, wrap(spot, 1))
    return put(full, send(block, (axis, 2)), dim, wrap(spot, 2))


def gather_ring(block, axis, spot, dim):
    half = block.shape[-2] // 2
    shape = list(block.shape)
    shape.insert(dim, 4)
    left = send(block, (axis, 1))
    right = send(block, (axis, -1))
    low = send(left[..., :half, :], (axis, 1))
    high = send(right[..., half:, :], (axis, -1))
    full = jnp.zeros(shape, block.dtype)
    full = put(full, block, dim, spot)
    full = put(full, left, dim, wrap(spot, -1))
    full = put(full, right, dim, wrap(spot, 1))
    far = jnp.concatenate([low, high], axis=-2)
    return put(full, far, dim, wrap(spot, 2))


def reduce_direct(parts, axis, spot, dim):
    low = parts.astype(BF)
    first = send(pick(low, dim, wrap(spot, 1)), (axis, 1))
    second = send(pick(low, dim, wrap(spot, -1)), (axis, -1))
    third = send(pick(low, dim, wrap(spot, 2)), (axis, 2))
    return pick(parts, dim, spot) + first + second + third


def normal(values):
    scale = lax.rsqrt(jnp.mean(values * values, axis=-1, keepdims=True) + EPSILON)
    return values * scale, scale


def normal_pull(hat, scale, grad):
    return scale * (grad - hat * jnp.mean(grad * hat, axis=-1, keepdims=True))


def halves_swapped(values):
    lane = lax.broadcasted_iota(jnp.int32, values.shape, 1)
    return jnp.where(
        lane % HD < HD // 2, pltpu.roll(values, 96, 1), pltpu.roll(values, 32, 1)
    )


SMEM = pl.BlockSpec(memory_space=pltpu.SMEM)
HERE = pl.BlockSpec(memory_space=pltpu.HBM)
FAR = "far"


def call(body, outs, args, flops, scratch=(), places=None, megabytes=24):
    total = sum(math.prod(a.shape) * a.dtype.itemsize for a in args)
    total += sum(math.prod(shape) * jnp.dtype(kind).itemsize for shape, kind in outs)
    places = places or {}

    def spec(index, shape):
        if places.get(index, FAR) is not FAR:
            return places[index]
        return pl.BlockSpec(
            shape, lambda i: (0,) * len(shape), pipeline_mode=pl.Buffered(1)
        )

    in_specs = [spec(i, a.shape) for i, a in enumerate(args)]
    out_specs = [spec(len(args) + i, shape) for i, (shape, _) in enumerate(outs)]
    return pl.pallas_call(
        body,
        grid=(1,),
        out_shape=[
            pltpu.HBM(shape, kind)
            if places.get(len(args) + i) in (HERE, FAR)
            else jax.ShapeDtypeStruct(shape, kind)
            for i, (shape, kind) in enumerate(outs)
        ],
        in_specs=in_specs,
        out_specs=out_specs,
        scratch_shapes=list(scratch),
        compiler_params=pltpu.CompilerParams(vmem_limit_bytes=megabytes << 20),
        cost_estimate=pl.CostEstimate(flops=flops, bytes_accessed=total, transcendentals=0),
    )(
        *[
            pltpu.with_memory_space_constraint(a, pltpu.HBM)
            if places.get(i) in (HERE, FAR)
            else a
            for i, a in enumerate(args)
        ]
    )


SCALE = 1.0 / math.sqrt(HD)


def sequence(s):
    return pl.ds(pl.multiple_of(s * ROWS, ROWS), ROWS)


def each_sequence(body):
    def step(s, carry):
        body(s)
        return carry

    lax.fori_loop(0, 2, step, 0)


def project_kernel(
    x_ref, g_ref, wqk_ref, wvo_ref, cos_ref, sin_ref, doc_ref,
    n1_ref, qk_ref, kv_ref, raw_ref, v_ref,
):
    hat, _ = normal(x_ref[...].astype(F32))
    n1 = (hat * g_ref[...]).astype(BF)
    n1_ref[...] = n1
    raw_ref[...] = mm(n1, wqk_ref[:, :768])
    v_ref[...] = mm(n1, wvo_ref[:, :VPAD]).astype(BF)
    cosine, sine = cos_ref[...], sin_ref[...]
    lane = lax.broadcasted_iota(jnp.int32, (ROWS, 128), 1)

    def turn(s):
        rows = sequence(s)
        for j in range(6):
            at = slice(j * 128, j * 128 + 128)
            tile = raw_ref[rows, at]
            turned = (tile * cosine + halves_swapped(tile) * sine).astype(BF)
            qk_ref[rows, at] = turned
            if j == 0:
                kv_ref[rows, 0:128] = turned
            if j == 1:
                kv_ref[rows, 128:256] = jnp.where(lane < 64, turned, v_ref[rows, 0:128])
        kv_ref[rows, 256:384] = v_ref[rows, 128:256]

    each_sequence(turn)
    kv_ref[TOK:, :] = doc_ref[...]


def head_data(h, qk, kv, early):
    base = 192 + h * 192
    q = jnp.concatenate(
        [qk[:, base + 64 * g : base + 64 * g + 64] for g in range(GROUP)], axis=0
    )
    keys, vals = slice(64 * h, 64 * h + 64), slice(192 + 64 * h, 256 + 64 * h)
    return q, early[:, keys], kv[:, keys], early[:, vals], kv[:, vals]


def early_docs(late_ref, early_ref, row_ref):
    rows = early_ref[TOK:, :ROWS].astype(F32)
    row_ref[...] = jnp.where(late_ref[0] == 1, rows, -1.0)


def masks(s, dcol_ref, drow_ref, derow_ref):
    col = dcol_ref[sequence(s), :]
    at = lax.broadcasted_iota(jnp.int32, (ROWS, ROWS), 0)
    to = lax.broadcasted_iota(jnp.int32, (ROWS, ROWS), 1)
    mask_o = (to <= at) & (col == drow_ref[s])
    mask_e = col == derow_ref[pl.ds(s, 1), :]
    wide = lambda m: jnp.concatenate([jnp.where(m, 0.0, NEGATIVE)] * GROUP, axis=0)
    return wide(mask_e), wide(mask_o)


def softmax(q, ke, ko, mask_e, mask_o):
    se = jnp.where(mask_e == 0.0, mm_t(q, ke) * SCALE, NEGATIVE)
    so = jnp.where(mask_o == 0.0, mm_t(q, ko) * SCALE, NEGATIVE)
    top = jnp.maximum(
        jnp.max(se, axis=-1, keepdims=True), jnp.max(so, axis=-1, keepdims=True)
    )
    ee, eo = jnp.exp(se - top), jnp.exp(so - top)
    total = jnp.sum(ee, axis=-1, keepdims=True) + jnp.sum(eo, axis=-1, keepdims=True)
    return ee / total, eo / total


def split_heads(stacked):
    return [stacked[g * ROWS : g * ROWS + ROWS] for g in range(GROUP)]


def attend_kernel(qk_ref, kv_ref, early_ref, late_ref, dcol_ref, drow_ref, o_ref, derow_ref):
    early_docs(late_ref, early_ref, derow_ref)

    def one(s):
        rows = sequence(s)
        qk, kv, early = qk_ref[rows, :], kv_ref[rows, :], early_ref[rows, :]
        mask_e, mask_o = masks(s, dcol_ref, drow_ref, derow_ref)
        pieces = []
        for h in range(HK):
            q, ke, ko, ve, vo = head_data(h, qk, kv, early)
            pe, po = softmax(q, ke, ko, mask_e, mask_o)
            pieces += split_heads(mm(pe.astype(BF), ve) + mm(po.astype(BF), vo))
        pieces.append(jnp.zeros((ROWS, LANES - OWN), F32))
        o_ref[rows, :] = jnp.concatenate(pieces, axis=1).astype(BF)

    each_sequence(one)


def attend_back_kernel(
    qk_ref, kv_ref, early_ref, late_ref, dcol_ref, drow_ref, do_ref, got_ref,
    dqk_ref, dv_ref, de_ref, derow_ref,
):
    early_docs(late_ref, early_ref, derow_ref)

    def one(s):
        rows = sequence(s)
        qk, kv, early = qk_ref[rows, :], kv_ref[rows, :], early_ref[rows, :]
        do_all = (do_ref[rows, :] + got_ref[rows, :OWN].astype(F32)).astype(BF)
        mask_e, mask_o = masks(s, dcol_ref, drow_ref, derow_ref)
        dqs, dke, dko, dve, dvo = [], [], [], [], []
        for h in range(HK):
            q, ke, ko, ve, vo = head_data(h, qk, kv, early)
            pe, po = softmax(q, ke, ko, mask_e, mask_o)
            do = jnp.concatenate(
                [do_all[:, (GROUP * h + g) * 64 : (GROUP * h + g) * 64 + 64] for g in range(GROUP)],
                axis=0,
            )
            dpe, dpo = mm_t(do, ve), mm_t(do, vo)
            centre = jnp.sum(pe * dpe, axis=-1, keepdims=True) + jnp.sum(
                po * dpo, axis=-1, keepdims=True
            )
            dse = (pe * (dpe - centre)).astype(BF)
            dso = (po * (dpo - centre)).astype(BF)
            dqs += split_heads((mm(dse, ke) + mm(dso, ko)) * SCALE)
            dke.append(inner(dse, q) * SCALE)
            dko.append(inner(dso, q) * SCALE)
            dve.append(inner(pe.astype(BF), do))
            dvo.append(inner(po.astype(BF), do))
        dqk_ref[rows, :] = jnp.concatenate(dko + dqs, axis=1)
        dv_ref[rows, :] = jnp.concatenate([jnp.zeros((ROWS, 64), F32)] + dvo, axis=1)
        de_ref[rows, :] = jnp.concatenate(dke + dve, axis=1).astype(BF)

    each_sequence(one)


def project_back_kernel(
    dqk_ref, dv_ref, got_ref, cos_ref, sin_ref, wqk_ref, wvo_ref, low_ref, dn1_ref
):
    cosine, sine = cos_ref[...], sin_ref[...]
    lane = lax.broadcasted_iota(jnp.int32, (ROWS, 128), 1)

    def turn(s):
        rows = sequence(s)
        got = got_ref[rows, :].astype(F32)
        for j in range(6):
            at = slice(j * 128, j * 128 + 128)
            tile = dqk_ref[rows, at]
            if j == 0:
                tile = tile + got[:, 0:128]
            if j == 1:
                tile = tile + jnp.where(lane < 64, got[:, 128:256], 0.0)
            low_ref[rows, at] = (tile * cosine - halves_swapped(tile) * sine).astype(BF)
        dv0 = dv_ref[rows, 0:128] + jnp.where(lane < 64, 0.0, got[:, 128:256])
        low_ref[rows, 768:896] = dv0.astype(BF)
        low_ref[rows, 896:1024] = (dv_ref[rows, 128:256] + got[:, 256:384]).astype(BF)

    each_sequence(turn)
    dn1_ref[...] = mm_t(low_ref[:, :768], wqk_ref[:, :768]) + mm_t(
        low_ref[:, 768:], wvo_ref[:, :VPAD]
    )


def out_chunks_kernel(x_ref, o_ref, ba_ref, own_ref, ahead_ref, behind_ref, far_ref):
    for step, out in ((0, own_ref), (1, ahead_ref), (-1, behind_ref), (2, far_ref)):
        out[...] = mm(o_ref[wrap(x_ref[0], step)], ba_ref[...]).astype(BF)


def far_kernel(x_ref, n1_ref, dqkv_ref, low_ref, high_ref):
    chunk = mm(n1_ref[wrap(x_ref[0], 2)], dqkv_ref[...]).astype(BF)
    low_ref[...] = chunk[:144]
    high_ref[...] = chunk[144:]


def near_kernel(x_ref, n1_ref, dqkv_ref, low_ref, high_ref, ahead_ref, behind_ref):
    for step, out, add, first in ((1, ahead_ref, low_ref, 0), (-1, behind_ref, high_ref, 144)):
        chunk = mm(n1_ref[wrap(x_ref[0], step)], dqkv_ref[...])
        rows = slice(first, first + 144)
        out[...] = chunk.astype(BF)
        out[rows, :] = (chunk[rows] + add[...].astype(F32)).astype(BF)


def own_kernel(
    x_ref, n1_ref, dqkv_ref, first_ref, second_ref,
    o0_ref, o1_ref, o2_ref, o3_ref, order_ref, out_ref, sum_ref,
):
    total = mm(n1_ref[x_ref[0]], dqkv_ref[...])
    total = total + first_ref[...].astype(F32) + second_ref[...].astype(F32)
    sum_ref[:, :1024] = total.astype(BF)
    total = o0_ref[...].astype(F32) + o1_ref[...].astype(F32)
    total = total + o2_ref[...].astype(F32) + o3_ref[...].astype(F32)
    sum_ref[:, 1024:] = total.astype(BF)
    out_ref[...] = mm(order_ref[...], sum_ref[...]).astype(BF)


def out_rows(w_ref, c):
    return w_ref[pl.ds(pl.multiple_of(c * OWN, 64), OWN), VPAD:]


def out_kernel(c_ref, o_ref, got_ref, w_ref, kf_ref, part_ref):
    c = c_ref[0]
    total = mm(o_ref[:, :OWN], out_rows(w_ref, c)) + mm(
        got_ref[:, :OWN], out_rows(w_ref, 1 - c)
    )
    part_ref[:, :OWN] = kf_ref[...] * total
    part_ref[:, OWN:] = jnp.zeros((TOK, LANES - OWN), F32)


def feed_kernel(
    c_ref, g_ref, x_hbm, part_hbm, got_hbm, fs_hbm, bm_hbm, w_ref,
    mid_hbm, grad_ref, act_hbm, dgu_hbm,
    x_ref, part_ref, got_ref, fs_ref, bm_ref, mid_ref, act_ref, dgu_ref,
    n2_ref, n2t_ref, wb, gb, in_sem, out_sem, side_sem,
):
    tile = 512
    steps = HALF // tile

    def spots(t):
        at = pl.multiple_of(t * tile, tile)
        return (
            (slice(None), pl.ds(at, tile)),
            (slice(None), pl.ds(HALF + at, tile)),
            (pl.ds(at, tile), pl.ds(FF, D)),
        )

    def loads(t):
        return [
            pltpu.make_async_copy(w_ref.at[spot], wb.at[spot], in_sem.at[t, i])
            for i, spot in enumerate(spots(t))
        ]

    def stores(t):
        return [
            pltpu.make_async_copy(gb.at[spot], grad_ref.at[spot], out_sem.at[t, i])
            for i, spot in enumerate(spots(t))
        ]

    sides = [
        pltpu.make_async_copy(src, dst, side_sem.at[i])
        for i, (src, dst) in enumerate(
            (
                (x_hbm, x_ref), (part_hbm, part_ref), (got_hbm, got_ref),
                (fs_hbm, fs_ref), (bm_hbm, bm_ref), (mid_ref, mid_hbm),
                (act_ref, act_hbm), (dgu_ref, dgu_hbm),
            )
        )
    ]
    for copy in sides[:5] + loads(0):
        copy.start()
    for copy in sides[:3]:
        copy.wait()
    for t in range(1, steps):
        for copy in loads(t):
            copy.start()

    first = c_ref[0] == 0
    part, got = part_ref[:, :OWN], got_ref[:, :OWN]
    low = jnp.where(first, part, got)
    high = jnp.where(first, got, part)
    middle = x_ref[...].astype(F32) + jnp.concatenate([low, high], axis=1)
    mid_ref[...] = middle
    sides[5].start()
    hat, _ = normal(middle)
    normed = (hat * g_ref[...]).astype(BF)
    for copy in sides[3:5]:
        copy.wait()
    n2_ref[...] = mm_t(normed, fs_ref[...]).astype(BF)
    n2t_ref[...] = n2_ref[...].T

    def step(t, carry):
        for copy in loads(t):
            copy.wait()
        gate_at, up_at, down_at = spots(t)
        n2, n2t, bm = n2_ref[...], n2t_ref[...], bm_ref[...]
        gate = mm(n2, wb[gate_at])
        up = mm(n2, wb[up_at])
        dact = mm_t(bm, wb[down_at])
        sig = jax.nn.sigmoid(gate)
        silu = gate * sig
        act = (silu * up).astype(BF)
        dgate = (dact * up * (sig * (1.0 + gate * (1.0 - sig)))).astype(BF)
        dup = (dact * silu).astype(BF)
        act_ref[gate_at] = act
        dgu_ref[gate_at] = dgate
        dgu_ref[up_at] = dup
        gb[gate_at] = mm(n2t, dgate).astype(BF)
        gb[up_at] = mm(n2t, dup).astype(BF)
        gb[down_at] = inner(act, bm).astype(BF)
        for copy in stores(t):
            copy.start()
        return carry

    lax.fori_loop(0, steps, step, 0)
    for copy in sides[6:]:
        copy.start()
    for copy in sides[5:]:
        copy.wait()
    for t in range(steps):
        for copy in stores(t):
            copy.wait()


def feed_back_kernel(dgu_ref, w_ref, fs_ref, dn2_ref, wb, dgt_ref, slots_ref, sem):
    tile = 256
    steps = SLOTS // tile

    def load(t):
        rows = pl.ds(pl.multiple_of(t * tile, tile), tile)
        return pltpu.make_async_copy(w_ref.at[rows, pl.ds(0, FF)], wb.at[rows, :], sem.at[t])

    for t in range(steps):
        load(t).start()
    dgt_ref[...] = dgu_ref[...].T

    def step(t, carry):
        load(t).wait()
        rows = pl.ds(pl.multiple_of(t * tile, tile), tile)
        slots_ref[rows, :] = mm(wb[rows, :], dgt_ref[...]).astype(BF)
        return carry

    lax.fori_loop(0, steps, step, 0)
    dn2_ref[...] = inner(slots_ref[...], fs_ref[...])


def down_kernel(act_ref, w_ref, down_ref, wb, sem):
    load = pltpu.make_async_copy(w_ref.at[:, pl.ds(FF, D)], wb, sem)
    load.start()
    load.wait()
    down_ref[...] = mm(act_ref[...], wb[...])


def middle_back_kernel(
    c_ref, part_ref, got_ref, mid_ref, cot_ref, g_ref, kf_ref, w_ref,
    dmid_ref, ba_ref, do_ref, other_ref,
):
    c = c_ref[0]
    dn2 = part_ref[...] + got_ref[...].astype(F32)
    hat, scale = normal(mid_ref[...])
    dmiddle = cot_ref[...] + normal_pull(hat, scale, dn2 * g_ref[...])
    dmid_ref[...] = dmiddle
    ba = kf_ref[...] * dmiddle
    half = jnp.where(c == 0, ba[:, :576], ba[:, 576:]).astype(BF)
    ba_ref[:, :OWN] = half
    ba_ref[:, OWN:] = jnp.zeros((TOK, LANES - OWN), BF)
    do_ref[...] = mm_t(half, out_rows(w_ref, c))
    other_ref[:, :OWN] = mm_t(half, out_rows(w_ref, 1 - c)).astype(BF)
    other_ref[:, OWN:] = jnp.zeros((TOK, LANES - OWN), BF)


def on_device(
    tokens, doc_ids, keep, gain_one, wq, wk, wv, wo, gain_two, wg, wu, wd, cotangent
):
    y, z, c = lax.axis_index("y"), lax.axis_index("z"), lax.axis_index("c")
    xl = lax.axis_index("xl")
    x = lax.axis_index("xh") * 2 + xl
    first_core = c == 0

    def both(own, other):
        return jnp.where(first_core, jnp.stack([own, other]), jnp.stack([other, own]))

    def attention_half(h):
        return jnp.concatenate(
            [
                wk[:, h * 192 : h * 192 + 192],
                wq[:, h * 576 : h * 576 + 576],
                gain_one[:, None],
                gain_two[:, None],
                jnp.zeros((9, PART - 770), BF),
                jnp.zeros((9, VPAD - 192), BF),
                wv[:, h * 192 : h * 192 + 192],
                wo[:, h * 576 : h * 576 + 576],
            ],
            axis=1,
        )

    def own_other(zero, one):
        return jnp.where(first_core, zero, one), jnp.where(first_core, one, zero)

    r = lax.broadcasted_iota(jnp.int32, (72, 96), 0)
    s = lax.broadcasted_iota(jnp.int32, (72, 96), 1)
    xh_r, rest = r // 36, r % 36
    c_r, rest = rest // 18, rest % 18
    xl_r, i_r = rest // 9, rest % 9
    k_r = lax.rem(xh_r * 2 + xl_r - x + 4, 4)
    select = (s == k_r * 24 + jnp.where(c_r == c, 0, 9) + i_r).astype(BF)

    def rows72(own, got):
        block = jnp.concatenate([own, got, jnp.zeros((6, own.shape[1]), BF)], axis=0)
        stacked = jnp.concatenate(
            [block, send(block, ("x", -1)), send(block, ("x", 2)), send(block, ("x", 1))], axis=0
        )
        return mm(select, stacked).astype(BF)

    def gather_zy(block):
        return gather_ring(
            gather_direct(block, "z", z, 0).reshape(288, -1), "y", y, 0
        ).reshape(D, -1)

    def gather_yz(block):
        return gather_ring(gather_direct(block, "y", y, 0), "z", z, 1).reshape(D, -1)

    by_core = jnp.concatenate([wg, wu]).reshape(18, 32, 2, 48)
    halves = [by_core[:, :, h, :].reshape(18, HALF) for h in range(2)]
    zero_half, one_half = [jnp.concatenate([h[:9], h[9:]], axis=1) for h in halves]
    own, other = own_other(zero_half, one_half)
    got = send(other, "c")
    feed_block = jnp.concatenate(
        [jnp.where(first_core, own, got), jnp.where(first_core, got, own), jnp.zeros((6, FF), BF)]
    )
    feed_w = lax.all_gather(
        jnp.concatenate([feed_block, wd], axis=1), CHIPS, axis=0, tiled=True
    )
    a_own, a_other = own_other(attention_half(0), attention_half(1))
    marks = jnp.stack([doc_ids, keep])
    a_got, x_got, marks_got, cot_got = lax.optimization_barrier(
        tuple(send(v, "c") for v in (a_other, tokens, marks, cotangent))
    )
    x_all = both(tokens, x_got).reshape(TOK, D)
    marks = both(marks, marks_got)
    docs, kf = marks[:, 0].astype(F32), marks[:, 1].astype(F32).reshape(TOK, 1)
    doc_args = (docs.reshape(TOK, 1), docs.reshape(2, 1, ROWS))
    doc_rows = jnp.pad(docs, ((0, 14), (0, 384 - ROWS))).astype(BF)
    cot = both(cotangent, cot_got).reshape(TOK, D)

    a72 = rows72(a_own, a_got)
    slot = jnp.arange(SLOTS, dtype=jnp.int32)
    chip, inside = slot // 24, slot % 24
    of_slot = (chip // 2) * 36 + (inside // 9) * 18 + (chip % 2) * 9 + inside % 9
    of_slot = jnp.where(inside < 18, of_slot, -1)
    spot = jnp.arange(D, dtype=jnp.int32)
    along, plane, inside = spot // 288, (spot % 288) // 18, spot % 18
    of_x = plane * 72 + (along // 2) * 36 + (inside // 9) * 18 + (along % 2) * 9 + inside % 9
    spot = jnp.arange(288, dtype=jnp.int32)
    of_z = ((spot % 72) // 18 * 4 + spot // 72) * 18 + spot % 18
    spot = jnp.arange(96, dtype=jnp.int32)
    of_y = jnp.where(spot % 24 < 18, spot // 24 * 18 + spot % 24, -1)
    orders, a72 = lax.optimization_barrier(((of_slot, of_x, of_z, of_y), a72))

    def one_hot(rows, columns):
        return (
            rows[:, None] == lax.broadcasted_iota(jnp.int32, (rows.shape[0], columns), 1)
        ).astype(BF)

    from_slots, by_x, by_z, by_y = [
        one_hot(rows, columns) for rows, columns in zip(orders, (D, D, 288, 72))
    ]

    qk_w = gather_zy(a72[:, :PART])
    vo_w = gather_yz(a72[:, PART:])

    unit = (
        lax.broadcasted_iota(jnp.int32, (8, 64), 1)
        == lax.broadcasted_iota(jnp.int32, (8, 64), 0)
    ).astype(BF)
    gains = mm_t(unit, qk_w[:, 768:])
    g1, g2 = gains[0:1], gains[1:2]

    half = HD // 2
    freqs = 10000.0 ** (-(jnp.arange(half).astype(F32) * 2.0 / HD))
    position = xl * ROWS + jnp.arange(ROWS, dtype=jnp.int32)
    angle = position.astype(F32)[:, None] * freqs[None, :]
    cosine = jnp.tile(jnp.cos(angle), (1, 4))
    sine = jnp.sin(angle)
    sine = jnp.concatenate([-sine, sine, -sine, sine], axis=1)
    core = c.astype(jnp.int32).reshape(1)
    bm = (kf * cot).astype(BF)
    early_work = (x_all, from_slots, bm, cosine, sine, kf, cot, by_x, doc_rows) + doc_args
    early_work, a_blocks = lax.optimization_barrier((early_work, (qk_w, vo_w)))
    x_all, from_slots, bm, cosine, sine, kf, cot, by_x, doc_rows = early_work[:9]
    late = (xl == 1).astype(jnp.int32).reshape(1)
    doc_args = (late,) + early_work[9:]
    qk_w, vo_w = a_blocks

    n1, qk, kv = call(
        project_kernel,
        [((TOK, D), BF), ((TOK, 768), BF), ((TOK + 16, 384), BF)],
        (x_all, g1, qk_w, vo_w, cosine, sine, doc_rows),
        2 * TOK * D * 1024,
        scratch=[pltpu.VMEM((TOK, 768), F32), pltpu.VMEM((TOK, VPAD), BF)],
        places={0: FAR, 2: FAR, 3: FAR, 7: FAR, 8: FAR, 9: FAR},
    )
    n1_x = mm_t(by_x, n1).astype(BF).reshape(4, 288, TOK)
    kv_early, n1_x = lax.optimization_barrier((send(kv, "late"), n1_x))
    (o,) = call(
        attend_kernel,
        [((TOK, LANES), BF)],
        (qk, kv, kv_early) + doc_args,
        4 * TOK * 576 * 256,
        scratch=[pltpu.VMEM((16, ROWS), F32)],
        places={0: FAR, 1: FAR, 2: FAR, 3: SMEM, 6: FAR},
    )
    o_got = send(o, "c")
    (part,) = call(
        out_kernel,
        [((TOK, LANES), F32)],
        (core, o, o_got, vo_w, kf),
        2 * TOK * D * 576,
        places={0: SMEM, 1: FAR, 2: FAR, 3: FAR, 5: FAR},
    )
    part_got = send(part, "c")
    middle, feed_grad, act, dgu = call(
        feed_kernel,
        [((TOK, D), F32), ((SLOTS, WIDE), BF), ((TOK, HALF), BF), ((TOK, FF), BF)],
        (core, g2, x_all, part, part_got, from_slots, bm, feed_w),
        4 * TOK * SLOTS * (WIDE + D),
        scratch=[
            pltpu.VMEM((TOK, D), BF),
            pltpu.VMEM((TOK, LANES), F32),
            pltpu.VMEM((TOK, LANES), F32),
            pltpu.VMEM((SLOTS, D), BF),
            pltpu.VMEM((TOK, D), BF),
            pltpu.VMEM((TOK, D), F32),
            pltpu.VMEM((TOK, HALF), BF),
            pltpu.VMEM((TOK, FF), BF),
            pltpu.VMEM((TOK, SLOTS), BF),
            pltpu.VMEM((SLOTS, TOK), BF),
            pltpu.VMEM((SLOTS, WIDE), BF),
            pltpu.VMEM((SLOTS, WIDE), BF),
            pltpu.SemaphoreType.DMA((3, 3)),
            pltpu.SemaphoreType.DMA((3, 3)),
            pltpu.SemaphoreType.DMA((8,)),
        ],
        places={0: SMEM} | {i: HERE for i in range(2, 12)},
        megabytes=52,
    )
    feed_sum = lax.psum_scatter(feed_grad, ("y", "z"), scatter_dimension=0, tiled=True)
    (dn2_part,) = call(
        feed_back_kernel,
        [((TOK, D), F32)],
        (dgu, feed_w, from_slots),
        2 * TOK * SLOTS * (FF + D),
        scratch=[
            pltpu.VMEM((SLOTS, FF), BF),
            pltpu.VMEM((FF, TOK), BF),
            pltpu.VMEM((SLOTS, TOK), BF),
            pltpu.SemaphoreType.DMA((6,)),
        ],
        megabytes=40,
        places={0: FAR, 1: HERE, 2: FAR},
    )
    dn2_got = send(dn2_part.astype(BF), "c")
    dmiddle, ba_own, do_part, do_other = call(
        middle_back_kernel,
        [((TOK, D), F32), ((TOK, LANES), BF), ((TOK, OWN), F32), ((TOK, LANES), BF)],
        (core, dn2_part, dn2_got, middle, cot, g2, kf, vo_w),
        4 * TOK * D * 576,
        places={0: SMEM, 3: FAR, 4: FAR, 7: FAR, 8: FAR},
    )
    do_got = send(do_other, "c")
    o_all = jnp.where(
        first_core,
        jnp.concatenate([o[:, :OWN], o_got[:, :OWN]], axis=1),
        jnp.concatenate([o_got[:, :OWN], o[:, :OWN]], axis=1),
    )
    o_x = mm_t(by_x, o_all).astype(BF).reshape(4, 288, TOK)
    spot_x = x.astype(jnp.int32).reshape(1)
    out_sums = call(
        out_chunks_kernel,
        [((288, LANES), BF)] * 4,
        (spot_x, o_x, ba_own),
        2 * D * TOK * LANES,
        places={0: SMEM},
    )
    out_sums = [
        out_sums[0],
        send(out_sums[1], ("x", 1)),
        send(out_sums[2], ("x", -1)),
        send(out_sums[3], ("x", 2)),
    ]
    dqk_raw, dv_raw, de = call(
        attend_back_kernel,
        [((TOK, 768), F32), ((TOK, 256), F32), ((TOK, 384), BF)],
        (qk, kv, kv_early) + doc_args + (do_part, do_got),
        10 * TOK * 576 * 256,
        scratch=[pltpu.VMEM((16, ROWS), F32)],
        places={0: FAR, 1: FAR, 2: FAR, 3: SMEM},
    )
    d_got = send(de, "early")
    dqkv, dn1_part = call(
        project_back_kernel,
        [((TOK, 1024), BF), ((TOK, D), F32)],
        (dqk_raw, dv_raw, d_got, cosine, sine, qk_w, vo_w),
        2 * TOK * D * 1024,
        places={5: FAR, 6: FAR},
    )
    dn1_part = dn1_part.reshape(2, ROWS, D)
    grads = (spot_x, n1_x, dqkv)
    low, high = call(
        far_kernel,
        [((144, 1024), BF), ((144, 1024), BF)],
        grads,
        2 * 288 * TOK * 1024,
        places={0: SMEM},
    )
    low, high, act = lax.optimization_barrier((low, high, act))
    ahead, behind = call(
        near_kernel,
        [((288, 1024), BF), ((288, 1024), BF)],
        grads + (send(low, ("x", 1)), send(high, ("x", -1))),
        4 * 288 * TOK * 1024,
        places={0: SMEM},
    )
    (by_place,) = call(
        own_kernel,
        [((288, 2 * PART), BF)],
        grads + (send(ahead, ("x", 1)), send(behind, ("x", -1))) + tuple(out_sums) + (by_z,),
        2 * 288 * TOK * 2 * PART,
        scratch=[pltpu.VMEM((288, 2 * PART), BF)],
        places={0: SMEM},
    )
    (down,) = call(
        down_kernel,
        [((TOK, D), F32)],
        (act, feed_w),
        2 * TOK * HALF * D,
        scratch=[pltpu.VMEM((HALF, D), BF), pltpu.SemaphoreType.DMA],
        places={0: FAR, 1: HERE},
    )
    down = down.reshape(2, ROWS, D)
    down_got = send(pick(down, 0, 1 - c).astype(BF), "c")
    own_kf = pick(kf.reshape(2, ROWS, 1), 0, c)
    mixed = pick(middle.reshape(2, ROWS, D), 0, c) + own_kf * (pick(down, 0, c) + down_got)

    attention_sum = reduce_direct(by_place.astype(F32).reshape(4, 72, 2 * PART), "z", z, 0)
    attention_sum = mm(by_y, attention_sum.astype(BF)).reshape(4, 24, 2 * PART)
    a24 = reduce_direct(attention_sum, "y", y, 0)
    a24, feed_sum = lax.optimization_barrier((a24, feed_sum))
    dn1 = pick(dn1_part, 0, c) + send(pick(dn1_part, 0, 1 - c).astype(BF), "c")
    hat_own, scale_own = normal(tokens.astype(F32))
    back_tokens = pick(dmiddle.reshape(2, ROWS, D), 0, c) + normal_pull(
        hat_own, scale_own, dn1 * g1
    )

    def swap(own, other):
        got = send(other.astype(BF), "c").astype(F32)
        return jnp.where(first_core, own, got), jnp.where(first_core, got, own)

    def hidden_join(zero, one):
        return jnp.stack([zero.reshape(9, 32, 48), one.reshape(9, 32, 48)], axis=2).reshape(9, FF)

    feed24 = reduce_direct(feed_sum.astype(F32).reshape(4, 24, WIDE), "x", x, 0)
    back_down = feed24[:, FF:]
    core0, core1 = feed24[:9, :FF], feed24[9:18, :FF]
    f0, f1 = swap(jnp.where(first_core, core0, core1), jnp.where(first_core, core1, core0))
    back_gate = hidden_join(f0[:, :HALF], f1[:, :HALF])
    back_up = hidden_join(f0[:, HALF:], f1[:, HALF:])
    core0, core1 = a24[:9], a24[9:18]
    a0, a1 = swap(jnp.where(first_core, core0, core1), jnp.where(first_core, core1, core0))
    join = lambda low, high: jnp.concatenate([a0[:, low:high], a1[:, low:high]], axis=1)
    back_query = join(192, 768)
    back_key = join(0, 192)
    back_value = join(832, 1024)
    back_out = join(1024, 1600)
    dots = lambda weight, grad: jnp.sum(weight.astype(F32) * grad, axis=1)
    back_one = (
        dots(wq, back_query) + dots(wk, back_key) + dots(wv, back_value)
    ) / gain_one.astype(F32)
    back_two = (dots(wg, back_gate) + dots(wu, back_up)) / gain_two.astype(F32)
    return (
        mixed.astype(BF),
        back_tokens,
        back_one,
        back_query,
        back_key,
        back_value,
        back_out,
        back_two,
        back_gate,
        back_up,
        back_down,
    )


def solution(mesh):
    fine = Mesh(mesh.devices.reshape([SIZES[name] for name in AXES]), AXES)
    row, rows = P(AXES), P(AXES, None)
    in_specs = (rows, row, row, row, rows, rows, rows, rows, row, rows, rows, rows, rows)
    out_specs = (rows, rows, row, rows, rows, rows, rows, row, rows, rows, rows)
    return jax.shard_map(
        on_device, mesh=fine, in_specs=in_specs, out_specs=out_specs, check_vma=False
    )
```

```python
import math

import jax
import jax.numpy as jnp
from jax import lax
from jax.experimental import pallas as pl
from jax.experimental.pallas import tpu as pltpu
from jax.sharding import Mesh, PartitionSpec as P

H = 18
KV = 6
HD = 64
D = 1152
FF = 3072
ROWS = 128
EPSILON = 1e-05
NEGATIVE = -1e30
AXES = ("y", "z", "xh", "c", "xl")
SIZES = {"y": 4, "z": 4, "xh": 2, "c": 2, "xl": 2}
BF = jnp.bfloat16
F32 = jnp.float32
HQ = H // 2
HK = KV // 2
GROUP = H // KV
PART = 832
VPAD = 256
OWN = 576
LANES = 640
TOK = 2 * ROWS
HALF = FF // 2
SLOTS = 1536
SECOND, EXTRA, DOWN = FF, 2 * FF, 2 * FF + 768
WIDE = DOWN + 3 * D
TILE = 512
CHIPS = ("y", "z", "xh", "xl")


def places():
    for y in range(4):
        for z in range(4):
            for xh in range(2):
                for c in range(2):
                    for xl in range(2):
                        yield {"y": y, "z": z, "xh": xh, "c": c, "xl": xl}


def index_of(place):
    total = 0
    for name in AXES:
        total = total * SIZES[name] + place[name]
    return total


def shift_pairs(axis, step):
    pairs = []
    for place in places():
        other = dict(place)
        if axis == "x":
            spot = (place["xh"] * 2 + place["xl"] + step) % 4
            other["xh"], other["xl"] = spot // 2, spot % 2
        elif axis == "c":
            other["c"] = 1 - place["c"]
        else:
            other[axis] = (place[axis] + step) % 4
        pairs.append((index_of(place), index_of(other)))
    return pairs


PAIRS = {(axis, step): shift_pairs(axis, step) for axis in "xyz" for step in (1, -1, 2)}
PAIRS["c"] = shift_pairs("c", 1)
PAIRS["late"] = [
    (index_of(place), index_of({**place, "xl": 1})) for place in places() if place["xl"] == 0
]
PAIRS["early"] = [
    (index_of(place), index_of({**place, "xl": 0})) for place in places() if place["xl"] == 1
]


def send(value, key):
    return lax.ppermute(value, AXES, PAIRS[key])


def mm(left, right):
    return jnp.dot(left, right, preferred_element_type=F32)


def mm_t(left, right):
    return lax.dot_general(left, right, (((1,), (1,)), ((), ())), preferred_element_type=F32)


def inner(left, right):
    return lax.dot_general(left, right, (((0,), (0,)), ((), ())), preferred_element_type=F32)


def put(full, block, axis, index):
    starts = [0] * full.ndim
    starts[axis] = index
    return lax.dynamic_update_slice(full, jnp.expand_dims(block, axis), starts)


def pick(array, axis, index):
    return lax.dynamic_index_in_dim(array, index, axis, keepdims=False)


def wrap(spot, step):
    return lax.rem(spot + step + 4, 4)


def gather_direct(block, axis, spot, dim):
    shape = list(block.shape)
    shape.insert(dim, 4)
    full = jnp.zeros(shape, block.dtype)
    full = put(full, block, dim, spot)
    full = put(full, send(block, (axis, 1)), dim, wrap(spot, -1))
    full = put(full, send(block, (axis, -1)), dim, wrap(spot, 1))
    return put(full, send(block, (axis, 2)), dim, wrap(spot, 2))


def gather_ring(block, axis, spot, dim):
    half = block.shape[-2] // 2
    shape = list(block.shape)
    shape.insert(dim, 4)
    left = send(block, (axis, 1))
    right = send(block, (axis, -1))
    low = send(left[..., :half, :], (axis, 1))
    high = send(right[..., half:, :], (axis, -1))
    full = jnp.zeros(shape, block.dtype)
    full = put(full, block, dim, spot)
    full = put(full, left, dim, wrap(spot, -1))
    full = put(full, right, dim, wrap(spot, 1))
    far = jnp.concatenate([low, high], axis=-2)
    return put(full, far, dim, wrap(spot, 2))


def reduce_direct(parts, axis, spot, dim):
    low = parts.astype(BF)
    first = send(pick(low, dim, wrap(spot, 1)), (axis, 1))
    second = send(pick(low, dim, wrap(spot, -1)), (axis, -1))
    third = send(pick(low, dim, wrap(spot, 2)), (axis, 2))
    return pick(parts, dim, spot) + first + second + third


def normal(values):
    scale = lax.rsqrt(jnp.mean(values * values, axis=-1, keepdims=True) + EPSILON)
    return values * scale, scale


def normal_pull(hat, scale, grad):
    return scale * (grad - hat * jnp.mean(grad * hat, axis=-1, keepdims=True))


def halves_swapped(values):
    lane = lax.broadcasted_iota(jnp.int32, values.shape, 1)
    return jnp.where(
        lane % HD < HD // 2, pltpu.roll(values, 96, 1), pltpu.roll(values, 32, 1)
    )


SMEM = pl.BlockSpec(memory_space=pltpu.SMEM)
HERE = pl.BlockSpec(memory_space=pltpu.HBM)
FAR = "far"


def call(body, outs, args, flops, scratch=(), places=None, megabytes=24):
    total = sum(math.prod(a.shape) * a.dtype.itemsize for a in args)
    total += sum(math.prod(shape) * jnp.dtype(kind).itemsize for shape, kind in outs)
    places = places or {}

    def spec(index, shape):
        if places.get(index, FAR) is not FAR:
            return places[index]
        return pl.BlockSpec(
            shape, lambda i: (0,) * len(shape), pipeline_mode=pl.Buffered(1)
        )

    in_specs = [spec(i, a.shape) for i, a in enumerate(args)]
    out_specs = [spec(len(args) + i, shape) for i, (shape, _) in enumerate(outs)]
    return pl.pallas_call(
        body,
        grid=(1,),
        out_shape=[
            pltpu.HBM(shape, kind)
            if places.get(len(args) + i) in (HERE, FAR)
            else jax.ShapeDtypeStruct(shape, kind)
            for i, (shape, kind) in enumerate(outs)
        ],
        in_specs=in_specs,
        out_specs=out_specs,
        scratch_shapes=list(scratch),
        compiler_params=pltpu.CompilerParams(vmem_limit_bytes=megabytes << 20),
        cost_estimate=pl.CostEstimate(flops=flops, bytes_accessed=total, transcendentals=0),
    )(
        *[
            pltpu.with_memory_space_constraint(a, pltpu.HBM)
            if places.get(i) in (HERE, FAR)
            else a
            for i, a in enumerate(args)
        ]
    )


SCALE = 1.0 / math.sqrt(HD)


def sequence(s):
    return pl.ds(pl.multiple_of(s * ROWS, ROWS), ROWS)


def each_sequence(body):
    def step(s, carry):
        body(s)
        return carry

    lax.fori_loop(0, 2, step, 0)


def project_kernel(
    x_ref, wqk_ref, wvo_hbm, cos_ref, sin_ref, doc_ref,
    gain_ref, n1_ref, qk_ref, kv_ref, raw_ref, v_ref, wv_ref, sem,
):
    load = pltpu.make_async_copy(wvo_hbm.at[:, pl.ds(0, VPAD)], wv_ref, sem)
    load.start()
    unit = (
        lax.broadcasted_iota(jnp.int32, (8, 64), 1)
        == lax.broadcasted_iota(jnp.int32, (8, 64), 0)
    ).astype(BF)
    gain_ref[...] = mm_t(unit, wqk_ref[:, 768:])
    hat, _ = normal(x_ref[...].astype(F32))
    n1 = (hat * gain_ref[0:1, :]).astype(BF)
    n1_ref[...] = n1
    raw_ref[...] = mm(n1, wqk_ref[:, :768])
    load.wait()
    v_ref[...] = mm(n1, wv_ref[...]).astype(BF)
    cosine, sine = cos_ref[...], sin_ref[...]
    lane = lax.broadcasted_iota(jnp.int32, (ROWS, 128), 1)

    def turn(s):
        rows = sequence(s)
        for j in range(6):
            at = slice(j * 128, j * 128 + 128)
            tile = raw_ref[rows, at]
            turned = (tile * cosine + halves_swapped(tile) * sine).astype(BF)
            qk_ref[rows, at] = turned
            if j == 0:
                kv_ref[rows, 0:128] = turned
            if j == 1:
                kv_ref[rows, 128:256] = jnp.where(lane < 64, turned, v_ref[rows, 0:128])
        kv_ref[rows, 256:384] = v_ref[rows, 128:256]

    each_sequence(turn)
    kv_ref[TOK:, :] = doc_ref[...]


def head_data(h, qk, kv, early):
    base = 192 + h * 192
    q = jnp.concatenate(
        [qk[:, base + 64 * g : base + 64 * g + 64] for g in range(GROUP)], axis=0
    )
    keys, vals = slice(64 * h, 64 * h + 64), slice(192 + 64 * h, 256 + 64 * h)
    return q, early[:, keys], kv[:, keys], early[:, vals], kv[:, vals]


def early_docs(late_ref, early_ref, row_ref):
    rows = early_ref[TOK:, :ROWS].astype(F32)
    row_ref[...] = jnp.where(late_ref[0] == 1, rows, -1.0)


def masks(s, dcol_ref, drow_ref, derow_ref):
    col = dcol_ref[sequence(s), :]
    at = lax.broadcasted_iota(jnp.int32, (ROWS, ROWS), 0)
    to = lax.broadcasted_iota(jnp.int32, (ROWS, ROWS), 1)
    mask_o = (to <= at) & (col == drow_ref[s])
    mask_e = col == derow_ref[pl.ds(s, 1), :]
    wide = lambda m: jnp.concatenate([jnp.where(m, 0.0, NEGATIVE)] * GROUP, axis=0)
    return wide(mask_e), wide(mask_o)


def softmax(q, ke, ko, mask_e, mask_o):
    se = jnp.where(mask_e == 0.0, mm_t(q, ke) * SCALE, NEGATIVE)
    so = jnp.where(mask_o == 0.0, mm_t(q, ko) * SCALE, NEGATIVE)
    top = jnp.maximum(
        jnp.max(se, axis=-1, keepdims=True), jnp.max(so, axis=-1, keepdims=True)
    )
    ee, eo = jnp.exp(se - top), jnp.exp(so - top)
    total = jnp.sum(ee, axis=-1, keepdims=True) + jnp.sum(eo, axis=-1, keepdims=True)
    return ee / total, eo / total


def split_heads(stacked):
    return [stacked[g * ROWS : g * ROWS + ROWS] for g in range(GROUP)]


def attend_kernel(qk_ref, kv_ref, early_ref, late_ref, dcol_ref, drow_ref, o_ref, derow_ref):
    early_docs(late_ref, early_ref, derow_ref)

    def one(s):
        rows = sequence(s)
        qk, kv, early = qk_ref[rows, :], kv_ref[rows, :], early_ref[rows, :]
        mask_e, mask_o = masks(s, dcol_ref, drow_ref, derow_ref)
        pieces = []
        for h in range(HK):
            q, ke, ko, ve, vo = head_data(h, qk, kv, early)
            pe, po = softmax(q, ke, ko, mask_e, mask_o)
            pieces += split_heads(mm(pe.astype(BF), ve) + mm(po.astype(BF), vo))
        pieces.append(jnp.zeros((ROWS, LANES - OWN), F32))
        o_ref[rows, :] = jnp.concatenate(pieces, axis=1).astype(BF)

    each_sequence(one)


def attend_back_kernel(
    qk_ref, kv_ref, early_ref, late_ref, dcol_ref, drow_ref, do_ref, got_ref,
    dqk_ref, dv_ref, de_ref, derow_ref,
):
    early_docs(late_ref, early_ref, derow_ref)

    def one(s):
        rows = sequence(s)
        qk, kv, early = qk_ref[rows, :], kv_ref[rows, :], early_ref[rows, :]
        do_all = (do_ref[rows, :] + got_ref[rows, :OWN].astype(F32)).astype(BF)
        mask_e, mask_o = masks(s, dcol_ref, drow_ref, derow_ref)
        dqs, dke, dko, dve, dvo = [], [], [], [], []
        for h in range(HK):
            q, ke, ko, ve, vo = head_data(h, qk, kv, early)
            pe, po = softmax(q, ke, ko, mask_e, mask_o)
            do = jnp.concatenate(
                [do_all[:, (GROUP * h + g) * 64 : (GROUP * h + g) * 64 + 64] for g in range(GROUP)],
                axis=0,
            )
            dpe, dpo = mm_t(do, ve), mm_t(do, vo)
            centre = jnp.sum(pe * dpe, axis=-1, keepdims=True) + jnp.sum(
                po * dpo, axis=-1, keepdims=True
            )
            dse = (pe * (dpe - centre)).astype(BF)
            dso = (po * (dpo - centre)).astype(BF)
            dqs += split_heads((mm(dse, ke) + mm(dso, ko)) * SCALE)
            dke.append(inner(dse, q) * SCALE)
            dko.append(inner(dso, q) * SCALE)
            dve.append(inner(pe.astype(BF), do))
            dvo.append(inner(po.astype(BF), do))
        dqk_ref[rows, :] = jnp.concatenate(dko + dqs, axis=1)
        dv_ref[rows, :] = jnp.concatenate([jnp.zeros((ROWS, 64), F32)] + dvo, axis=1)
        de_ref[rows, :] = jnp.concatenate(dke + dve, axis=1).astype(BF)

    each_sequence(one)


def project_back_kernel(
    dqk_ref, dv_ref, got_ref, cos_ref, sin_ref, low_ref
):
    cosine, sine = cos_ref[...], sin_ref[...]
    lane = lax.broadcasted_iota(jnp.int32, (ROWS, 128), 1)

    def turn(s):
        rows = sequence(s)
        got = got_ref[rows, :].astype(F32)
        for j in range(6):
            at = slice(j * 128, j * 128 + 128)
            tile = dqk_ref[rows, at]
            if j == 0:
                tile = tile + got[:, 0:128]
            if j == 1:
                tile = tile + jnp.where(lane < 64, got[:, 128:256], 0.0)
            low_ref[rows, at] = (tile * cosine - halves_swapped(tile) * sine).astype(BF)
        dv0 = dv_ref[rows, 0:128] + jnp.where(lane < 64, 0.0, got[:, 128:256])
        low_ref[rows, 768:896] = dv0.astype(BF)
        low_ref[rows, 896:1024] = (dv_ref[rows, 128:256] + got[:, 256:384]).astype(BF)

    each_sequence(turn)


def normed_back_kernel(low_ref, wqk_ref, wvo_ref, dn1_ref):
    dn1_ref[...] = mm_t(low_ref[:, :768], wqk_ref[:, :768]) + mm_t(
        low_ref[:, 768:], wvo_ref[:, :VPAD]
    )


def out_far_kernel(x_ref, o_ref, ba_ref, far_ref):
    far_ref[...] = mm(o_ref[wrap(x_ref[0], 2)], ba_ref[...]).astype(BF)


def out_near_kernel(x_ref, o_ref, ba_ref, own_ref, ahead_ref, behind_ref):
    for step, out in ((0, own_ref), (1, ahead_ref), (-1, behind_ref)):
        out[...] = mm(o_ref[wrap(x_ref[0], step)], ba_ref[...]).astype(BF)


def far_kernel(x_ref, n1_ref, dqkv_ref, low_ref, high_ref):
    chunk = mm(n1_ref[wrap(x_ref[0], 2)], dqkv_ref[...]).astype(BF)
    low_ref[...] = chunk[:144]
    high_ref[...] = chunk[144:]


def near_kernel(x_ref, n1_ref, dqkv_ref, low_ref, high_ref, ahead_ref, behind_ref):
    for step, out, add, first in ((1, ahead_ref, low_ref, 0), (-1, behind_ref, high_ref, 144)):
        chunk = mm(n1_ref[wrap(x_ref[0], step)], dqkv_ref[...])
        rows = slice(first, first + 144)
        out[...] = chunk.astype(BF)
        out[rows, :] = (chunk[rows] + add[...].astype(F32)).astype(BF)


def own_kernel(
    x_ref, n1_ref, dqkv_ref, first_ref, second_ref,
    o0_ref, o1_ref, o2_ref, o3_ref, order_ref, out_ref, sum_ref,
):
    total = mm(n1_ref[x_ref[0]], dqkv_ref[...])
    total = total + first_ref[...].astype(F32) + second_ref[...].astype(F32)
    sum_ref[:, :1024] = total.astype(BF)
    total = o0_ref[...].astype(F32) + o1_ref[...].astype(F32)
    total = total + o2_ref[...].astype(F32) + o3_ref[...].astype(F32)
    sum_ref[:, 1024:] = total.astype(BF)
    out_ref[...] = mm(order_ref[...], sum_ref[...]).astype(BF)


def out_rows(w_ref, c, first=VPAD):
    return w_ref[pl.ds(pl.multiple_of(c * OWN, 64), OWN), first:]


def out_kernel(c_ref, o_ref, got_ref, w_hbm, kf_ref, part_ref, w_ref, sem):
    load = pltpu.make_async_copy(w_hbm.at[:, pl.ds(VPAD, OWN)], w_ref, sem)
    load.start()
    load.wait()
    c = c_ref[0]
    total = mm(o_ref[:, :OWN], out_rows(w_ref, c, 0)) + mm(
        got_ref[:, :OWN], out_rows(w_ref, 1 - c, 0)
    )
    part_ref[:, :OWN] = kf_ref[...] * total
    part_ref[:, OWN:] = jnp.zeros((TOK, LANES - OWN), F32)


def shuffle_map(shape, dim):
    to = lax.broadcasted_iota(jnp.int32, shape, dim)
    core, group = to // 384, (to % 384) // 128
    plane, along, unit = (to % 128) // 16, (to % 16) // 8, to % 8
    return plane * 96 + core * 48 + along * 24 + group * 8 + unit


def split_kernel(
    c_ref, one_ref, two_ref, wg_ref, wu_ref, wq_ref, wk_ref, wv_ref, wo_ref, own_ref, other_ref
):
    at = lax.broadcasted_iota(jnp.int32, (768, 768), 0)
    order = (at == shuffle_map((1, 768), 1)).astype(F32).astype(BF)
    first = c_ref[0] == 0

    def write(at, zero, one):
        cols = slice(at, at + zero.shape[1])
        own_ref[:, cols] = jnp.where(first, zero, one).astype(BF)
        other_ref[:, cols] = jnp.where(first, one, zero).astype(BF)

    for side, ref in enumerate((wg_ref, wu_ref)):
        for block in range(4):
            moved = mm(ref[:, block * 768 : block * 768 + 768], order)
            for group in range(3):
                zero = moved[:, group * 128 : group * 128 + 128]
                one = moved[:, 384 + group * 128 : 512 + group * 128]
                write(side * HALF + group * TILE + block * 128, zero, one)
    row = lax.broadcasted_iota(jnp.int32, (9, 64), 0)
    lane = lax.broadcasted_iota(jnp.int32, (9, 64), 1)
    gains = jnp.zeros((9, 64), F32)
    for i in range(9):
        gains = jnp.where((row == i) & (lane == 0), one_ref[i], gains)
        gains = jnp.where((row == i) & (lane == 1), two_ref[i], gains)
    blank = jnp.zeros((9, 64), F32)
    wq, wk, wv, wo = [ref[...].astype(F32) for ref in (wq_ref, wk_ref, wv_ref, wo_ref)]
    halves = [
        jnp.concatenate(
            [
                wk[:, h * 192 : h * 192 + 192],
                wq[:, h * OWN : h * OWN + OWN],
                gains,
                blank,
                wv[:, h * 192 : h * 192 + 192],
                wo[:, h * OWN : h * OWN + OWN],
            ],
            axis=1,
        )
        for h in range(2)
    ]
    write(FF, *halves)


def pack_kernel(c_ref, own_ref, got_ref, wd_ref, out_ref, block_ref):
    first = c_ref[0] == 0
    own, got = own_ref[:, :FF].astype(F32), got_ref[:, :FF].astype(F32)
    zero, one = jnp.where(first, own, got), jnp.where(first, got, own)
    out_ref[:, :SECOND] = zero[:8].astype(BF)
    out_ref[:, SECOND:EXTRA] = jnp.concatenate([zero[8:9], one[:7]], axis=0).astype(BF)
    for group in range(3):
        rows = []
        for row in (7, 8):
            for side in range(2):
                for half in range(2):
                    at = side * HALF + group * TILE + half * 256
                    rows.append(one[row : row + 1, at : at + 256])
        at = EXTRA + group * 256
        out_ref[:, at : at + 256] = jnp.concatenate(rows, axis=0).astype(BF)
        at = DOWN + group * D
        out_ref[:, at : at + D] = wd_ref[group * 8 : group * 8 + 8, :]
    own, got = own_ref[:, FF:].astype(F32), got_ref[:, FF:].astype(F32)
    blank = jnp.zeros((6, 2 * PART), F32)
    block_ref[...] = jnp.concatenate([own, got, blank], axis=0).astype(BF)


def unpack_kernel(c_ref, own_ref, a_ref, b_ref, d_ref, mine_ref, other_ref, down_ref):
    def total(at, size):
        cols = slice(at, at + size)
        low = own_ref[:, cols].astype(F32) + a_ref[:, cols].astype(F32)
        return low + b_ref[:, cols].astype(F32) + d_ref[:, cols].astype(F32)

    first = c_ref[0] == 0
    for group in range(3):
        down_ref[group * 8 : group * 8 + 8, :] = total(DOWN + group * D, D)
        extra = total(EXTRA + group * 256, 256)
        for side in range(2):
            at = side * HALF + group * TILE
            head, tail = total(at, TILE), total(SECOND + at, TILE)
            last = [
                jnp.concatenate(
                    [extra[4 * row + 2 * side + half :][:1] for half in range(2)], axis=1
                )
                for row in range(2)
            ]
            zero = jnp.concatenate([head, tail[:1]], axis=0)
            one = jnp.concatenate([tail[1:]] + last, axis=0)
            cols = slice(at, at + TILE)
            mine_ref[:, cols] = jnp.where(first, zero, one).astype(BF)
            other_ref[:, cols] = jnp.where(first, one, zero).astype(BF)


def join_kernel(
    c_ref, mine_ref, got_ref, wg_ref, wu_ref, gain_ref, gate_ref, up_ref, dot_ref
):
    at = lax.broadcasted_iota(jnp.int32, (768, 768), 1)
    order = (at == shuffle_map((768, 1), 0)).astype(F32).astype(BF)
    first = c_ref[0] == 0
    dots = jnp.zeros((9, 1), F32)
    for side, (w_ref, ref) in enumerate(((wg_ref, gate_ref), (wu_ref, up_ref))):
        for block in range(4):
            pieces = []
            for core in range(2):
                for group in range(3):
                    at = side * HALF + group * TILE + block * 128
                    mine, got = mine_ref[:, at : at + 128], got_ref[:, at : at + 128]
                    pieces.append(
                        jnp.where(first, mine, got) if core == 0 else jnp.where(first, got, mine)
                    )
            natural = mm(jnp.concatenate(pieces, axis=1), order)
            cols = slice(block * 768, block * 768 + 768)
            ref[:, cols] = natural
            weight = w_ref[:, cols].astype(F32)
            dots = dots + jnp.sum(weight * natural, axis=1, keepdims=True)
    dot_ref[...] = dots / gain_ref[...]


def feed_kernel(
    c_ref, g_ref, x_hbm, part_hbm, got_hbm, fs_hbm, bm_hbm, w_ref,
    mid_hbm, grad_ref, act_hbm, dgu_hbm,
    x_ref, part_ref, got_ref, fs_ref, bm_ref, mid_ref, act_ref, dgu_ref,
    n2_ref, n2t_ref, last_ref, last_t_ref, wm, we, wd, gm, ge, gd, in_sem, out_sem, side_sem,
):
    steps = HALF // TILE

    def places(t):
        at = pl.multiple_of(t * TILE, TILE)
        return (
            pl.ds(at, TILE),
            pl.ds(HALF + at, TILE),
            pl.ds(pl.multiple_of(t * 256, 256), 256),
            pl.ds(pl.multiple_of(t * D, 128), D),
        )

    def pairs(t, far, main, more, down):
        at = pl.multiple_of(t * TILE, TILE)
        gate_at, up_at, extra_at, down_at = places(t)
        everything, head, tail = slice(None), pl.ds(0, TILE), pl.ds(TILE, TILE)
        return (
            (far.at[:, pl.ds(at, TILE)], main.at[head, gate_at]),
            (far.at[:, pl.ds(SECOND + at, TILE)], main.at[tail, gate_at]),
            (far.at[:, pl.ds(HALF + at, TILE)], main.at[head, up_at]),
            (far.at[:, pl.ds(SECOND + HALF + at, TILE)], main.at[tail, up_at]),
            (far.at[:, pl.ds(EXTRA + pl.multiple_of(t * 256, 256), 256)], more.at[:, extra_at]),
            (far.at[:, pl.ds(DOWN + pl.multiple_of(t * D, 128), D)], down.at[:, down_at]),
        )

    def loads(t):
        return [
            pltpu.make_async_copy(far, near, in_sem.at[t, i])
            for i, (far, near) in enumerate(pairs(t, w_ref, wm, we, wd))
        ]

    def stores(t):
        return [
            pltpu.make_async_copy(near, far, out_sem.at[t, i])
            for i, (far, near) in enumerate(pairs(t, grad_ref, gm, ge, gd))
        ]

    sides = [
        pltpu.make_async_copy(src, dst, side_sem.at[i])
        for i, (src, dst) in enumerate(
            (
                (x_hbm, x_ref), (part_hbm, part_ref), (got_hbm, got_ref),
                (fs_hbm, fs_ref), (bm_hbm, bm_ref), (mid_ref, mid_hbm),
                (act_ref, act_hbm), (dgu_ref, dgu_hbm),
            )
        )
    ]
    for copy in sides[:5] + loads(0):
        copy.start()
    for copy in sides[:3]:
        copy.wait()
    for t in range(1, steps):
        for copy in loads(t):
            copy.start()

    first = c_ref[0] == 0
    part, got = part_ref[:, :OWN], got_ref[:, :OWN]
    low = jnp.where(first, part, got)
    high = jnp.where(first, got, part)
    middle = x_ref[...].astype(F32) + jnp.concatenate([low, high], axis=1)
    mid_ref[...] = middle
    sides[5].start()
    hat, _ = normal(middle)
    normed = (hat * g_ref[...]).astype(BF)
    for copy in sides[3:5]:
        copy.wait()
    n2_ref[...] = mm_t(normed, fs_ref[...]).astype(BF)
    n2t_ref[...] = n2_ref[...].T
    lane = lax.broadcasted_iota(jnp.int32, (TOK, TILE), 1) % 4
    row = lax.broadcasted_iota(jnp.int32, (TILE, TOK), 0) % 4
    last = n2_ref[:, 2 * TILE :].astype(F32)
    last_t = n2t_ref[2 * TILE :, :].astype(F32)
    for m in range(4):
        at = slice(m * TOK, m * TOK + TOK)
        last_ref[at, :] = jnp.where(lane == m, last, 0.0).astype(BF)
        last_t_ref[:, at] = jnp.where(row == m, last_t, 0.0).astype(BF)

    def step(t, carry):
        for copy in loads(t):
            copy.wait()
        gate_at, up_at, extra_at, down_at = places(t)
        rows, bm = n2_ref[:, : 2 * TILE], bm_ref[...]
        more = mm(last_ref[...], we[:, extra_at])
        parts = [more[m * TOK : m * TOK + TOK] for m in range(4)]
        gate = mm(rows, wm[:, gate_at]) + jnp.concatenate(parts[:2], axis=1)
        up = mm(rows, wm[:, up_at]) + jnp.concatenate(parts[2:], axis=1)
        dact = mm_t(bm, wd[:, down_at])
        sig = jax.nn.sigmoid(gate)
        silu = gate * sig
        act = (silu * up).astype(BF)
        dgate = (dact * up * (sig * (1.0 + gate * (1.0 - sig)))).astype(BF)
        dup = (dact * silu).astype(BF)
        act_ref[:, gate_at] = act
        dgu_ref[:, gate_at] = dgate
        dgu_ref[:, up_at] = dup
        rows_t = n2t_ref[: 2 * TILE, :]
        gm[:, gate_at] = mm(rows_t, dgate).astype(BF)
        gm[:, up_at] = mm(rows_t, dup).astype(BF)
        four = jnp.concatenate(
            [dgate[:, :256], dgate[:, 256:], dup[:, :256], dup[:, 256:]], axis=0
        )
        ge[:, extra_at] = mm(last_t_ref[...], four).astype(BF)
        gd[:, down_at] = inner(act, bm).astype(BF)
        for copy in stores(t):
            copy.start()
        return carry

    lax.fori_loop(0, steps, step, 0)
    for copy in sides[6:]:
        copy.start()
    for copy in sides[5:]:
        copy.wait()
    for t in range(steps):
        for copy in stores(t):
            copy.wait()


def feed_back_kernel(
    dgu_hbm, w_ref, fs_hbm, dn2_ref, low_ref,
    dgu_ref, fs_ref, wb, dgt_ref, four_ref, slots_ref, sem, side_sem,
):
    rows_each = 128
    steps = TILE // rows_each

    def load(t):
        rows = pl.ds(pl.multiple_of(t * rows_each, rows_each), rows_each)
        return pltpu.make_async_copy(w_ref.at[rows, pl.ds(0, DOWN)], wb.at[rows, :], sem.at[t])

    sides = [
        pltpu.make_async_copy(dgu_hbm, dgu_ref, side_sem.at[0]),
        pltpu.make_async_copy(fs_hbm, fs_ref, side_sem.at[1]),
    ]
    sides[0].start()
    for t in range(steps):
        load(t).start()
    sides[1].start()
    sides[0].wait()
    dgt_ref[...] = dgu_ref[...].T
    for m in range(4):
        for group in range(3):
            at = (m // 2) * HALF + group * TILE + (m % 2) * 256
            four_ref[group * 256 : group * 256 + 256, m * TOK : m * TOK + TOK] = dgt_ref[
                at : at + 256, :
            ]

    def step(t, carry):
        load(t).wait()
        at = pl.multiple_of(t * rows_each, rows_each)
        rows = pl.ds(at, rows_each)
        dgt = dgt_ref[...]
        slots_ref[rows, :] = mm(wb[rows, :SECOND], dgt).astype(BF)
        slots_ref[pl.ds(TILE + at, rows_each), :] = mm(wb[rows, SECOND:EXTRA], dgt).astype(BF)
        more = mm(wb[rows, EXTRA:], four_ref[...])
        row = lax.broadcasted_iota(jnp.int32, (rows_each, TOK), 0) % 4
        last = jnp.zeros((rows_each, TOK), F32)
        for m in range(4):
            last = jnp.where(row == m, more[:, m * TOK : m * TOK + TOK], last)
        slots_ref[pl.ds(2 * TILE + at, rows_each), :] = last.astype(BF)
        return carry

    lax.fori_loop(0, steps, step, 0)
    sides[1].wait()
    dn2 = inner(slots_ref[...], fs_ref[...])
    dn2_ref[...] = dn2
    low_ref[...] = dn2.astype(BF)


def down_kernel(act_ref, w_ref, down_ref, wb, sem):
    load = pltpu.make_async_copy(w_ref.at[:, pl.ds(DOWN, 3 * D)], wb, sem)
    load.start()
    load.wait()
    total = mm(act_ref[:, :TILE], wb[:, :D])
    for group in (1, 2):
        total = total + mm(
            act_ref[:, group * TILE : group * TILE + TILE], wb[:, group * D : group * D + D]
        )
    down_ref[...] = total


def middle_back_kernel(
    c_ref, part_ref, got_ref, mid_ref, cot_ref, g_ref, kf_ref, w_ref,
    dmid_ref, ba_ref, do_ref, other_ref,
):
    c = c_ref[0]
    dn2 = part_ref[...] + got_ref[...].astype(F32)
    hat, scale = normal(mid_ref[...])
    dmiddle = cot_ref[...] + normal_pull(hat, scale, dn2 * g_ref[...])
    dmid_ref[...] = dmiddle
    ba = kf_ref[...] * dmiddle
    half = jnp.where(c == 0, ba[:, :576], ba[:, 576:]).astype(BF)
    ba_ref[:, :OWN] = half
    ba_ref[:, OWN:] = jnp.zeros((TOK, LANES - OWN), BF)
    do_ref[...] = mm_t(half, out_rows(w_ref, c))
    other_ref[:, :OWN] = mm_t(half, out_rows(w_ref, 1 - c)).astype(BF)
    other_ref[:, OWN:] = jnp.zeros((TOK, LANES - OWN), BF)


def on_device(
    tokens, doc_ids, keep, gain_one, wq, wk, wv, wo, gain_two, wg, wu, wd, cotangent
):
    y, z, c = lax.axis_index("y"), lax.axis_index("z"), lax.axis_index("c")
    xl = lax.axis_index("xl")
    x = lax.axis_index("xh") * 2 + xl
    first_core = c == 0

    def both(own, other):
        return jnp.where(first_core, jnp.stack([own, other]), jnp.stack([other, own]))

    r = lax.broadcasted_iota(jnp.int32, (72, 96), 0)
    s = lax.broadcasted_iota(jnp.int32, (72, 96), 1)
    xh_r, rest = r // 36, r % 36
    c_r, rest = rest // 18, rest % 18
    xl_r, i_r = rest // 9, rest % 9
    k_r = lax.rem(xh_r * 2 + xl_r - x + 4, 4)
    select = (s == k_r * 24 + jnp.where(c_r == c, 0, 9) + i_r).astype(BF)

    def rows72(block):
        stacked = jnp.concatenate(
            [block, send(block, ("x", -1)), send(block, ("x", 2)), send(block, ("x", 1))], axis=0
        )
        return mm(select, stacked).astype(BF)

    def gather_zy(block):
        return gather_ring(
            gather_direct(block, "z", z, 0).reshape(288, -1), "y", y, 0
        ).reshape(D, -1)

    def gather_yz(block):
        return gather_ring(gather_direct(block, "y", y, 0), "z", z, 1).reshape(D, -1)

    core = c.astype(jnp.int32).reshape(1)
    both_cols = FF + 2 * PART
    own, other = call(
        split_kernel,
        [((9, both_cols), BF), ((9, both_cols), BF)],
        (core, gain_one.astype(F32), gain_two.astype(F32), wg, wu, wq, wk, wv, wo),
        8 * 9 * 768 * 768 * 2,
        places={0: SMEM, 1: SMEM, 2: SMEM} | {i: FAR for i in range(3, 9)},
    )
    feed_block, a_block = call(
        pack_kernel,
        [((8, WIDE), BF), ((24, 2 * PART), BF)],
        (core, own, send(other, "c"), wd),
        1,
        places={0: SMEM, 3: FAR},
    )
    feed_w = lax.all_gather(feed_block, CHIPS, axis=0, tiled=True)

    marks = jnp.stack([doc_ids, keep])
    a_block, x_got, marks_got, cot_got = lax.optimization_barrier(
        (a_block,) + tuple(send(v, "c") for v in (tokens, marks, cotangent))
    )
    x_all = both(tokens, x_got).reshape(TOK, D)
    marks = both(marks, marks_got)
    docs, kf = marks[:, 0].astype(F32), marks[:, 1].astype(F32).reshape(TOK, 1)
    doc_args = (docs.reshape(TOK, 1), docs.reshape(2, 1, ROWS))
    doc_rows = jnp.pad(docs, ((0, 14), (0, 384 - ROWS))).astype(BF)
    cot = both(cotangent, cot_got).reshape(TOK, D)

    a72 = rows72(a_block)
    slot = jnp.arange(SLOTS, dtype=jnp.int32)
    chip, inside = slot % TILE // 8, slot % 8
    inside = jnp.where(slot < 2 * TILE, slot // TILE * 8 + inside, 16 + inside // 4)
    of_slot = (chip // 2) * 36 + (inside // 9) * 18 + (chip % 2) * 9 + inside % 9
    spot = jnp.arange(D, dtype=jnp.int32)
    along, plane, inside = spot // 288, (spot % 288) // 18, spot % 18
    of_x = plane * 72 + (along // 2) * 36 + (inside // 9) * 18 + (along % 2) * 9 + inside % 9
    spot = jnp.arange(288, dtype=jnp.int32)
    of_z = ((spot % 72) // 18 * 4 + spot // 72) * 18 + spot % 18
    spot = jnp.arange(96, dtype=jnp.int32)
    of_y = jnp.where(spot % 24 < 18, spot // 24 * 18 + spot % 24, -1)
    orders, a72 = lax.optimization_barrier(((of_slot, of_x, of_z, of_y), a72))

    def one_hot(rows, columns):
        return (
            rows[:, None] == lax.broadcasted_iota(jnp.int32, (rows.shape[0], columns), 1)
        ).astype(BF)

    from_slots, by_x, by_z, by_y = [
        one_hot(rows, columns) for rows, columns in zip(orders, (D, D, 288, 72))
    ]

    qk_w = gather_zy(a72[:, :PART])
    vo_w = gather_yz(a72[:, PART:])

    half = HD // 2
    freqs = 10000.0 ** (-(jnp.arange(half).astype(F32) * 2.0 / HD))
    position = xl * ROWS + jnp.arange(ROWS, dtype=jnp.int32)
    angle = position.astype(F32)[:, None] * freqs[None, :]
    cosine = jnp.tile(jnp.cos(angle), (1, 4))
    sine = jnp.sin(angle)
    sine = jnp.concatenate([-sine, sine, -sine, sine], axis=1)
    bm = (kf * cot).astype(BF)
    early_work = (x_all, from_slots, bm, cosine, sine, kf, cot, by_x, doc_rows) + doc_args
    early_work, a_blocks = lax.optimization_barrier((early_work, (qk_w, vo_w)))
    x_all, from_slots, bm, cosine, sine, kf, cot, by_x, doc_rows = early_work[:9]
    late = (xl == 1).astype(jnp.int32).reshape(1)
    doc_args = (late,) + early_work[9:]
    qk_w, vo_w = a_blocks

    gains, n1, qk, kv = call(
        project_kernel,
        [((8, D), F32), ((TOK, D), BF), ((TOK, 768), BF), ((TOK + 16, 384), BF)],
        (x_all, qk_w, vo_w, cosine, sine, doc_rows),
        2 * TOK * D * 1024,
        scratch=[
            pltpu.VMEM((TOK, 768), F32),
            pltpu.VMEM((TOK, VPAD), BF),
            pltpu.VMEM((D, VPAD), BF),
            pltpu.SemaphoreType.DMA,
        ],
        places={0: FAR, 1: FAR, 2: HERE, 7: FAR, 8: FAR, 9: FAR},
    )
    g1, g2 = gains[0:1], gains[1:2]
    n1_x = mm_t(by_x, n1).astype(BF).reshape(4, 288, TOK)
    kv_early, n1_x = lax.optimization_barrier((send(kv, "late"), n1_x))
    (o,) = call(
        attend_kernel,
        [((TOK, LANES), BF)],
        (qk, kv, kv_early) + doc_args,
        4 * TOK * 576 * 256,
        scratch=[pltpu.VMEM((16, ROWS), F32)],
        places={0: FAR, 1: FAR, 3: SMEM, 6: FAR},
    )
    o_got = send(o, "c")
    (part,) = call(
        out_kernel,
        [((TOK, LANES), F32)],
        (core, o, o_got, vo_w, kf),
        2 * TOK * D * 576,
        scratch=[pltpu.VMEM((D, OWN), BF), pltpu.SemaphoreType.DMA],
        places={0: SMEM, 1: FAR, 3: HERE, 5: FAR},
    )
    part_got = send(part, "c")
    middle, feed_grad, act, dgu = call(
        feed_kernel,
        [((TOK, D), F32), ((TILE, WIDE), BF), ((TOK, HALF), BF), ((TOK, FF), BF)],
        (core, g2, x_all, part, part_got, from_slots, bm, feed_w),
        4 * TOK * SLOTS * (WIDE + D),
        scratch=[
            pltpu.VMEM((TOK, D), BF),
            pltpu.VMEM((TOK, LANES), F32),
            pltpu.VMEM((TOK, LANES), F32),
            pltpu.VMEM((SLOTS, D), BF),
            pltpu.VMEM((TOK, D), BF),
            pltpu.VMEM((TOK, D), F32),
            pltpu.VMEM((TOK, HALF), BF),
            pltpu.VMEM((TOK, FF), BF),
            pltpu.VMEM((TOK, SLOTS), BF),
            pltpu.VMEM((SLOTS, TOK), BF),
            pltpu.VMEM((4 * TOK, TILE), BF),
            pltpu.VMEM((TILE, 4 * TOK), BF),
            pltpu.VMEM((2 * TILE, FF), BF),
            pltpu.VMEM((TILE, 768), BF),
            pltpu.VMEM((TILE, 3 * D), BF),
            pltpu.VMEM((2 * TILE, FF), BF),
            pltpu.VMEM((TILE, 768), BF),
            pltpu.VMEM((TILE, 3 * D), BF),
            pltpu.SemaphoreType.DMA((3, 6)),
            pltpu.SemaphoreType.DMA((3, 6)),
            pltpu.SemaphoreType.DMA((8,)),
        ],
        places={0: SMEM} | {i: HERE for i in range(2, 12)},
        megabytes=52,
    )
    feed_sum = lax.psum_scatter(feed_grad, ("y", "z"), scatter_dimension=0, tiled=True)
    dn2_part, dn2_low = call(
        feed_back_kernel,
        [((TOK, D), F32), ((TOK, D), BF)],
        (dgu, feed_w, from_slots),
        2 * TOK * SLOTS * (FF + D),
        scratch=[
            pltpu.VMEM((TOK, FF), BF),
            pltpu.VMEM((SLOTS, D), BF),
            pltpu.VMEM((TILE, DOWN), BF),
            pltpu.VMEM((FF, TOK), BF),
            pltpu.VMEM((768, 4 * TOK), BF),
            pltpu.VMEM((SLOTS, TOK), BF),
            pltpu.SemaphoreType.DMA((4,)),
            pltpu.SemaphoreType.DMA((2,)),
        ],
        megabytes=40,
        places={0: HERE, 1: HERE, 2: HERE},
    )
    dn2_got = send(dn2_low, "c")
    dmiddle, ba_own, do_part, do_other = call(
        middle_back_kernel,
        [((TOK, D), F32), ((TOK, LANES), BF), ((TOK, OWN), F32), ((TOK, LANES), BF)],
        (core, dn2_part, dn2_got, middle, cot, g2, kf, vo_w),
        4 * TOK * D * 576,
        places={0: SMEM, 3: FAR, 4: FAR, 7: FAR, 8: FAR},
    )
    do_got = send(do_other, "c")
    o_all = jnp.where(
        first_core,
        jnp.concatenate([o[:, :OWN], o_got[:, :OWN]], axis=1),
        jnp.concatenate([o_got[:, :OWN], o[:, :OWN]], axis=1),
    )
    o_x = mm_t(by_x, o_all).astype(BF).reshape(4, 288, TOK)
    spot_x = x.astype(jnp.int32).reshape(1)
    (out_far,) = call(
        out_far_kernel,
        [((288, LANES), BF)],
        (spot_x, o_x, ba_own),
        2 * 288 * TOK * LANES,
        places={0: SMEM},
    )
    do_got, out_far = lax.optimization_barrier((do_got, out_far))
    out_far = send(out_far, ("x", 2))
    dqk_raw, dv_raw, de = call(
        attend_back_kernel,
        [((TOK, 768), F32), ((TOK, 256), F32), ((TOK, 384), BF)],
        (qk, kv, kv_early) + doc_args + (do_part, do_got),
        10 * TOK * 576 * 256,
        scratch=[pltpu.VMEM((16, ROWS), F32)],
        places={0: FAR, 1: FAR, 2: FAR, 3: SMEM},
    )
    d_got = send(de, "early")
    o_later, de_later = lax.optimization_barrier((o_x, de))
    out_own, out_ahead, out_behind = call(
        out_near_kernel,
        [((288, LANES), BF)] * 3,
        (spot_x, o_later, ba_own),
        6 * 288 * TOK * LANES,
        places={0: SMEM},
    )
    out_ahead, out_behind = send(out_ahead, ("x", 1)), send(out_behind, ("x", -1))
    (dqkv,) = call(
        project_back_kernel,
        [((TOK, 1024), BF)],
        (dqk_raw, dv_raw, d_got, cosine, sine),
        TOK * D * 16,
    )
    grads = (spot_x, n1_x, dqkv)
    low, high = call(
        far_kernel,
        [((144, 1024), BF), ((144, 1024), BF)],
        grads,
        2 * 288 * TOK * 1024,
        places={0: SMEM},
    )
    low, high, act, dqkv_later = lax.optimization_barrier((low, high, act, dqkv))
    (dn1_part,) = call(
        normed_back_kernel,
        [((TOK, D), F32)],
        (dqkv_later, qk_w, vo_w),
        2 * TOK * D * 1024,
        places={1: FAR, 2: FAR},
    )
    dn1_part = dn1_part.reshape(2, ROWS, D)
    low_got, high_got, out_far = lax.optimization_barrier(
        (send(low, ("x", 1)), send(high, ("x", -1)), out_far)
    )
    ahead, behind = call(
        near_kernel,
        [((288, 1024), BF), ((288, 1024), BF)],
        grads + (low_got, high_got),
        4 * 288 * TOK * 1024,
        places={0: SMEM},
    )
    (by_place,) = call(
        own_kernel,
        [((288, 2 * PART), BF)],
        grads + (send(ahead, ("x", 1)), send(behind, ("x", -1)))
        + (out_own, out_ahead, out_behind, out_far, by_z),
        2 * 288 * TOK * 2 * PART,
        scratch=[pltpu.VMEM((288, 2 * PART), BF)],
        places={0: SMEM},
    )
    (down,) = call(
        down_kernel,
        [((TOK, D), F32)],
        (act, feed_w),
        2 * TOK * HALF * D,
        scratch=[pltpu.VMEM((TILE, 3 * D), BF), pltpu.SemaphoreType.DMA],
        places={0: FAR, 1: HERE},
    )
    down = down.reshape(2, ROWS, D)
    down_got = send(pick(down, 0, 1 - c).astype(BF), "c")
    own_kf = pick(kf.reshape(2, ROWS, 1), 0, c)
    mixed = pick(middle.reshape(2, ROWS, D), 0, c) + own_kf * (pick(down, 0, c) + down_got)

    attention_sum = reduce_direct(by_place.astype(F32).reshape(4, 72, 2 * PART), "z", z, 0)
    attention_sum = mm(by_y, attention_sum.astype(BF)).reshape(4, 24, 2 * PART)
    a24 = reduce_direct(attention_sum, "y", y, 0)
    a24, feed_sum = lax.optimization_barrier((a24, feed_sum))
    dn1 = pick(dn1_part, 0, c) + send(pick(dn1_part, 0, 1 - c).astype(BF), "c")
    hat_own, scale_own = normal(tokens.astype(F32))
    back_tokens = pick(dmiddle.reshape(2, ROWS, D), 0, c) + normal_pull(
        hat_own, scale_own, dn1 * g1
    )

    def swap(own, other):
        got = send(other.astype(BF), "c").astype(F32)
        return jnp.where(first_core, own, got), jnp.where(first_core, got, own)

    by_chip = feed_sum.reshape(4, 8, WIDE)
    mine, other_rows, back_down = call(
        unpack_kernel,
        [((9, FF), BF), ((9, FF), BF), ((24, D), F32)],
        (
            core,
            pick(by_chip, 0, x),
            send(pick(by_chip, 0, wrap(x, 1)), ("x", 1)),
            send(pick(by_chip, 0, wrap(x, -1)), ("x", -1)),
            send(pick(by_chip, 0, wrap(x, 2)), ("x", 2)),
        ),
        1,
        places={0: SMEM},
    )
    back_gate, back_up, back_two = call(
        join_kernel,
        [((9, FF), F32), ((9, FF), F32), ((9, 1), F32)],
        (core, mine, send(other_rows, "c"), wg, wu, gain_two.astype(F32).reshape(9, 1)),
        8 * 9 * 768 * 768 * 2,
        places={0: SMEM},
    )
    back_two = back_two.reshape(9)
    core0, core1 = a24[:9], a24[9:18]
    a0, a1 = swap(jnp.where(first_core, core0, core1), jnp.where(first_core, core1, core0))
    join = lambda low, high: jnp.concatenate([a0[:, low:high], a1[:, low:high]], axis=1)
    back_query = join(192, 768)
    back_key = join(0, 192)
    back_value = join(832, 1024)
    back_out = join(1024, 1600)
    dots = lambda weight, grad: jnp.sum(weight.astype(F32) * grad, axis=1)
    back_one = (
        dots(wq, back_query) + dots(wk, back_key) + dots(wv, back_value)
    ) / gain_one.astype(F32)
    return (
        mixed.astype(BF),
        back_tokens,
        back_one,
        back_query,
        back_key,
        back_value,
        back_out,
        back_two,
        back_gate,
        back_up,
        back_down,
    )


def solution(mesh):
    fine = Mesh(mesh.devices.reshape([SIZES[name] for name in AXES]), AXES)
    row, rows = P(AXES), P(AXES, None)
    in_specs = (rows, row, row, row, rows, rows, rows, rows, row, rows, rows, rows, rows)
    out_specs = (rows, rows, row, rows, rows, rows, rows, row, rows, rows, rows)
    return jax.shard_map(
        on_device, mesh=fine, in_specs=in_specs, out_specs=out_specs, check_vma=False
    )
```

```python
import math

import jax
import jax.numpy as jnp
from jax import lax
from jax.experimental import pallas as pl
from jax.experimental.pallas import tpu as pltpu
from jax.sharding import Mesh, PartitionSpec as P

H = 18
KV = 6
HD = 64
D = 1152
FF = 3072
ROWS = 128
EPSILON = 1e-05
NEGATIVE = -1e30
AXES = ("y", "z", "xh", "c", "xl")
SIZES = {"y": 4, "z": 4, "xh": 2, "c": 2, "xl": 2}
BF = jnp.bfloat16
F32 = jnp.float32
HQ = H // 2
HK = KV // 2
GROUP = H // KV
PART = 832
VPAD = 256
OWN = 576
LANES = 640
TOK = 2 * ROWS
HALF = FF // 2
SLOTS = 1536
SECOND, EXTRA, DOWN = FF, 2 * FF, 2 * FF + 768
WIDE = DOWN + 3 * D
TILE = 512
CHIPS = ("y", "z", "xh", "xl")


def places():
    for y in range(4):
        for z in range(4):
            for xh in range(2):
                for c in range(2):
                    for xl in range(2):
                        yield {"y": y, "z": z, "xh": xh, "c": c, "xl": xl}


def index_of(place):
    total = 0
    for name in AXES:
        total = total * SIZES[name] + place[name]
    return total


def shift_pairs(axis, step):
    pairs = []
    for place in places():
        other = dict(place)
        if axis == "x":
            spot = (place["xh"] * 2 + place["xl"] + step) % 4
            other["xh"], other["xl"] = spot // 2, spot % 2
        elif axis == "c":
            other["c"] = 1 - place["c"]
        else:
            other[axis] = (place[axis] + step) % 4
        pairs.append((index_of(place), index_of(other)))
    return pairs


PAIRS = {(axis, step): shift_pairs(axis, step) for axis in "xyz" for step in (1, -1, 2)}
PAIRS["c"] = shift_pairs("c", 1)
PAIRS["late"] = [
    (index_of(place), index_of({**place, "xl": 1})) for place in places() if place["xl"] == 0
]
PAIRS["early"] = [
    (index_of(place), index_of({**place, "xl": 0})) for place in places() if place["xl"] == 1
]


def send(value, key):
    return lax.ppermute(value, AXES, PAIRS[key])


def mm(left, right):
    return jnp.dot(left, right, preferred_element_type=F32)


def mm_t(left, right):
    return lax.dot_general(left, right, (((1,), (1,)), ((), ())), preferred_element_type=F32)


def inner(left, right):
    return lax.dot_general(left, right, (((0,), (0,)), ((), ())), preferred_element_type=F32)


def put(full, block, axis, index):
    starts = [0] * full.ndim
    starts[axis] = index
    return lax.dynamic_update_slice(full, jnp.expand_dims(block, axis), starts)


def pick(array, axis, index):
    return lax.dynamic_index_in_dim(array, index, axis, keepdims=False)


def wrap(spot, step):
    return lax.rem(spot + step + 4, 4)


def gather_direct(block, axis, spot, dim):
    shape = list(block.shape)
    shape.insert(dim, 4)
    full = jnp.zeros(shape, block.dtype)
    full = put(full, block, dim, spot)
    full = put(full, send(block, (axis, 1)), dim, wrap(spot, -1))
    full = put(full, send(block, (axis, -1)), dim, wrap(spot, 1))
    return put(full, send(block, (axis, 2)), dim, wrap(spot, 2))


def gather_ring(block, axis, spot, dim):
    half = block.shape[-2] // 2
    shape = list(block.shape)
    shape.insert(dim, 4)
    left = send(block, (axis, 1))
    right = send(block, (axis, -1))
    low = send(left[..., :half, :], (axis, 1))
    high = send(right[..., half:, :], (axis, -1))
    full = jnp.zeros(shape, block.dtype)
    full = put(full, block, dim, spot)
    full = put(full, left, dim, wrap(spot, -1))
    full = put(full, right, dim, wrap(spot, 1))
    far = jnp.concatenate([low, high], axis=-2)
    return put(full, far, dim, wrap(spot, 2))


def reduce_direct(parts, axis, spot, dim):
    low = parts.astype(BF)
    first = send(pick(low, dim, wrap(spot, 1)), (axis, 1))
    second = send(pick(low, dim, wrap(spot, -1)), (axis, -1))
    third = send(pick(low, dim, wrap(spot, 2)), (axis, 2))
    return pick(parts, dim, spot) + first + second + third


def normal(values):
    scale = lax.rsqrt(jnp.mean(values * values, axis=-1, keepdims=True) + EPSILON)
    return values * scale, scale


def normal_pull(hat, scale, grad):
    return scale * (grad - hat * jnp.mean(grad * hat, axis=-1, keepdims=True))


def halves_swapped(values):
    lane = lax.broadcasted_iota(jnp.int32, values.shape, 1)
    return jnp.where(
        lane % HD < HD // 2, pltpu.roll(values, 96, 1), pltpu.roll(values, 32, 1)
    )


SMEM = pl.BlockSpec(memory_space=pltpu.SMEM)
HERE = pl.BlockSpec(memory_space=pltpu.HBM)
FAR = "far"


def call(body, outs, args, flops, scratch=(), places=None, megabytes=24):
    total = sum(math.prod(a.shape) * a.dtype.itemsize for a in args)
    total += sum(math.prod(shape) * jnp.dtype(kind).itemsize for shape, kind in outs)
    places = places or {}

    def spec(index, shape):
        if places.get(index, FAR) is not FAR:
            return places[index]
        return pl.BlockSpec(
            shape, lambda i: (0,) * len(shape), pipeline_mode=pl.Buffered(1)
        )

    in_specs = [spec(i, a.shape) for i, a in enumerate(args)]
    out_specs = [spec(len(args) + i, shape) for i, (shape, _) in enumerate(outs)]
    return pl.pallas_call(
        body,
        grid=(1,),
        out_shape=[
            pltpu.HBM(shape, kind)
            if places.get(len(args) + i) in (HERE, FAR)
            else jax.ShapeDtypeStruct(shape, kind)
            for i, (shape, kind) in enumerate(outs)
        ],
        in_specs=in_specs,
        out_specs=out_specs,
        scratch_shapes=list(scratch),
        compiler_params=pltpu.CompilerParams(vmem_limit_bytes=megabytes << 20),
        cost_estimate=pl.CostEstimate(flops=flops, bytes_accessed=total, transcendentals=0),
    )(
        *[
            pltpu.with_memory_space_constraint(a, pltpu.HBM)
            if places.get(i) in (HERE, FAR)
            else a
            for i, a in enumerate(args)
        ]
    )


SCALE = 1.0 / math.sqrt(HD)


def sequence(s):
    return pl.ds(pl.multiple_of(s * ROWS, ROWS), ROWS)


def each_sequence(body):
    def step(s, carry):
        body(s)
        return carry

    lax.fori_loop(0, 2, step, 0)


def project_kernel(
    x_ref, wqk_ref, wvo_ref, cos_ref, sin_ref, doc_ref,
    gain_ref, n1_ref, qk_ref, kv_ref, raw_ref, v_ref,
):
    unit = (
        lax.broadcasted_iota(jnp.int32, (8, 64), 1)
        == lax.broadcasted_iota(jnp.int32, (8, 64), 0)
    ).astype(BF)
    gain_ref[...] = mm_t(unit, wqk_ref[:, 768:])
    hat, _ = normal(x_ref[...].astype(F32))
    n1 = (hat * gain_ref[0:1, :]).astype(BF)
    n1_ref[...] = n1
    raw_ref[...] = mm(n1, wqk_ref[:, :768])
    v_ref[...] = mm(n1, wvo_ref[:, :VPAD]).astype(BF)
    cosine, sine = cos_ref[...], sin_ref[...]
    lane = lax.broadcasted_iota(jnp.int32, (ROWS, 128), 1)

    def turn(s):
        rows = sequence(s)
        for j in range(6):
            at = slice(j * 128, j * 128 + 128)
            tile = raw_ref[rows, at]
            turned = (tile * cosine + halves_swapped(tile) * sine).astype(BF)
            qk_ref[rows, at] = turned
            if j == 0:
                kv_ref[rows, 0:128] = turned
            if j == 1:
                kv_ref[rows, 128:256] = jnp.where(lane < 64, turned, v_ref[rows, 0:128])
        kv_ref[rows, 256:384] = v_ref[rows, 128:256]

    each_sequence(turn)
    kv_ref[TOK:, :] = doc_ref[...]


def head_data(h, qk, kv, early):
    base = 192 + h * 192
    q = jnp.concatenate(
        [qk[:, base + 64 * g : base + 64 * g + 64] for g in range(GROUP)], axis=0
    )
    keys, vals = slice(64 * h, 64 * h + 64), slice(192 + 64 * h, 256 + 64 * h)
    return q, early[:, keys], kv[:, keys], early[:, vals], kv[:, vals]


def early_docs(late_ref, early_ref, row_ref):
    rows = early_ref[TOK:, :ROWS].astype(F32)
    row_ref[...] = jnp.where(late_ref[0] == 1, rows, -1.0)


def masks(s, dcol_ref, drow_ref, derow_ref):
    col = dcol_ref[sequence(s), :]
    at = lax.broadcasted_iota(jnp.int32, (ROWS, ROWS), 0)
    to = lax.broadcasted_iota(jnp.int32, (ROWS, ROWS), 1)
    mask_o = (to <= at) & (col == drow_ref[s])
    mask_e = col == derow_ref[pl.ds(s, 1), :]
    wide = lambda m: jnp.concatenate([jnp.where(m, 0.0, NEGATIVE)] * GROUP, axis=0)
    return wide(mask_e), wide(mask_o)


def softmax(q, ke, ko, mask_e, mask_o):
    se = jnp.where(mask_e == 0.0, mm_t(q, ke) * SCALE, NEGATIVE)
    so = jnp.where(mask_o == 0.0, mm_t(q, ko) * SCALE, NEGATIVE)
    top = jnp.maximum(
        jnp.max(se, axis=-1, keepdims=True), jnp.max(so, axis=-1, keepdims=True)
    )
    ee, eo = jnp.exp(se - top), jnp.exp(so - top)
    total = jnp.sum(ee, axis=-1, keepdims=True) + jnp.sum(eo, axis=-1, keepdims=True)
    return ee / total, eo / total


def split_heads(stacked):
    return [stacked[g * ROWS : g * ROWS + ROWS] for g in range(GROUP)]


def attend_kernel(
    qk_ref, kv_ref, early_ref, late_ref, dcol_ref, drow_ref, c_ref, w_hbm,
    o_ref, own_ref, derow_ref, w_ref, sem,
):
    load = pltpu.make_async_copy(out_rows(w_hbm, c_ref[0]), w_ref, sem)
    load.start()
    early_docs(late_ref, early_ref, derow_ref)

    def one(s):
        rows = sequence(s)
        qk, kv, early = qk_ref[rows, :], kv_ref[rows, :], early_ref[rows, :]
        mask_e, mask_o = masks(s, dcol_ref, drow_ref, derow_ref)
        pieces = []
        for h in range(HK):
            q, ke, ko, ve, vo = head_data(h, qk, kv, early)
            pe, po = softmax(q, ke, ko, mask_e, mask_o)
            pieces += split_heads(mm(pe.astype(BF), ve) + mm(po.astype(BF), vo))
        pieces.append(jnp.zeros((ROWS, LANES - OWN), F32))
        o_ref[rows, :] = jnp.concatenate(pieces, axis=1).astype(BF)

    each_sequence(one)
    load.wait()
    own_ref[...] = mm(o_ref[:, :OWN], w_ref[...])


def attend_back_kernel(
    qk_ref, kv_ref, early_ref, late_ref, dcol_ref, drow_ref, do_ref, got_ref,
    dqk_ref, dv_ref, de_ref, derow_ref,
):
    early_docs(late_ref, early_ref, derow_ref)

    def one(s):
        rows = sequence(s)
        qk, kv, early = qk_ref[rows, :], kv_ref[rows, :], early_ref[rows, :]
        do_all = (do_ref[rows, :] + got_ref[rows, :OWN].astype(F32)).astype(BF)
        mask_e, mask_o = masks(s, dcol_ref, drow_ref, derow_ref)
        dqs, dke, dko, dve, dvo = [], [], [], [], []
        for h in range(HK):
            q, ke, ko, ve, vo = head_data(h, qk, kv, early)
            pe, po = softmax(q, ke, ko, mask_e, mask_o)
            do = jnp.concatenate(
                [do_all[:, (GROUP * h + g) * 64 : (GROUP * h + g) * 64 + 64] for g in range(GROUP)],
                axis=0,
            )
            dpe, dpo = mm_t(do, ve), mm_t(do, vo)
            centre = jnp.sum(pe * dpe, axis=-1, keepdims=True) + jnp.sum(
                po * dpo, axis=-1, keepdims=True
            )
            dse = (pe * (dpe - centre)).astype(BF)
            dso = (po * (dpo - centre)).astype(BF)
            dqs += split_heads((mm(dse, ke) + mm(dso, ko)) * SCALE)
            dke.append(inner(dse, q) * SCALE)
            dko.append(inner(dso, q) * SCALE)
            dve.append(inner(pe.astype(BF), do))
            dvo.append(inner(po.astype(BF), do))
        dqk_ref[rows, :] = jnp.concatenate(dko + dqs, axis=1)
        dv_ref[rows, :] = jnp.concatenate([jnp.zeros((ROWS, 64), F32)] + dvo, axis=1)
        de_ref[rows, :] = jnp.concatenate(dke + dve, axis=1).astype(BF)

    each_sequence(one)


def project_back_kernel(
    dqk_ref, dv_ref, got_ref, cos_ref, sin_ref, low_ref
):
    cosine, sine = cos_ref[...], sin_ref[...]
    lane = lax.broadcasted_iota(jnp.int32, (ROWS, 128), 1)

    def turn(s):
        rows = sequence(s)
        got = got_ref[rows, :].astype(F32)
        for j in range(6):
            at = slice(j * 128, j * 128 + 128)
            tile = dqk_ref[rows, at]
            if j == 0:
                tile = tile + got[:, 0:128]
            if j == 1:
                tile = tile + jnp.where(lane < 64, got[:, 128:256], 0.0)
            low_ref[rows, at] = (tile * cosine - halves_swapped(tile) * sine).astype(BF)
        dv0 = dv_ref[rows, 0:128] + jnp.where(lane < 64, 0.0, got[:, 128:256])
        low_ref[rows, 768:896] = dv0.astype(BF)
        low_ref[rows, 896:1024] = (dv_ref[rows, 128:256] + got[:, 256:384]).astype(BF)

    each_sequence(turn)


def normed_back_kernel(low_ref, wqk_ref, wvo_ref, dn1_ref):
    dn1_ref[...] = mm_t(low_ref[:, :768], wqk_ref[:, :768]) + mm_t(
        low_ref[:, 768:], wvo_ref[:, :VPAD]
    )


def out_far_kernel(x_ref, o_ref, ba_ref, far_ref):
    far_ref[...] = mm(o_ref[wrap(x_ref[0], 2)], ba_ref[...]).astype(BF)


def out_near_kernel(x_ref, o_ref, ba_ref, own_ref, ahead_ref, behind_ref):
    for step, out in ((0, own_ref), (1, ahead_ref), (-1, behind_ref)):
        out[...] = mm(o_ref[wrap(x_ref[0], step)], ba_ref[...]).astype(BF)


def far_kernel(x_ref, n1_ref, dqkv_ref, low_ref, high_ref):
    chunk = mm(n1_ref[wrap(x_ref[0], 2)], dqkv_ref[...]).astype(BF)
    low_ref[...] = chunk[:144]
    high_ref[...] = chunk[144:]


def near_kernel(x_ref, n1_ref, dqkv_ref, low_ref, high_ref, ahead_ref, behind_ref):
    for step, out, add, first in ((1, ahead_ref, low_ref, 0), (-1, behind_ref, high_ref, 144)):
        chunk = mm(n1_ref[wrap(x_ref[0], step)], dqkv_ref[...])
        rows = slice(first, first + 144)
        out[...] = chunk.astype(BF)
        out[rows, :] = (chunk[rows] + add[...].astype(F32)).astype(BF)


def own_kernel(
    x_ref, n1_ref, dqkv_ref, first_ref, second_ref,
    o0_ref, o1_ref, o2_ref, o3_ref, order_ref, out_ref, sum_ref,
):
    total = mm(n1_ref[x_ref[0]], dqkv_ref[...])
    total = total + first_ref[...].astype(F32) + second_ref[...].astype(F32)
    sum_ref[:, :1024] = total.astype(BF)
    total = o0_ref[...].astype(F32) + o1_ref[...].astype(F32)
    total = total + o2_ref[...].astype(F32) + o3_ref[...].astype(F32)
    sum_ref[:, 1024:] = total.astype(BF)
    out_ref[...] = mm(order_ref[...], sum_ref[...]).astype(BF)


def out_rows(w_ref, c):
    return w_ref.at[pl.ds(pl.multiple_of(c * OWN, 64), OWN), pl.ds(VPAD, OWN)]


def out_kernel(c_ref, own_ref, got_ref, w_hbm, kf_ref, part_ref, low_ref, w_ref, sem):
    load = pltpu.make_async_copy(out_rows(w_hbm, 1 - c_ref[0]), w_ref, sem)
    load.start()
    load.wait()
    part = kf_ref[...] * (own_ref[...] + mm(got_ref[:, :OWN], w_ref[...]))
    part_ref[:, :OWN] = part
    part_ref[:, OWN:] = jnp.zeros((TOK, LANES - OWN), F32)
    low_ref[:, :OWN] = part.astype(BF)
    low_ref[:, OWN:] = jnp.zeros((TOK, LANES - OWN), BF)


def shuffle_map(shape, dim):
    to = lax.broadcasted_iota(jnp.int32, shape, dim)
    core, group = to // 384, (to % 384) // 128
    plane, along, unit = (to % 128) // 16, (to % 16) // 8, to % 8
    return plane * 96 + core * 48 + along * 24 + group * 8 + unit


def split_kernel(
    c_ref, gain_ref, wg_ref, wu_ref, wq_ref, wk_ref, wv_ref, wo_ref,
    own_ref, other_ref, rows_ref,
):
    at = lax.broadcasted_iota(jnp.int32, (768, 768), 0)
    order = (at == shuffle_map((1, 768), 1)).astype(F32).astype(BF)
    first = c_ref[0] == 0

    def write(at, zero, one):
        cols = slice(at, at + zero.shape[1])
        own_ref[:, cols] = jnp.where(first, zero, one).astype(BF)
        other_ref[:, cols] = jnp.where(first, one, zero).astype(BF)

    rows_ref[...] = jnp.zeros_like(rows_ref)
    for side, ref in enumerate((wg_ref, wu_ref)):
        for block in range(4):
            at = (side * 4 + block) * 16
            rows_ref[at : at + 9, :] = ref[:, block * 768 : block * 768 + 768]
    moved = mm(rows_ref[...], order)
    for side in range(2):
        for block in range(4):
            at = (side * 4 + block) * 16
            for group in range(3):
                zero = moved[at : at + 9, group * 128 : group * 128 + 128]
                one = moved[at : at + 9, 384 + group * 128 : 512 + group * 128]
                write(side * HALF + group * TILE + block * 128, zero, one)
    row = lax.broadcasted_iota(jnp.int32, (9, 64), 0)
    lane = lax.broadcasted_iota(jnp.int32, (9, 64), 1)
    gains = jnp.zeros((9, 64), F32)
    for i in range(9):
        for j in range(2):
            gains = jnp.where((row == i) & (lane == j), gain_ref[j, i], gains)
    blank = jnp.zeros((9, 64), F32)
    wq, wk, wv, wo = [ref[...].astype(F32) for ref in (wq_ref, wk_ref, wv_ref, wo_ref)]
    halves = [
        jnp.concatenate(
            [
                wk[:, h * 192 : h * 192 + 192],
                wq[:, h * OWN : h * OWN + OWN],
                gains,
                blank,
                wv[:, h * 192 : h * 192 + 192],
                wo[:, h * OWN : h * OWN + OWN],
            ],
            axis=1,
        )
        for h in range(2)
    ]
    write(FF, *halves)


def pack_kernel(c_ref, own_ref, got_ref, wd_ref, out_ref, block_ref):
    first = c_ref[0] == 0
    own, got = own_ref[:, :FF].astype(F32), got_ref[:, :FF].astype(F32)
    zero, one = jnp.where(first, own, got), jnp.where(first, got, own)
    out_ref[:, :SECOND] = zero[:8].astype(BF)
    out_ref[:, SECOND:EXTRA] = jnp.concatenate([zero[8:9], one[:7]], axis=0).astype(BF)
    for group in range(3):
        rows = []
        for row in (7, 8):
            for side in range(2):
                for half in range(2):
                    at = side * HALF + group * TILE + half * 256
                    rows.append(one[row : row + 1, at : at + 256])
        at = EXTRA + group * 256
        out_ref[:, at : at + 256] = jnp.concatenate(rows, axis=0).astype(BF)
        at = DOWN + group * D
        out_ref[:, at : at + D] = wd_ref[group * 8 : group * 8 + 8, :]
    own, got = own_ref[:, FF:].astype(F32), got_ref[:, FF:].astype(F32)
    blank = jnp.zeros((6, 2 * PART), F32)
    block_ref[...] = jnp.concatenate([own, got, blank], axis=0).astype(BF)


def unpack_kernel(c_ref, own_ref, a_ref, b_ref, d_ref, mine_ref, other_ref, down_ref):
    def total(at, size):
        cols = slice(at, at + size)
        low = own_ref[:, cols].astype(F32) + a_ref[:, cols].astype(F32)
        return low + b_ref[:, cols].astype(F32) + d_ref[:, cols].astype(F32)

    first = c_ref[0] == 0
    for group in range(3):
        down_ref[group * 8 : group * 8 + 8, :] = total(DOWN + group * D, D)
        extra = total(EXTRA + group * 256, 256)
        for side in range(2):
            at = side * HALF + group * TILE
            head, tail = total(at, TILE), total(SECOND + at, TILE)
            last = [
                jnp.concatenate(
                    [extra[4 * row + 2 * side + half :][:1] for half in range(2)], axis=1
                )
                for row in range(2)
            ]
            zero = jnp.concatenate([head, tail[:1]], axis=0)
            one = jnp.concatenate([tail[1:]] + last, axis=0)
            cols = slice(at, at + TILE)
            mine_ref[:, cols] = jnp.where(first, zero, one).astype(BF)
            other_ref[:, cols] = jnp.where(first, one, zero).astype(BF)


def join_kernel(
    c_ref, mine_ref, got_ref, wg_ref, wu_ref, gain_ref, gate_ref, up_ref, dot_ref, rows_ref
):
    at = lax.broadcasted_iota(jnp.int32, (768, 768), 1)
    order = (at == shuffle_map((768, 1), 0)).astype(F32).astype(BF)
    first = c_ref[0] == 0
    rows_ref[...] = jnp.zeros_like(rows_ref)
    for side in range(2):
        for block in range(4):
            rows = slice((side * 4 + block) * 16, (side * 4 + block) * 16 + 9)
            for core in range(2):
                for group in range(3):
                    at = side * HALF + group * TILE + block * 128
                    mine, got = mine_ref[:, at : at + 128], got_ref[:, at : at + 128]
                    piece = (
                        jnp.where(first, mine, got) if core == 0 else jnp.where(first, got, mine)
                    )
                    at = core * 384 + group * 128
                    rows_ref[rows, at : at + 128] = piece
    natural = mm(rows_ref[...], order)
    dots = jnp.zeros((9, 1), F32)
    for side, (w_ref, ref) in enumerate(((wg_ref, gate_ref), (wu_ref, up_ref))):
        for block in range(4):
            at = (side * 4 + block) * 16
            grad = natural[at : at + 9]
            cols = slice(block * 768, block * 768 + 768)
            ref[:, cols] = grad
            dots = dots + jnp.sum(w_ref[:, cols].astype(F32) * grad, axis=1, keepdims=True)
    row = lax.broadcasted_iota(jnp.int32, (9, 1), 0)
    gains = jnp.ones((9, 1), F32)
    for i in range(9):
        gains = jnp.where(row == i, gain_ref[1, i], gains)
    dots = dots / gains
    for i in range(9):
        dot_ref[i] = jnp.sum(jnp.where(row == i, dots, 0.0))


def feed_kernel(
    c_ref, g_ref, x_hbm, part_hbm, got_hbm, fs_hbm, bm_hbm, w_ref,
    mid_hbm, grad_ref, act_hbm, dgu_hbm,
    x_ref, part_ref, got_ref, fs_ref, bm_ref, mid_ref, act_ref, dgu_ref,
    n2_ref, n2t_ref, last_ref, last_t_ref, wm, we, wd, gm, ge, gd, in_sem, out_sem, side_sem,
):
    steps = HALF // TILE

    def places(t):
        at = pl.multiple_of(t * TILE, TILE)
        return (
            pl.ds(at, TILE),
            pl.ds(HALF + at, TILE),
            pl.ds(pl.multiple_of(t * 256, 256), 256),
            pl.ds(pl.multiple_of(t * D, 128), D),
        )

    def pairs(t, far, main, more, down):
        at = pl.multiple_of(t * TILE, TILE)
        gate_at, up_at, extra_at, down_at = places(t)
        everything, head, tail = slice(None), pl.ds(0, TILE), pl.ds(TILE, TILE)
        return (
            (far.at[:, pl.ds(at, TILE)], main.at[head, gate_at]),
            (far.at[:, pl.ds(SECOND + at, TILE)], main.at[tail, gate_at]),
            (far.at[:, pl.ds(HALF + at, TILE)], main.at[head, up_at]),
            (far.at[:, pl.ds(SECOND + HALF + at, TILE)], main.at[tail, up_at]),
            (far.at[:, pl.ds(EXTRA + pl.multiple_of(t * 256, 256), 256)], more.at[:, extra_at]),
            (far.at[:, pl.ds(DOWN + pl.multiple_of(t * D, 128), D)], down.at[:, down_at]),
        )

    def loads(t):
        return [
            pltpu.make_async_copy(far, near, in_sem.at[t, i])
            for i, (far, near) in enumerate(pairs(t, w_ref, wm, we, wd))
        ]

    def stores(t):
        return [
            pltpu.make_async_copy(near, far, out_sem.at[t, i])
            for i, (far, near) in enumerate(pairs(t, grad_ref, gm, ge, gd))
        ]

    sides = [
        pltpu.make_async_copy(src, dst, side_sem.at[i])
        for i, (src, dst) in enumerate(
            (
                (x_hbm, x_ref), (part_hbm, part_ref), (got_hbm, got_ref),
                (fs_hbm, fs_ref), (bm_hbm, bm_ref), (mid_ref, mid_hbm),
                (act_ref, act_hbm), (dgu_ref, dgu_hbm),
            )
        )
    ]
    for copy in sides[:5] + loads(0):
        copy.start()
    for copy in sides[:3]:
        copy.wait()
    for t in range(1, steps):
        for copy in loads(t):
            copy.start()

    first = c_ref[0] == 0
    part, got = part_ref[:, :OWN], got_ref[:, :OWN].astype(F32)
    low = jnp.where(first, part, got)
    high = jnp.where(first, got, part)
    middle = x_ref[...].astype(F32) + jnp.concatenate([low, high], axis=1)
    mid_ref[...] = middle
    sides[5].start()
    hat, _ = normal(middle)
    normed = (hat * g_ref[...]).astype(BF)
    for copy in sides[3:5]:
        copy.wait()
    n2_ref[...] = mm_t(normed, fs_ref[...]).astype(BF)
    n2t_ref[...] = n2_ref[...].T
    lane = lax.broadcasted_iota(jnp.int32, (TOK, TILE), 1) % 4
    row = lax.broadcasted_iota(jnp.int32, (TILE, TOK), 0) % 4
    last = n2_ref[:, 2 * TILE :].astype(F32)
    last_t = n2t_ref[2 * TILE :, :].astype(F32)
    for m in range(4):
        at = slice(m * TOK, m * TOK + TOK)
        last_ref[at, :] = jnp.where(lane == m, last, 0.0).astype(BF)
        last_t_ref[:, at] = jnp.where(row == m, last_t, 0.0).astype(BF)

    def step(t, carry):
        for copy in loads(t):
            copy.wait()
        gate_at, up_at, extra_at, down_at = places(t)
        rows, bm = n2_ref[:, : 2 * TILE], bm_ref[...]
        more = mm(last_ref[...], we[:, extra_at])
        parts = [more[m * TOK : m * TOK + TOK] for m in range(4)]
        gate = mm(rows, wm[:, gate_at]) + jnp.concatenate(parts[:2], axis=1)
        up = mm(rows, wm[:, up_at]) + jnp.concatenate(parts[2:], axis=1)
        dact = mm_t(bm, wd[:, down_at])
        sig = jax.nn.sigmoid(gate)
        silu = gate * sig
        act = (silu * up).astype(BF)
        dgate = (dact * up * (sig * (1.0 + gate * (1.0 - sig)))).astype(BF)
        dup = (dact * silu).astype(BF)
        act_ref[:, gate_at] = act
        dgu_ref[:, gate_at] = dgate
        dgu_ref[:, up_at] = dup
        rows_t, out = n2t_ref[: 2 * TILE, :], stores(t)
        gm[:, gate_at] = mm(rows_t, dgate).astype(BF)
        for copy in out[:2]:
            copy.start()
        gm[:, up_at] = mm(rows_t, dup).astype(BF)
        for copy in out[2:4]:
            copy.start()
        four = jnp.concatenate(
            [dgate[:, :256], dgate[:, 256:], dup[:, :256], dup[:, 256:]], axis=0
        )
        ge[:, extra_at] = mm(last_t_ref[...], four).astype(BF)
        out[4].start()
        gd[:, down_at] = inner(act, bm).astype(BF)
        out[5].start()
        return carry

    lax.fori_loop(0, steps, step, 0)
    for copy in sides[6:]:
        copy.start()
    for copy in sides[5:]:
        copy.wait()
    for t in range(steps):
        for copy in stores(t):
            copy.wait()


def feed_back_kernel(
    dgu_hbm, w_ref, fs_hbm, dn2_ref, low_ref,
    dgu_ref, fs_ref, wb, dgt_ref, four_ref, slots_ref, sem, side_sem,
):
    rows_each = 128
    steps = TILE // rows_each

    def load(t):
        rows = pl.ds(pl.multiple_of(t * rows_each, rows_each), rows_each)
        return pltpu.make_async_copy(w_ref.at[rows, pl.ds(0, DOWN)], wb.at[rows, :], sem.at[t])

    sides = [
        pltpu.make_async_copy(dgu_hbm, dgu_ref, side_sem.at[0]),
        pltpu.make_async_copy(fs_hbm, fs_ref, side_sem.at[1]),
    ]
    sides[0].start()
    for t in range(steps):
        load(t).start()
    sides[1].start()
    sides[0].wait()
    dgt_ref[...] = dgu_ref[...].T
    for m in range(4):
        for group in range(3):
            at = (m // 2) * HALF + group * TILE + (m % 2) * 256
            four_ref[group * 256 : group * 256 + 256, m * TOK : m * TOK + TOK] = dgt_ref[
                at : at + 256, :
            ]

    def step(t, carry):
        load(t).wait()
        at = pl.multiple_of(t * rows_each, rows_each)
        rows = pl.ds(at, rows_each)
        dgt = dgt_ref[...]
        slots_ref[rows, :] = mm(wb[rows, :SECOND], dgt).astype(BF)
        slots_ref[pl.ds(TILE + at, rows_each), :] = mm(wb[rows, SECOND:EXTRA], dgt).astype(BF)
        more = mm(wb[rows, EXTRA:], four_ref[...])
        row = lax.broadcasted_iota(jnp.int32, (rows_each, TOK), 0) % 4
        last = jnp.zeros((rows_each, TOK), F32)
        for m in range(4):
            last = jnp.where(row == m, more[:, m * TOK : m * TOK + TOK], last)
        slots_ref[pl.ds(2 * TILE + at, rows_each), :] = last.astype(BF)
        return carry

    lax.fori_loop(0, steps, step, 0)
    sides[1].wait()
    dn2 = inner(slots_ref[...], fs_ref[...])
    dn2_ref[...] = dn2
    low_ref[...] = dn2.astype(BF)


def down_kernel(act_ref, w_ref, down_ref, wb, sem):
    load = pltpu.make_async_copy(w_ref.at[:, pl.ds(DOWN, 3 * D)], wb, sem)
    load.start()
    load.wait()
    total = mm(act_ref[:, :TILE], wb[:, :D])
    for group in (1, 2):
        total = total + mm(
            act_ref[:, group * TILE : group * TILE + TILE], wb[:, group * D : group * D + D]
        )
    down_ref[...] = total


def middle_back_kernel(
    c_ref, part_ref, got_ref, mid_ref, cot_ref, g_ref, kf_ref, w_ref,
    dmid_ref, ba_ref, do_ref, other_ref,
):
    c = c_ref[0]
    dn2 = part_ref[...] + got_ref[...].astype(F32)
    hat, scale = normal(mid_ref[...])
    dmiddle = cot_ref[...] + normal_pull(hat, scale, dn2 * g_ref[...])
    dmid_ref[...] = dmiddle
    ba = kf_ref[...] * dmiddle
    half = jnp.where(c == 0, ba[:, :576], ba[:, 576:]).astype(BF)
    ba_ref[:, :OWN] = half
    ba_ref[:, OWN:] = jnp.zeros((TOK, LANES - OWN), BF)
    do_ref[...] = mm_t(half, out_rows(w_ref, c)[...])
    other_ref[:, :OWN] = mm_t(half, out_rows(w_ref, 1 - c)[...]).astype(BF)
    other_ref[:, OWN:] = jnp.zeros((TOK, LANES - OWN), BF)


def on_device(
    tokens, doc_ids, keep, gain_one, wq, wk, wv, wo, gain_two, wg, wu, wd, cotangent
):
    y, z, c = lax.axis_index("y"), lax.axis_index("z"), lax.axis_index("c")
    xl = lax.axis_index("xl")
    x = lax.axis_index("xh") * 2 + xl
    first_core = c == 0

    def both(own, other):
        return jnp.where(first_core, jnp.stack([own, other]), jnp.stack([other, own]))

    r = lax.broadcasted_iota(jnp.int32, (72, 96), 0)
    s = lax.broadcasted_iota(jnp.int32, (72, 96), 1)
    xh_r, rest = r // 36, r % 36
    c_r, rest = rest // 18, rest % 18
    xl_r, i_r = rest // 9, rest % 9
    k_r = lax.rem(xh_r * 2 + xl_r - x + 4, 4)
    select = (s == k_r * 24 + jnp.where(c_r == c, 0, 9) + i_r).astype(BF)

    def rows72(block):
        stacked = jnp.concatenate(
            [block, send(block, ("x", -1)), send(block, ("x", 2)), send(block, ("x", 1))], axis=0
        )
        return mm(select, stacked).astype(BF)

    def gather_zy(block):
        return gather_ring(
            gather_direct(block, "z", z, 0).reshape(288, -1), "y", y, 0
        ).reshape(D, -1)

    def gather_yz(block):
        return gather_ring(gather_direct(block, "y", y, 0), "z", z, 1).reshape(D, -1)

    core = c.astype(jnp.int32).reshape(1)
    both_cols = FF + 2 * PART
    both_gains = jnp.stack([gain_one, gain_two]).astype(F32)
    own, other = call(
        split_kernel,
        [((9, both_cols), BF), ((9, both_cols), BF)],
        (core, both_gains, wg, wu, wq, wk, wv, wo),
        8 * 9 * 768 * 768 * 2,
        scratch=[pltpu.VMEM((128, 768), BF)],
        places={0: SMEM, 1: SMEM} | {i: FAR for i in range(2, 8)},
    )
    feed_block, a_block = call(
        pack_kernel,
        [((8, WIDE), BF), ((24, 2 * PART), BF)],
        (core, own, send(other, "c"), wd),
        1,
        places={0: SMEM, 3: FAR},
    )
    feed_w = lax.all_gather(feed_block, CHIPS, axis=0, tiled=True)

    marks = jnp.stack([doc_ids, keep])
    a_block, x_got, marks_got, cot_got = lax.optimization_barrier(
        (a_block,) + tuple(send(v, "c") for v in (tokens, marks, cotangent))
    )
    x_all = both(tokens, x_got).reshape(TOK, D)
    marks = both(marks, marks_got)
    docs, kf = marks[:, 0].astype(F32), marks[:, 1].astype(F32).reshape(TOK, 1)
    doc_args = (docs.reshape(TOK, 1), docs.reshape(2, 1, ROWS))
    doc_rows = jnp.pad(docs, ((0, 14), (0, 384 - ROWS))).astype(BF)
    cot = both(cotangent, cot_got).reshape(TOK, D)

    a72 = rows72(a_block)
    slot = jnp.arange(SLOTS, dtype=jnp.int32)
    chip, inside = slot % TILE // 8, slot % 8
    inside = jnp.where(slot < 2 * TILE, slot // TILE * 8 + inside, 16 + inside // 4)
    of_slot = (chip // 2) * 36 + (inside // 9) * 18 + (chip % 2) * 9 + inside % 9
    spot = jnp.arange(D, dtype=jnp.int32)
    along, plane, inside = spot // 288, (spot % 288) // 18, spot % 18
    of_x = plane * 72 + (along // 2) * 36 + (inside // 9) * 18 + (along % 2) * 9 + inside % 9
    spot = jnp.arange(288, dtype=jnp.int32)
    of_z = ((spot % 72) // 18 * 4 + spot // 72) * 18 + spot % 18
    spot = jnp.arange(96, dtype=jnp.int32)
    of_y = jnp.where(spot % 24 < 18, spot // 24 * 18 + spot % 24, -1)
    orders, a72 = lax.optimization_barrier(((of_slot, of_x, of_z, of_y), a72))

    def one_hot(rows, columns):
        return (
            rows[:, None] == lax.broadcasted_iota(jnp.int32, (rows.shape[0], columns), 1)
        ).astype(BF)

    from_slots, by_x, by_z, by_y = [
        one_hot(rows, columns) for rows, columns in zip(orders, (D, D, 288, 72))
    ]

    qk_w = gather_zy(a72[:, :PART])
    vo_w = gather_yz(a72[:, PART:])

    lane = lax.broadcasted_iota(jnp.int32, (ROWS, 128), 1)
    spot = lax.broadcasted_iota(jnp.int32, (ROWS, 128), 0) + xl * ROWS
    freqs = 10000.0 ** (-((lane % (HD // 2)).astype(F32) * 2.0 / HD))
    angle = spot.astype(F32) * freqs
    cosine = jnp.cos(angle)
    sine = jnp.where(lane % HD < HD // 2, -1.0, 1.0) * jnp.sin(angle)
    bm = (kf * cot).astype(BF)
    early_work = (x_all, from_slots, bm, cosine, sine, kf, cot, by_x, doc_rows) + doc_args
    early_work, a_blocks = lax.optimization_barrier((early_work, (qk_w, vo_w)))
    x_all, from_slots, bm, cosine, sine, kf, cot, by_x, doc_rows = early_work[:9]
    late = (xl == 1).astype(jnp.int32).reshape(1)
    doc_args = (late,) + early_work[9:]
    qk_w, vo_w = a_blocks

    gains, n1, qk, kv = call(
        project_kernel,
        [((8, D), F32), ((TOK, D), BF), ((TOK, 768), BF), ((TOK + 16, 384), BF)],
        (x_all, qk_w, vo_w, cosine, sine, doc_rows),
        2 * TOK * D * 1024,
        scratch=[
            pltpu.VMEM((TOK, 768), F32),
            pltpu.VMEM((TOK, VPAD), BF),
        ],
        places={0: FAR, 7: FAR, 8: FAR, 9: FAR},
        megabytes=12,
    )
    g1, g2 = gains[0:1], gains[1:2]
    n1_x = mm_t(by_x, n1).astype(BF).reshape(4, 288, TOK)
    kv_early, n1_x = lax.optimization_barrier((send(kv, "late"), n1_x))
    o, out_own = call(
        attend_kernel,
        [((TOK, LANES), BF), ((TOK, OWN), F32)],
        (qk, kv, kv_early) + doc_args + (core, vo_w),
        4 * TOK * 576 * 256,
        scratch=[
            pltpu.VMEM((16, ROWS), F32),
            pltpu.VMEM((OWN, OWN), BF),
            pltpu.SemaphoreType.DMA,
        ],
        places={0: FAR, 1: FAR, 3: SMEM, 6: SMEM, 7: HERE, 8: FAR},
        megabytes=12,
    )
    o_got = send(o, "c")
    part, part_low = call(
        out_kernel,
        [((TOK, LANES), F32), ((TOK, LANES), BF)],
        (core, out_own, o_got, vo_w, kf),
        2 * TOK * OWN * OWN,
        scratch=[pltpu.VMEM((OWN, OWN), BF), pltpu.SemaphoreType.DMA],
        places={0: SMEM, 3: HERE, 5: FAR},
        megabytes=12,
    )
    part_got = send(part_low, "c")
    middle, feed_grad, act, dgu = call(
        feed_kernel,
        [((TOK, D), F32), ((TILE, WIDE), BF), ((TOK, HALF), BF), ((TOK, FF), BF)],
        (core, g2, x_all, part, part_got, from_slots, bm, feed_w),
        4 * TOK * SLOTS * (WIDE + D),
        scratch=[
            pltpu.VMEM((TOK, D), BF),
            pltpu.VMEM((TOK, LANES), F32),
            pltpu.VMEM((TOK, LANES), BF),
            pltpu.VMEM((SLOTS, D), BF),
            pltpu.VMEM((TOK, D), BF),
            pltpu.VMEM((TOK, D), F32),
            pltpu.VMEM((TOK, HALF), BF),
            pltpu.VMEM((TOK, FF), BF),
            pltpu.VMEM((TOK, SLOTS), BF),
            pltpu.VMEM((SLOTS, TOK), BF),
            pltpu.VMEM((4 * TOK, TILE), BF),
            pltpu.VMEM((TILE, 4 * TOK), BF),
            pltpu.VMEM((2 * TILE, FF), BF),
            pltpu.VMEM((TILE, 768), BF),
            pltpu.VMEM((TILE, 3 * D), BF),
            pltpu.VMEM((2 * TILE, FF), BF),
            pltpu.VMEM((TILE, 768), BF),
            pltpu.VMEM((TILE, 3 * D), BF),
            pltpu.SemaphoreType.DMA((3, 6)),
            pltpu.SemaphoreType.DMA((3, 6)),
            pltpu.SemaphoreType.DMA((8,)),
        ],
        places={0: SMEM} | {i: HERE for i in range(2, 12)},
        megabytes=52,
    )
    feed_sum = lax.psum_scatter(feed_grad, ("y", "z"), scatter_dimension=0, tiled=True)
    dn2_part, dn2_low = call(
        feed_back_kernel,
        [((TOK, D), F32), ((TOK, D), BF)],
        (dgu, feed_w, from_slots),
        2 * TOK * SLOTS * (FF + D),
        scratch=[
            pltpu.VMEM((TOK, FF), BF),
            pltpu.VMEM((SLOTS, D), BF),
            pltpu.VMEM((TILE, DOWN), BF),
            pltpu.VMEM((FF, TOK), BF),
            pltpu.VMEM((768, 4 * TOK), BF),
            pltpu.VMEM((SLOTS, TOK), BF),
            pltpu.SemaphoreType.DMA((4,)),
            pltpu.SemaphoreType.DMA((2,)),
        ],
        megabytes=40,
        places={0: HERE, 1: HERE, 2: HERE},
    )
    dn2_got = send(dn2_low, "c")
    dmiddle, ba_own, do_part, do_other = call(
        middle_back_kernel,
        [((TOK, D), F32), ((TOK, LANES), BF), ((TOK, OWN), F32), ((TOK, LANES), BF)],
        (core, dn2_part, dn2_got, middle, cot, g2, kf, vo_w),
        4 * TOK * D * 576,
        places={0: SMEM, 3: FAR, 4: FAR, 7: FAR, 8: FAR},
    )
    do_got = send(do_other, "c")
    o_all = jnp.where(
        first_core,
        jnp.concatenate([o[:, :OWN], o_got[:, :OWN]], axis=1),
        jnp.concatenate([o_got[:, :OWN], o[:, :OWN]], axis=1),
    )
    o_x = mm_t(by_x, o_all).astype(BF).reshape(4, 288, TOK)
    spot_x = x.astype(jnp.int32).reshape(1)
    (out_far,) = call(
        out_far_kernel,
        [((288, LANES), BF)],
        (spot_x, o_x, ba_own),
        2 * 288 * TOK * LANES,
        places={0: SMEM},
    )
    do_got, out_far = lax.optimization_barrier((do_got, out_far))
    out_far = send(out_far, ("x", 2))
    dqk_raw, dv_raw, de = call(
        attend_back_kernel,
        [((TOK, 768), F32), ((TOK, 256), F32), ((TOK, 384), BF)],
        (qk, kv, kv_early) + doc_args + (do_part, do_got),
        10 * TOK * 576 * 256,
        scratch=[pltpu.VMEM((16, ROWS), F32)],
        places={0: FAR, 1: FAR, 2: FAR, 3: SMEM},
    )
    d_got = send(de, "early")
    o_later, de_later = lax.optimization_barrier((o_x, de))
    out_own, out_ahead, out_behind = call(
        out_near_kernel,
        [((288, LANES), BF)] * 3,
        (spot_x, o_later, ba_own),
        6 * 288 * TOK * LANES,
        places={0: SMEM},
    )
    out_ahead, out_behind = send(out_ahead, ("x", 1)), send(out_behind, ("x", -1))
    (dqkv,) = call(
        project_back_kernel,
        [((TOK, 1024), BF)],
        (dqk_raw, dv_raw, d_got, cosine, sine),
        TOK * D * 16,
    )
    grads = (spot_x, n1_x, dqkv)
    low, high = call(
        far_kernel,
        [((144, 1024), BF), ((144, 1024), BF)],
        grads,
        2 * 288 * TOK * 1024,
        places={0: SMEM},
    )
    low, high, act, dqkv_later = lax.optimization_barrier((low, high, act, dqkv))
    (dn1_part,) = call(
        normed_back_kernel,
        [((TOK, D), F32)],
        (dqkv_later, qk_w, vo_w),
        2 * TOK * D * 1024,
        places={1: FAR, 2: FAR},
    )
    dn1_part = dn1_part.reshape(2, ROWS, D)
    low_got, high_got, out_far = lax.optimization_barrier(
        (send(low, ("x", 1)), send(high, ("x", -1)), out_far)
    )
    ahead, behind = call(
        near_kernel,
        [((288, 1024), BF), ((288, 1024), BF)],
        grads + (low_got, high_got),
        4 * 288 * TOK * 1024,
        places={0: SMEM},
    )
    (by_place,) = call(
        own_kernel,
        [((288, 2 * PART), BF)],
        grads + (send(ahead, ("x", 1)), send(behind, ("x", -1)))
        + (out_own, out_ahead, out_behind, out_far, by_z),
        2 * 288 * TOK * 2 * PART,
        scratch=[pltpu.VMEM((288, 2 * PART), BF)],
        places={0: SMEM},
    )
    (down,) = call(
        down_kernel,
        [((TOK, D), F32)],
        (act, feed_w),
        2 * TOK * HALF * D,
        scratch=[pltpu.VMEM((TILE, 3 * D), BF), pltpu.SemaphoreType.DMA],
        places={0: FAR, 1: HERE},
    )
    down = down.reshape(2, ROWS, D)
    down_got = send(pick(down, 0, 1 - c).astype(BF), "c")
    own_kf = pick(kf.reshape(2, ROWS, 1), 0, c)
    mixed = pick(middle.reshape(2, ROWS, D), 0, c) + own_kf * (pick(down, 0, c) + down_got)

    attention_sum = reduce_direct(by_place.astype(F32).reshape(4, 72, 2 * PART), "z", z, 0)
    attention_sum = mm(by_y, attention_sum.astype(BF)).reshape(4, 24, 2 * PART)
    a24 = reduce_direct(attention_sum, "y", y, 0)
    a24, feed_sum = lax.optimization_barrier((a24, feed_sum))
    dn1 = pick(dn1_part, 0, c) + send(pick(dn1_part, 0, 1 - c).astype(BF), "c")
    hat_own, scale_own = normal(tokens.astype(F32))
    back_tokens = pick(dmiddle.reshape(2, ROWS, D), 0, c) + normal_pull(
        hat_own, scale_own, dn1 * g1
    )

    def swap(own, other):
        got = send(other.astype(BF), "c").astype(F32)
        return jnp.where(first_core, own, got), jnp.where(first_core, got, own)

    by_chip = feed_sum.reshape(4, 8, WIDE)
    mine, other_rows, back_down = call(
        unpack_kernel,
        [((9, FF), BF), ((9, FF), BF), ((24, D), F32)],
        (
            core,
            pick(by_chip, 0, x),
            send(pick(by_chip, 0, wrap(x, 1)), ("x", 1)),
            send(pick(by_chip, 0, wrap(x, -1)), ("x", -1)),
            send(pick(by_chip, 0, wrap(x, 2)), ("x", 2)),
        ),
        1,
        places={0: SMEM},
    )
    back_gate, back_up, back_two = call(
        join_kernel,
        [((9, FF), F32), ((9, FF), F32), ((9,), F32)],
        (core, mine, send(other_rows, "c"), wg, wu, both_gains),
        8 * 9 * 768 * 768 * 2,
        scratch=[pltpu.VMEM((128, 768), BF)],
        places={0: SMEM, 3: FAR, 4: FAR, 5: SMEM, 8: SMEM},
    )
    core0, core1 = a24[:9], a24[9:18]
    a0, a1 = swap(jnp.where(first_core, core0, core1), jnp.where(first_core, core1, core0))
    join = lambda low, high: jnp.concatenate([a0[:, low:high], a1[:, low:high]], axis=1)
    back_query = join(192, 768)
    back_key = join(0, 192)
    back_value = join(832, 1024)
    back_out = join(1024, 1600)
    dots = lambda weight, grad: jnp.sum(weight.astype(F32) * grad, axis=1)
    back_one = (
        dots(wq, back_query) + dots(wk, back_key) + dots(wv, back_value)
    ) / gain_one.astype(F32)
    return (
        mixed.astype(BF),
        back_tokens,
        back_one,
        back_query,
        back_key,
        back_value,
        back_out,
        back_two,
        back_gate,
        back_up,
        back_down,
    )


def solution(mesh):
    fine = Mesh(mesh.devices.reshape([SIZES[name] for name in AXES]), AXES)
    row, rows = P(AXES), P(AXES, None)
    in_specs = (rows, row, row, row, rows, rows, rows, rows, row, rows, rows, rows, rows)
    out_specs = (rows, rows, row, rows, rows, rows, rows, row, rows, rows, rows)
    return jax.shard_map(
        on_device, mesh=fine, in_specs=in_specs, out_specs=out_specs, check_vma=False
    )
```

```python
import math

import jax
import jax.numpy as jnp
from jax import lax
from jax.experimental import pallas as pl
from jax.experimental.pallas import tpu as pltpu
from jax.sharding import Mesh, PartitionSpec as P

H = 18
KV = 6
HD = 64
D = 1152
FF = 3072
ROWS = 128
EPSILON = 1e-05
NEGATIVE = -1e30
AXES = ("y", "z", "xh", "c", "xl")
SIZES = {"y": 4, "z": 4, "xh": 2, "c": 2, "xl": 2}
BF = jnp.bfloat16
F32 = jnp.float32
HQ = H // 2
HK = KV // 2
GROUP = H // KV
PART = 832
VPAD = 256
OWN = 576
LANES = 640
TOK = 2 * ROWS
HALF = FF // 2
SLOTS = 1536
SECOND, EXTRA, DOWN = FF, 2 * FF, 2 * FF + 768
WIDE = DOWN + 3 * D
TILE = 512
CHIPS = ("y", "z", "xh", "xl")


def places():
    for y in range(4):
        for z in range(4):
            for xh in range(2):
                for c in range(2):
                    for xl in range(2):
                        yield {"y": y, "z": z, "xh": xh, "c": c, "xl": xl}


def index_of(place):
    total = 0
    for name in AXES:
        total = total * SIZES[name] + place[name]
    return total


def shift_pairs(axis, step):
    pairs = []
    for place in places():
        other = dict(place)
        if axis == "x":
            spot = (place["xh"] * 2 + place["xl"] + step) % 4
            other["xh"], other["xl"] = spot // 2, spot % 2
        elif axis == "c":
            other["c"] = 1 - place["c"]
        else:
            other[axis] = (place[axis] + step) % 4
        pairs.append((index_of(place), index_of(other)))
    return pairs


PAIRS = {(axis, step): shift_pairs(axis, step) for axis in "xyz" for step in (1, -1, 2)}
PAIRS["c"] = shift_pairs("c", 1)
PAIRS["late"] = [
    (index_of(place), index_of({**place, "xl": 1})) for place in places() if place["xl"] == 0
]
PAIRS["early"] = [
    (index_of(place), index_of({**place, "xl": 0})) for place in places() if place["xl"] == 1
]


def send(value, key):
    return lax.ppermute(value, AXES, PAIRS[key])


def mm(left, right):
    return jnp.dot(left, right, preferred_element_type=F32)


def mm_t(left, right):
    return lax.dot_general(left, right, (((1,), (1,)), ((), ())), preferred_element_type=F32)


def inner(left, right):
    return lax.dot_general(left, right, (((0,), (0,)), ((), ())), preferred_element_type=F32)


def put(full, block, axis, index):
    starts = [0] * full.ndim
    starts[axis] = index
    return lax.dynamic_update_slice(full, jnp.expand_dims(block, axis), starts)


def pick(array, axis, index):
    return lax.dynamic_index_in_dim(array, index, axis, keepdims=False)


def wrap(spot, step):
    return lax.rem(spot + step + 4, 4)


def gather_direct(block, axis, spot, dim):
    shape = list(block.shape)
    shape.insert(dim, 4)
    full = jnp.zeros(shape, block.dtype)
    full = put(full, block, dim, spot)
    full = put(full, send(block, (axis, 1)), dim, wrap(spot, -1))
    full = put(full, send(block, (axis, -1)), dim, wrap(spot, 1))
    return put(full, send(block, (axis, 2)), dim, wrap(spot, 2))


def gather_ring(block, axis, spot, dim):
    half = block.shape[-2] // 2
    shape = list(block.shape)
    shape.insert(dim, 4)
    left = send(block, (axis, 1))
    right = send(block, (axis, -1))
    low = send(left[..., :half, :], (axis, 1))
    high = send(right[..., half:, :], (axis, -1))
    full = jnp.zeros(shape, block.dtype)
    full = put(full, block, dim, spot)
    full = put(full, left, dim, wrap(spot, -1))
    full = put(full, right, dim, wrap(spot, 1))
    far = jnp.concatenate([low, high], axis=-2)
    return put(full, far, dim, wrap(spot, 2))


def reduce_direct(parts, axis, spot, dim):
    low = parts.astype(BF)
    first = send(pick(low, dim, wrap(spot, 1)), (axis, 1))
    second = send(pick(low, dim, wrap(spot, -1)), (axis, -1))
    third = send(pick(low, dim, wrap(spot, 2)), (axis, 2))
    return pick(parts, dim, spot) + first + second + third


def normal(values):
    scale = lax.rsqrt(jnp.mean(values * values, axis=-1, keepdims=True) + EPSILON)
    return values * scale, scale


def normal_pull(hat, scale, grad):
    return scale * (grad - hat * jnp.mean(grad * hat, axis=-1, keepdims=True))


def halves_swapped(values):
    lane = lax.broadcasted_iota(jnp.int32, values.shape, 1)
    return jnp.where(
        lane % HD < HD // 2, pltpu.roll(values, 96, 1), pltpu.roll(values, 32, 1)
    )


SMEM = pl.BlockSpec(memory_space=pltpu.SMEM)
HERE = pl.BlockSpec(memory_space=pltpu.HBM)
FAR = "far"


def call(body, outs, args, flops, scratch=(), places=None, megabytes=24):
    total = sum(math.prod(a.shape) * a.dtype.itemsize for a in args)
    total += sum(math.prod(shape) * jnp.dtype(kind).itemsize for shape, kind in outs)
    places = places or {}

    def spec(index, shape):
        if places.get(index, FAR) is not FAR:
            return places[index]
        return pl.BlockSpec(
            shape, lambda i: (0,) * len(shape), pipeline_mode=pl.Buffered(1)
        )

    in_specs = [spec(i, a.shape) for i, a in enumerate(args)]
    out_specs = [spec(len(args) + i, shape) for i, (shape, _) in enumerate(outs)]
    return pl.pallas_call(
        body,
        grid=(1,),
        out_shape=[
            pltpu.HBM(shape, kind)
            if places.get(len(args) + i) in (HERE, FAR)
            else jax.ShapeDtypeStruct(shape, kind)
            for i, (shape, kind) in enumerate(outs)
        ],
        in_specs=in_specs,
        out_specs=out_specs,
        scratch_shapes=list(scratch),
        compiler_params=pltpu.CompilerParams(vmem_limit_bytes=megabytes << 20),
        cost_estimate=pl.CostEstimate(flops=flops, bytes_accessed=total, transcendentals=0),
    )(
        *[
            pltpu.with_memory_space_constraint(a, pltpu.HBM)
            if places.get(i) in (HERE, FAR)
            else a
            for i, a in enumerate(args)
        ]
    )


SCALE = 1.0 / math.sqrt(HD)


def sequence(s):
    return pl.ds(pl.multiple_of(s * ROWS, ROWS), ROWS)


def each_sequence(body):
    def step(s, carry):
        body(s)
        return carry

    lax.fori_loop(0, 2, step, 0)


def project_kernel(
    x_ref, wqk_ref, wvo_ref, cos_ref, sin_ref, doc_ref,
    gain_ref, n1_ref, qk_ref, kv_ref, raw_ref, v_ref,
):
    unit = (
        lax.broadcasted_iota(jnp.int32, (8, 64), 1)
        == lax.broadcasted_iota(jnp.int32, (8, 64), 0)
    ).astype(BF)
    gain_ref[...] = mm_t(unit, wqk_ref[:, 768:])
    hat, _ = normal(x_ref[...].astype(F32))
    n1 = (hat * gain_ref[0:1, :]).astype(BF)
    n1_ref[...] = n1
    raw_ref[...] = mm(n1, wqk_ref[:, :768])
    v_ref[...] = mm(n1, wvo_ref[:, :VPAD]).astype(BF)
    cosine, sine = cos_ref[...], sin_ref[...]
    lane = lax.broadcasted_iota(jnp.int32, (ROWS, 128), 1)

    def turn(s):
        rows = sequence(s)
        for j in range(6):
            at = slice(j * 128, j * 128 + 128)
            tile = raw_ref[rows, at]
            turned = (tile * cosine + halves_swapped(tile) * sine).astype(BF)
            qk_ref[rows, at] = turned
            if j == 0:
                kv_ref[rows, 0:128] = turned
            if j == 1:
                kv_ref[rows, 128:256] = jnp.where(lane < 64, turned, v_ref[rows, 0:128])
        kv_ref[rows, 256:384] = v_ref[rows, 128:256]

    each_sequence(turn)
    kv_ref[TOK:, :] = doc_ref[...]


def head_data(h, qk, kv, early):
    base = 192 + h * 192
    q = jnp.concatenate(
        [qk[:, base + 64 * g : base + 64 * g + 64] for g in range(GROUP)], axis=0
    )
    keys, vals = slice(64 * h, 64 * h + 64), slice(192 + 64 * h, 256 + 64 * h)
    return q, early[:, keys], kv[:, keys], early[:, vals], kv[:, vals]


def early_docs(late_ref, early_ref, row_ref):
    rows = early_ref[TOK:, :ROWS].astype(F32)
    row_ref[...] = jnp.where(late_ref[0] == 1, rows, -1.0)


def masks(s, dcol_ref, drow_ref, derow_ref):
    col = dcol_ref[sequence(s), :]
    at = lax.broadcasted_iota(jnp.int32, (ROWS, ROWS), 0)
    to = lax.broadcasted_iota(jnp.int32, (ROWS, ROWS), 1)
    mask_o = (to <= at) & (col == drow_ref[s])
    mask_e = col == derow_ref[pl.ds(s, 1), :]
    wide = lambda m: jnp.concatenate([jnp.where(m, 0.0, NEGATIVE)] * GROUP, axis=0)
    return wide(mask_e), wide(mask_o)


def softmax(q, ke, ko, mask_e, mask_o):
    se = jnp.where(mask_e == 0.0, mm_t(q, ke) * SCALE, NEGATIVE)
    so = jnp.where(mask_o == 0.0, mm_t(q, ko) * SCALE, NEGATIVE)
    top = jnp.maximum(
        jnp.max(se, axis=-1, keepdims=True), jnp.max(so, axis=-1, keepdims=True)
    )
    ee, eo = jnp.exp(se - top), jnp.exp(so - top)
    total = jnp.sum(ee, axis=-1, keepdims=True) + jnp.sum(eo, axis=-1, keepdims=True)
    return ee / total, eo / total


def split_heads(stacked):
    return [stacked[g * ROWS : g * ROWS + ROWS] for g in range(GROUP)]


def attend_kernel(
    qk_ref, kv_ref, early_ref, late_ref, dcol_ref, drow_ref, c_ref, w_hbm,
    o_ref, own_ref, derow_ref, w_ref, sem,
):
    load = pltpu.make_async_copy(out_rows(w_hbm, c_ref[0]), w_ref, sem)
    load.start()
    early_docs(late_ref, early_ref, derow_ref)

    def one(s):
        rows = sequence(s)
        qk, kv, early = qk_ref[rows, :], kv_ref[rows, :], early_ref[rows, :]
        mask_e, mask_o = masks(s, dcol_ref, drow_ref, derow_ref)
        pieces = []
        for h in range(HK):
            q, ke, ko, ve, vo = head_data(h, qk, kv, early)
            pe, po = softmax(q, ke, ko, mask_e, mask_o)
            pieces += split_heads(mm(pe.astype(BF), ve) + mm(po.astype(BF), vo))
        pieces.append(jnp.zeros((ROWS, LANES - OWN), F32))
        o_ref[rows, :] = jnp.concatenate(pieces, axis=1).astype(BF)

    each_sequence(one)
    load.wait()
    own_ref[...] = mm(o_ref[:, :OWN], w_ref[...])


def attend_back_kernel(
    qk_ref, kv_ref, early_ref, late_ref, dcol_ref, drow_ref, do_ref, got_ref,
    dqk_ref, dv_ref, de_ref, derow_ref,
):
    early_docs(late_ref, early_ref, derow_ref)

    def one(s):
        rows = sequence(s)
        qk, kv, early = qk_ref[rows, :], kv_ref[rows, :], early_ref[rows, :]
        do_all = (do_ref[rows, :] + got_ref[rows, :OWN].astype(F32)).astype(BF)
        mask_e, mask_o = masks(s, dcol_ref, drow_ref, derow_ref)
        dqs, dke, dko, dve, dvo = [], [], [], [], []
        for h in range(HK):
            q, ke, ko, ve, vo = head_data(h, qk, kv, early)
            pe, po = softmax(q, ke, ko, mask_e, mask_o)
            do = jnp.concatenate(
                [do_all[:, (GROUP * h + g) * 64 : (GROUP * h + g) * 64 + 64] for g in range(GROUP)],
                axis=0,
            )
            dpe, dpo = mm_t(do, ve), mm_t(do, vo)
            centre = jnp.sum(pe * dpe, axis=-1, keepdims=True) + jnp.sum(
                po * dpo, axis=-1, keepdims=True
            )
            dse = (pe * (dpe - centre)).astype(BF)
            dso = (po * (dpo - centre)).astype(BF)
            dqs += split_heads((mm(dse, ke) + mm(dso, ko)) * SCALE)
            dke.append(inner(dse, q) * SCALE)
            dko.append(inner(dso, q) * SCALE)
            dve.append(inner(pe.astype(BF), do))
            dvo.append(inner(po.astype(BF), do))
        dqk_ref[rows, :] = jnp.concatenate(dko + dqs, axis=1)
        dv_ref[rows, :] = jnp.concatenate([jnp.zeros((ROWS, 64), F32)] + dvo, axis=1)
        de_ref[rows, :] = jnp.concatenate(dke + dve, axis=1).astype(BF)

    each_sequence(one)


def project_back_kernel(
    dqk_ref, dv_ref, got_ref, cos_ref, sin_ref, low_ref
):
    cosine, sine = cos_ref[...], sin_ref[...]
    lane = lax.broadcasted_iota(jnp.int32, (ROWS, 128), 1)

    def turn(s):
        rows = sequence(s)
        got = got_ref[rows, :].astype(F32)
        for j in range(6):
            at = slice(j * 128, j * 128 + 128)
            tile = dqk_ref[rows, at]
            if j == 0:
                tile = tile + got[:, 0:128]
            if j == 1:
                tile = tile + jnp.where(lane < 64, got[:, 128:256], 0.0)
            low_ref[rows, at] = (tile * cosine - halves_swapped(tile) * sine).astype(BF)
        dv0 = dv_ref[rows, 0:128] + jnp.where(lane < 64, 0.0, got[:, 128:256])
        low_ref[rows, 768:896] = dv0.astype(BF)
        low_ref[rows, 896:1024] = (dv_ref[rows, 128:256] + got[:, 256:384]).astype(BF)

    each_sequence(turn)


def normed_back_kernel(low_ref, wqk_ref, wvo_ref, dn1_ref):
    dn1_ref[...] = mm_t(low_ref[:, :768], wqk_ref[:, :768]) + mm_t(
        low_ref[:, 768:], wvo_ref[:, :VPAD]
    )


def out_far_kernel(x_ref, o_ref, ba_ref, far_ref):
    far_ref[...] = mm(o_ref[wrap(x_ref[0], 2)], ba_ref[...]).astype(BF)


def out_near_kernel(x_ref, o_ref, ba_ref, own_ref, ahead_ref, behind_ref):
    for step, out in ((0, own_ref), (1, ahead_ref), (-1, behind_ref)):
        out[...] = mm(o_ref[wrap(x_ref[0], step)], ba_ref[...]).astype(BF)


def far_kernel(x_ref, n1_ref, dqkv_ref, low_ref, high_ref):
    chunk = mm(n1_ref[wrap(x_ref[0], 2)], dqkv_ref[...]).astype(BF)
    low_ref[...] = chunk[:144]
    high_ref[...] = chunk[144:]


def near_kernel(x_ref, n1_ref, dqkv_ref, low_ref, high_ref, ahead_ref, behind_ref):
    for step, out, add, first in ((1, ahead_ref, low_ref, 0), (-1, behind_ref, high_ref, 144)):
        chunk = mm(n1_ref[wrap(x_ref[0], step)], dqkv_ref[...])
        rows = slice(first, first + 144)
        out[...] = chunk.astype(BF)
        out[rows, :] = (chunk[rows] + add[...].astype(F32)).astype(BF)


def own_kernel(
    x_ref, n1_ref, dqkv_ref, first_ref, second_ref,
    o0_ref, o1_ref, o2_ref, o3_ref, order_ref, out_ref, sum_ref,
):
    total = mm(n1_ref[x_ref[0]], dqkv_ref[...])
    total = total + first_ref[...].astype(F32) + second_ref[...].astype(F32)
    sum_ref[:, :1024] = total.astype(BF)
    total = o0_ref[...].astype(F32) + o1_ref[...].astype(F32)
    total = total + o2_ref[...].astype(F32) + o3_ref[...].astype(F32)
    sum_ref[:, 1024:] = total.astype(BF)
    out_ref[...] = mm(order_ref[...], sum_ref[...]).astype(BF)


def out_rows(w_ref, c):
    return w_ref.at[pl.ds(pl.multiple_of(c * OWN, 64), OWN), pl.ds(VPAD, OWN)]


def out_kernel(c_ref, own_ref, got_ref, w_hbm, kf_ref, part_ref, low_ref, w_ref, sem):
    load = pltpu.make_async_copy(out_rows(w_hbm, 1 - c_ref[0]), w_ref, sem)
    load.start()
    load.wait()
    part = kf_ref[...] * (own_ref[...] + mm(got_ref[:, :OWN], w_ref[...]))
    part_ref[:, :OWN] = part
    part_ref[:, OWN:] = jnp.zeros((TOK, LANES - OWN), F32)
    low_ref[:, :OWN] = part.astype(BF)
    low_ref[:, OWN:] = jnp.zeros((TOK, LANES - OWN), BF)


def shuffle_map(shape, dim):
    to = lax.broadcasted_iota(jnp.int32, shape, dim)
    core, group = to // 384, (to % 384) // 128
    plane, along, unit = (to % 128) // 16, (to % 16) // 8, to % 8
    return plane * 96 + core * 48 + along * 24 + group * 8 + unit


def split_kernel(
    c_ref, gain_ref, wg_ref, wu_ref, wq_ref, wk_ref, wv_ref, wo_ref,
    own_ref, other_ref, rows_ref,
):
    at = lax.broadcasted_iota(jnp.int32, (768, 768), 0)
    order = (at == shuffle_map((1, 768), 1)).astype(F32).astype(BF)
    first = c_ref[0] == 0

    def write(at, zero, one):
        cols = slice(at, at + zero.shape[1])
        own_ref[:, cols] = jnp.where(first, zero, one).astype(BF)
        other_ref[:, cols] = jnp.where(first, one, zero).astype(BF)

    rows_ref[...] = jnp.zeros_like(rows_ref)
    for side, ref in enumerate((wg_ref, wu_ref)):
        for block in range(4):
            at = (side * 4 + block) * 16
            rows_ref[at : at + 9, :] = ref[:, block * 768 : block * 768 + 768]
    moved = mm(rows_ref[...], order)
    for side in range(2):
        for block in range(4):
            at = (side * 4 + block) * 16
            for group in range(3):
                zero = moved[at : at + 9, group * 128 : group * 128 + 128]
                one = moved[at : at + 9, 384 + group * 128 : 512 + group * 128]
                write(side * HALF + group * TILE + block * 128, zero, one)
    row = lax.broadcasted_iota(jnp.int32, (9, 64), 0)
    lane = lax.broadcasted_iota(jnp.int32, (9, 64), 1)
    gains = jnp.zeros((9, 64), F32)
    for i in range(9):
        for j in range(2):
            gains = jnp.where((row == i) & (lane == j), gain_ref[j, i], gains)
    blank = jnp.zeros((9, 64), F32)
    wq, wk, wv, wo = [ref[...].astype(F32) for ref in (wq_ref, wk_ref, wv_ref, wo_ref)]
    halves = [
        jnp.concatenate(
            [
                wk[:, h * 192 : h * 192 + 192],
                wq[:, h * OWN : h * OWN + OWN],
                gains,
                blank,
                wv[:, h * 192 : h * 192 + 192],
                wo[:, h * OWN : h * OWN + OWN],
            ],
            axis=1,
        )
        for h in range(2)
    ]
    write(FF, *halves)


def pack_kernel(c_ref, own_ref, got_ref, wd_ref, out_ref, block_ref):
    first = c_ref[0] == 0
    own, got = own_ref[:, :FF].astype(F32), got_ref[:, :FF].astype(F32)
    zero, one = jnp.where(first, own, got), jnp.where(first, got, own)
    out_ref[:, :SECOND] = zero[:8].astype(BF)
    out_ref[:, SECOND:EXTRA] = jnp.concatenate([zero[8:9], one[:7]], axis=0).astype(BF)
    for group in range(3):
        rows = []
        for row in (7, 8):
            for side in range(2):
                for half in range(2):
                    at = side * HALF + group * TILE + half * 256
                    rows.append(one[row : row + 1, at : at + 256])
        at = EXTRA + group * 256
        out_ref[:, at : at + 256] = jnp.concatenate(rows, axis=0).astype(BF)
        at = DOWN + group * D
        out_ref[:, at : at + D] = wd_ref[group * 8 : group * 8 + 8, :]
    own, got = own_ref[:, FF:].astype(F32), got_ref[:, FF:].astype(F32)
    blank = jnp.zeros((6, 2 * PART), F32)
    block_ref[...] = jnp.concatenate([own, got, blank], axis=0).astype(BF)


def unpack_kernel(c_ref, own_ref, a_ref, b_ref, d_ref, mine_ref, other_ref, down_ref):
    def total(at, size):
        cols = slice(at, at + size)
        low = own_ref[:, cols].astype(F32) + a_ref[:, cols].astype(F32)
        return low + b_ref[:, cols].astype(F32) + d_ref[:, cols].astype(F32)

    first = c_ref[0] == 0
    for group in range(3):
        down_ref[group * 8 : group * 8 + 8, :] = total(DOWN + group * D, D)
        extra = total(EXTRA + group * 256, 256)
        for side in range(2):
            at = side * HALF + group * TILE
            head, tail = total(at, TILE), total(SECOND + at, TILE)
            last = [
                jnp.concatenate(
                    [extra[4 * row + 2 * side + half :][:1] for half in range(2)], axis=1
                )
                for row in range(2)
            ]
            zero = jnp.concatenate([head, tail[:1]], axis=0)
            one = jnp.concatenate([tail[1:]] + last, axis=0)
            cols = slice(at, at + TILE)
            mine_ref[:, cols] = jnp.where(first, zero, one).astype(BF)
            other_ref[:, cols] = jnp.where(first, one, zero).astype(BF)


def join_kernel(
    c_ref, mine_ref, got_ref, wg_ref, wu_ref, gain_ref, gate_ref, up_ref, dot_ref, rows_ref
):
    at = lax.broadcasted_iota(jnp.int32, (768, 768), 1)
    order = (at == shuffle_map((768, 1), 0)).astype(F32).astype(BF)
    first = c_ref[0] == 0
    rows_ref[...] = jnp.zeros_like(rows_ref)
    for side in range(2):
        for block in range(4):
            rows = slice((side * 4 + block) * 16, (side * 4 + block) * 16 + 9)
            for core in range(2):
                for group in range(3):
                    at = side * HALF + group * TILE + block * 128
                    mine, got = mine_ref[:, at : at + 128], got_ref[:, at : at + 128]
                    piece = (
                        jnp.where(first, mine, got) if core == 0 else jnp.where(first, got, mine)
                    )
                    at = core * 384 + group * 128
                    rows_ref[rows, at : at + 128] = piece
    natural = mm(rows_ref[...], order)
    dots = jnp.zeros((9, 1), F32)
    for side, (w_ref, ref) in enumerate(((wg_ref, gate_ref), (wu_ref, up_ref))):
        for block in range(4):
            at = (side * 4 + block) * 16
            grad = natural[at : at + 9]
            cols = slice(block * 768, block * 768 + 768)
            ref[:, cols] = grad
            dots = dots + jnp.sum(w_ref[:, cols].astype(F32) * grad, axis=1, keepdims=True)
    row = lax.broadcasted_iota(jnp.int32, (9, 1), 0)
    gains = jnp.ones((9, 1), F32)
    for i in range(9):
        gains = jnp.where(row == i, gain_ref[1, i], gains)
    dots = dots / gains
    for i in range(9):
        dot_ref[i] = jnp.sum(jnp.where(row == i, dots, 0.0))


def feed_kernel(
    c_ref, g_ref, x_hbm, part_hbm, got_hbm, fs_hbm, bm_hbm, w_ref,
    mid_hbm, grad_ref, act_hbm, dgu_hbm,
    x_ref, part_ref, got_ref, fs_ref, bm_ref, mid_ref, act_ref, dgu_ref,
    n2_ref, n2t_ref, last_ref, last_t_ref, wm, we, wd, gm, ge, gd, in_sem, out_sem, side_sem,
):
    steps = HALF // TILE

    def places(t):
        at = pl.multiple_of(t * TILE, TILE)
        return (
            pl.ds(at, TILE),
            pl.ds(HALF + at, TILE),
            pl.ds(pl.multiple_of(t * 256, 256), 256),
            pl.ds(pl.multiple_of(t * D, 128), D),
        )

    def pairs(t, far, main, more, down):
        at = pl.multiple_of(t * TILE, TILE)
        gate_at, up_at, extra_at, down_at = places(t)
        everything, head, tail = slice(None), pl.ds(0, TILE), pl.ds(TILE, TILE)
        return (
            (far.at[:, pl.ds(at, TILE)], main.at[head, gate_at]),
            (far.at[:, pl.ds(SECOND + at, TILE)], main.at[tail, gate_at]),
            (far.at[:, pl.ds(HALF + at, TILE)], main.at[head, up_at]),
            (far.at[:, pl.ds(SECOND + HALF + at, TILE)], main.at[tail, up_at]),
            (far.at[:, pl.ds(EXTRA + pl.multiple_of(t * 256, 256), 256)], more.at[:, extra_at]),
            (far.at[:, pl.ds(DOWN + pl.multiple_of(t * D, 128), D)], down.at[:, down_at]),
        )

    def loads(t):
        return [
            pltpu.make_async_copy(far, near, in_sem.at[t, i])
            for i, (far, near) in enumerate(pairs(t, w_ref, wm, we, wd))
        ]

    def stores(t):
        return [
            pltpu.make_async_copy(near, far, out_sem.at[t, i])
            for i, (far, near) in enumerate(pairs(t, grad_ref, gm, ge, gd))
        ]

    sides = [
        pltpu.make_async_copy(src, dst, side_sem.at[i])
        for i, (src, dst) in enumerate(
            (
                (x_hbm, x_ref), (part_hbm, part_ref), (got_hbm, got_ref),
                (fs_hbm, fs_ref), (bm_hbm, bm_ref), (mid_ref, mid_hbm),
                (act_ref, act_hbm), (dgu_ref, dgu_hbm),
            )
        )
    ]
    for copy in sides[:5] + loads(0):
        copy.start()
    for copy in sides[:3]:
        copy.wait()
    for t in range(1, steps):
        for copy in loads(t):
            copy.start()

    first = c_ref[0] == 0
    part, got = part_ref[:, :OWN], got_ref[:, :OWN].astype(F32)
    low = jnp.where(first, part, got)
    high = jnp.where(first, got, part)
    middle = x_ref[...].astype(F32) + jnp.concatenate([low, high], axis=1)
    mid_ref[...] = middle
    sides[5].start()
    hat, _ = normal(middle)
    normed = (hat * g_ref[...]).astype(BF)
    for copy in sides[3:5]:
        copy.wait()
    n2_ref[...] = mm_t(normed, fs_ref[...]).astype(BF)
    n2t_ref[...] = n2_ref[...].T
    lane = lax.broadcasted_iota(jnp.int32, (TOK, TILE), 1) % 4
    row = lax.broadcasted_iota(jnp.int32, (TILE, TOK), 0) % 4
    last = n2_ref[:, 2 * TILE :].astype(F32)
    last_t = n2t_ref[2 * TILE :, :].astype(F32)
    for m in range(4):
        at = slice(m * TOK, m * TOK + TOK)
        last_ref[at, :] = jnp.where(lane == m, last, 0.0).astype(BF)
        last_t_ref[:, at] = jnp.where(row == m, last_t, 0.0).astype(BF)

    def step(t, carry):
        for copy in loads(t):
            copy.wait()
        gate_at, up_at, extra_at, down_at = places(t)
        rows, bm = n2_ref[:, : 2 * TILE], bm_ref[...]
        more = mm(last_ref[...], we[:, extra_at])
        parts = [more[m * TOK : m * TOK + TOK] for m in range(4)]
        gate = mm(rows, wm[:, gate_at]) + jnp.concatenate(parts[:2], axis=1)
        up = mm(rows, wm[:, up_at]) + jnp.concatenate(parts[2:], axis=1)
        dact = mm_t(bm, wd[:, down_at])
        sig = jax.nn.sigmoid(gate)
        silu = gate * sig
        act = (silu * up).astype(BF)
        dgate = (dact * up * (sig * (1.0 + gate * (1.0 - sig)))).astype(BF)
        dup = (dact * silu).astype(BF)
        act_ref[:, gate_at] = act
        dgu_ref[:, gate_at] = dgate
        dgu_ref[:, up_at] = dup
        rows_t, out = n2t_ref[: 2 * TILE, :], stores(t)
        gm[:, gate_at] = mm(rows_t, dgate).astype(BF)
        for copy in out[:2]:
            copy.start()
        gm[:, up_at] = mm(rows_t, dup).astype(BF)
        for copy in out[2:4]:
            copy.start()
        four = jnp.concatenate(
            [dgate[:, :256], dgate[:, 256:], dup[:, :256], dup[:, 256:]], axis=0
        )
        ge[:, extra_at] = mm(last_t_ref[...], four).astype(BF)
        out[4].start()
        gd[:, down_at] = inner(act, bm).astype(BF)
        out[5].start()
        return carry

    lax.fori_loop(0, steps, step, 0)
    for copy in sides[6:]:
        copy.start()
    for copy in sides[5:]:
        copy.wait()
    for t in range(steps):
        for copy in stores(t):
            copy.wait()


def feed_back_kernel(
    dgu_hbm, w_ref, fs_hbm, dn2_ref, low_ref,
    dgu_ref, fs_ref, wb, dgt_ref, four_ref, slots_ref, sem, side_sem,
):
    rows_each = 128
    steps = TILE // rows_each

    def load(t):
        rows = pl.ds(pl.multiple_of(t * rows_each, rows_each), rows_each)
        return pltpu.make_async_copy(w_ref.at[rows, pl.ds(0, DOWN)], wb.at[rows, :], sem.at[t])

    sides = [
        pltpu.make_async_copy(dgu_hbm, dgu_ref, side_sem.at[0]),
        pltpu.make_async_copy(fs_hbm, fs_ref, side_sem.at[1]),
    ]
    sides[0].start()
    for t in range(steps):
        load(t).start()
    sides[1].start()
    sides[0].wait()
    dgt_ref[...] = dgu_ref[...].T
    for m in range(4):
        for group in range(3):
            at = (m // 2) * HALF + group * TILE + (m % 2) * 256
            four_ref[group * 256 : group * 256 + 256, m * TOK : m * TOK + TOK] = dgt_ref[
                at : at + 256, :
            ]

    def step(t, carry):
        load(t).wait()
        at = pl.multiple_of(t * rows_each, rows_each)
        rows = pl.ds(at, rows_each)
        dgt = dgt_ref[...]
        slots_ref[rows, :] = mm(wb[rows, :SECOND], dgt).astype(BF)
        slots_ref[pl.ds(TILE + at, rows_each), :] = mm(wb[rows, SECOND:EXTRA], dgt).astype(BF)
        more = mm(wb[rows, EXTRA:], four_ref[...])
        row = lax.broadcasted_iota(jnp.int32, (rows_each, TOK), 0) % 4
        last = jnp.zeros((rows_each, TOK), F32)
        for m in range(4):
            last = jnp.where(row == m, more[:, m * TOK : m * TOK + TOK], last)
        slots_ref[pl.ds(2 * TILE + at, rows_each), :] = last.astype(BF)
        return carry

    lax.fori_loop(0, steps, step, 0)
    sides[1].wait()
    dn2 = inner(slots_ref[...], fs_ref[...])
    dn2_ref[...] = dn2
    low_ref[...] = dn2.astype(BF)


def down_kernel(act_ref, w_ref, down_ref, wb, sem):
    load = pltpu.make_async_copy(w_ref.at[:, pl.ds(DOWN, 3 * D)], wb, sem)
    load.start()
    load.wait()
    total = mm(act_ref[:, :TILE], wb[:, :D])
    for group in (1, 2):
        total = total + mm(
            act_ref[:, group * TILE : group * TILE + TILE], wb[:, group * D : group * D + D]
        )
    down_ref[...] = total


def middle_back_kernel(
    c_ref, part_ref, got_ref, mid_ref, cot_ref, g_ref, kf_ref, w_ref,
    dmid_ref, ba_ref, do_ref, other_ref,
):
    c = c_ref[0]
    dn2 = part_ref[...] + got_ref[...].astype(F32)
    hat, scale = normal(mid_ref[...])
    dmiddle = cot_ref[...] + normal_pull(hat, scale, dn2 * g_ref[...])
    dmid_ref[...] = dmiddle
    ba = kf_ref[...] * dmiddle
    half = jnp.where(c == 0, ba[:, :576], ba[:, 576:]).astype(BF)
    ba_ref[:, :OWN] = half
    ba_ref[:, OWN:] = jnp.zeros((TOK, LANES - OWN), BF)
    do_ref[...] = mm_t(half, out_rows(w_ref, c)[...])
    other_ref[:, :OWN] = mm_t(half, out_rows(w_ref, 1 - c)[...]).astype(BF)
    other_ref[:, OWN:] = jnp.zeros((TOK, LANES - OWN), BF)


def on_device(
    tokens, doc_ids, keep, gain_one, wq, wk, wv, wo, gain_two, wg, wu, wd, cotangent
):
    y, z, c = lax.axis_index("y"), lax.axis_index("z"), lax.axis_index("c")
    xl = lax.axis_index("xl")
    x = lax.axis_index("xh") * 2 + xl
    first_core = c == 0

    def both(own, other):
        return jnp.where(first_core, jnp.stack([own, other]), jnp.stack([other, own]))

    r = lax.broadcasted_iota(jnp.int32, (72, 96), 0)
    s = lax.broadcasted_iota(jnp.int32, (72, 96), 1)
    xh_r, rest = r // 36, r % 36
    c_r, rest = rest // 18, rest % 18
    xl_r, i_r = rest // 9, rest % 9
    k_r = lax.rem(xh_r * 2 + xl_r - x + 4, 4)
    select = (s == k_r * 24 + jnp.where(c_r == c, 0, 9) + i_r).astype(BF)

    def rows72(block):
        stacked = jnp.concatenate(
            [block, send(block, ("x", -1)), send(block, ("x", 2)), send(block, ("x", 1))], axis=0
        )
        return mm(select, stacked).astype(BF)

    def gather_zy(block):
        return gather_ring(
            gather_direct(block, "z", z, 0).reshape(288, -1), "y", y, 0
        ).reshape(D, -1)

    def gather_yz(block):
        return gather_ring(gather_direct(block, "y", y, 0), "z", z, 1).reshape(D, -1)

    core = c.astype(jnp.int32).reshape(1)
    both_cols = FF + 2 * PART
    both_gains = jnp.stack([gain_one, gain_two]).astype(F32)
    own, other = call(
        split_kernel,
        [((9, both_cols), BF), ((9, both_cols), BF)],
        (core, both_gains, wg, wu, wq, wk, wv, wo),
        8 * 9 * 768 * 768 * 2,
        scratch=[pltpu.VMEM((128, 768), BF)],
        places={0: SMEM, 1: SMEM} | {i: FAR for i in range(2, 8)},
    )
    feed_block, a_block = call(
        pack_kernel,
        [((8, WIDE), BF), ((24, 2 * PART), BF)],
        (core, own, send(other, "c"), wd),
        1,
        places={0: SMEM, 3: FAR},
    )
    feed_w = lax.all_gather(feed_block, CHIPS, axis=0, tiled=True)

    marks = jnp.stack([doc_ids, keep])
    a_block, x_got, marks_got, cot_got = lax.optimization_barrier(
        (a_block,) + tuple(send(v, "c") for v in (tokens, marks, cotangent))
    )
    x_all = both(tokens, x_got).reshape(TOK, D)
    marks = both(marks, marks_got)
    docs, kf = marks[:, 0].astype(F32), marks[:, 1].astype(F32).reshape(TOK, 1)
    doc_args = (docs.reshape(TOK, 1), docs.reshape(2, 1, ROWS))
    doc_rows = jnp.pad(docs, ((0, 14), (0, 384 - ROWS))).astype(BF)
    cot = both(cotangent, cot_got).reshape(TOK, D)

    a72 = rows72(a_block)
    slot = jnp.arange(SLOTS, dtype=jnp.int32)
    chip, inside = slot % TILE // 8, slot % 8
    inside = jnp.where(slot < 2 * TILE, slot // TILE * 8 + inside, 16 + inside // 4)
    of_slot = (chip // 2) * 36 + (inside // 9) * 18 + (chip % 2) * 9 + inside % 9
    spot = jnp.arange(D, dtype=jnp.int32)
    along, plane, inside = spot // 288, (spot % 288) // 18, spot % 18
    of_x = plane * 72 + (along // 2) * 36 + (inside // 9) * 18 + (along % 2) * 9 + inside % 9
    spot = jnp.arange(288, dtype=jnp.int32)
    of_z = ((spot % 72) // 18 * 4 + spot // 72) * 18 + spot % 18
    spot = jnp.arange(96, dtype=jnp.int32)
    of_y = jnp.where(spot % 24 < 18, spot // 24 * 18 + spot % 24, -1)
    orders, a72 = lax.optimization_barrier(((of_slot, of_x, of_z, of_y), a72))

    def one_hot(rows, columns):
        return (
            rows[:, None] == lax.broadcasted_iota(jnp.int32, (rows.shape[0], columns), 1)
        ).astype(BF)

    from_slots, by_x, by_z, by_y = [
        one_hot(rows, columns) for rows, columns in zip(orders, (D, D, 288, 72))
    ]

    qk_w = gather_zy(a72[:, :PART])
    vo_w = gather_yz(a72[:, PART:])

    lane = lax.broadcasted_iota(jnp.int32, (ROWS, 128), 1)
    spot = lax.broadcasted_iota(jnp.int32, (ROWS, 128), 0) + xl * ROWS
    freqs = 10000.0 ** (-((lane % (HD // 2)).astype(F32) * 2.0 / HD))
    angle = spot.astype(F32) * freqs
    cosine = jnp.cos(angle)
    sine = jnp.where(lane % HD < HD // 2, -1.0, 1.0) * jnp.sin(angle)
    bm = (kf * cot).astype(BF)
    early_work = (x_all, from_slots, bm, cosine, sine, kf, cot, by_x, doc_rows) + doc_args
    early_work, a_blocks = lax.optimization_barrier((early_work, (qk_w, vo_w)))
    x_all, from_slots, bm, cosine, sine, kf, cot, by_x, doc_rows = early_work[:9]
    late = (xl == 1).astype(jnp.int32).reshape(1)
    doc_args = (late,) + early_work[9:]
    qk_w, vo_w = a_blocks

    gains, n1, qk, kv = call(
        project_kernel,
        [((8, D), F32), ((TOK, D), BF), ((TOK, 768), BF), ((TOK + 16, 384), BF)],
        (x_all, qk_w, vo_w, cosine, sine, doc_rows),
        2 * TOK * D * 1024,
        scratch=[
            pltpu.VMEM((TOK, 768), F32),
            pltpu.VMEM((TOK, VPAD), BF),
        ],
        places={0: FAR, 7: FAR, 8: FAR, 9: FAR},
        megabytes=12,
    )
    g1, g2 = gains[0:1], gains[1:2]
    n1_x = mm_t(by_x, n1).astype(BF).reshape(4, 288, TOK)
    kv_early, n1_x = lax.optimization_barrier((send(kv, "late"), n1_x))
    o, out_own = call(
        attend_kernel,
        [((TOK, LANES), BF), ((TOK, OWN), F32)],
        (qk, kv, kv_early) + doc_args + (core, vo_w),
        4 * TOK * 576 * 256,
        scratch=[
            pltpu.VMEM((16, ROWS), F32),
            pltpu.VMEM((OWN, OWN), BF),
            pltpu.SemaphoreType.DMA,
        ],
        places={0: FAR, 1: FAR, 3: SMEM, 6: SMEM, 7: HERE, 8: FAR},
        megabytes=12,
    )
    o_got = send(o, "c")
    part, part_low = call(
        out_kernel,
        [((TOK, LANES), F32), ((TOK, LANES), BF)],
        (core, out_own, o_got, vo_w, kf),
        2 * TOK * OWN * OWN,
        scratch=[pltpu.VMEM((OWN, OWN), BF), pltpu.SemaphoreType.DMA],
        places={0: SMEM, 3: HERE, 5: FAR},
        megabytes=12,
    )
    o_all = jnp.where(
        first_core,
        jnp.concatenate([o[:, :OWN], o_got[:, :OWN]], axis=1),
        jnp.concatenate([o_got[:, :OWN], o[:, :OWN]], axis=1),
    )
    o_x = mm_t(by_x, o_all).astype(BF).reshape(4, 288, TOK)
    part_got, o_x = lax.optimization_barrier((send(part_low, "c"), o_x))
    middle, feed_grad, act, dgu = call(
        feed_kernel,
        [((TOK, D), F32), ((TILE, WIDE), BF), ((TOK, HALF), BF), ((TOK, FF), BF)],
        (core, g2, x_all, part, part_got, from_slots, bm, feed_w),
        4 * TOK * SLOTS * (WIDE + D),
        scratch=[
            pltpu.VMEM((TOK, D), BF),
            pltpu.VMEM((TOK, LANES), F32),
            pltpu.VMEM((TOK, LANES), BF),
            pltpu.VMEM((SLOTS, D), BF),
            pltpu.VMEM((TOK, D), BF),
            pltpu.VMEM((TOK, D), F32),
            pltpu.VMEM((TOK, HALF), BF),
            pltpu.VMEM((TOK, FF), BF),
            pltpu.VMEM((TOK, SLOTS), BF),
            pltpu.VMEM((SLOTS, TOK), BF),
            pltpu.VMEM((4 * TOK, TILE), BF),
            pltpu.VMEM((TILE, 4 * TOK), BF),
            pltpu.VMEM((2 * TILE, FF), BF),
            pltpu.VMEM((TILE, 768), BF),
            pltpu.VMEM((TILE, 3 * D), BF),
            pltpu.VMEM((2 * TILE, FF), BF),
            pltpu.VMEM((TILE, 768), BF),
            pltpu.VMEM((TILE, 3 * D), BF),
            pltpu.SemaphoreType.DMA((3, 6)),
            pltpu.SemaphoreType.DMA((3, 6)),
            pltpu.SemaphoreType.DMA((8,)),
        ],
        places={0: SMEM} | {i: HERE for i in range(2, 12)},
        megabytes=52,
    )
    feed_sum = lax.psum_scatter(feed_grad, ("y", "z"), scatter_dimension=0, tiled=True)
    dn2_part, dn2_low = call(
        feed_back_kernel,
        [((TOK, D), F32), ((TOK, D), BF)],
        (dgu, feed_w, from_slots),
        2 * TOK * SLOTS * (FF + D),
        scratch=[
            pltpu.VMEM((TOK, FF), BF),
            pltpu.VMEM((SLOTS, D), BF),
            pltpu.VMEM((TILE, DOWN), BF),
            pltpu.VMEM((FF, TOK), BF),
            pltpu.VMEM((768, 4 * TOK), BF),
            pltpu.VMEM((SLOTS, TOK), BF),
            pltpu.SemaphoreType.DMA((4,)),
            pltpu.SemaphoreType.DMA((2,)),
        ],
        megabytes=40,
        places={0: HERE, 1: HERE, 2: HERE},
    )
    dn2_got = send(dn2_low, "c")
    dmiddle, ba_own, do_part, do_other = call(
        middle_back_kernel,
        [((TOK, D), F32), ((TOK, LANES), BF), ((TOK, OWN), F32), ((TOK, LANES), BF)],
        (core, dn2_part, dn2_got, middle, cot, g2, kf, vo_w),
        4 * TOK * D * 576,
        places={0: SMEM, 3: FAR, 4: FAR, 7: FAR, 8: FAR},
    )
    do_got = send(do_other, "c")
    spot_x = x.astype(jnp.int32).reshape(1)
    (out_far,) = call(
        out_far_kernel,
        [((288, LANES), BF)],
        (spot_x, o_x, ba_own),
        2 * 288 * TOK * LANES,
        places={0: SMEM},
    )
    do_got, out_far = lax.optimization_barrier((do_got, out_far))
    out_far = send(out_far, ("x", 2))
    dqk_raw, dv_raw, de = call(
        attend_back_kernel,
        [((TOK, 768), F32), ((TOK, 256), F32), ((TOK, 384), BF)],
        (qk, kv, kv_early) + doc_args + (do_part, do_got),
        10 * TOK * 576 * 256,
        scratch=[pltpu.VMEM((16, ROWS), F32)],
        places={0: FAR, 1: FAR, 2: FAR, 3: SMEM},
    )
    d_got = send(de, "early")
    o_later, de_later = lax.optimization_barrier((o_x, de))
    out_own, out_ahead, out_behind = call(
        out_near_kernel,
        [((288, LANES), BF)] * 3,
        (spot_x, o_later, ba_own),
        6 * 288 * TOK * LANES,
        places={0: SMEM},
    )
    out_ahead, out_behind = send(out_ahead, ("x", 1)), send(out_behind, ("x", -1))
    (dqkv,) = call(
        project_back_kernel,
        [((TOK, 1024), BF)],
        (dqk_raw, dv_raw, d_got, cosine, sine),
        TOK * D * 16,
    )
    grads = (spot_x, n1_x, dqkv)
    low, high = call(
        far_kernel,
        [((144, 1024), BF), ((144, 1024), BF)],
        grads,
        2 * 288 * TOK * 1024,
        places={0: SMEM},
    )
    low, high, act, dqkv_later = lax.optimization_barrier((low, high, act, dqkv))
    (dn1_part,) = call(
        normed_back_kernel,
        [((TOK, D), F32)],
        (dqkv_later, qk_w, vo_w),
        2 * TOK * D * 1024,
        places={1: FAR, 2: FAR},
    )
    dn1_part = dn1_part.reshape(2, ROWS, D)
    low_got, high_got, out_far = lax.optimization_barrier(
        (send(low, ("x", 1)), send(high, ("x", -1)), out_far)
    )
    ahead, behind = call(
        near_kernel,
        [((288, 1024), BF), ((288, 1024), BF)],
        grads + (low_got, high_got),
        4 * 288 * TOK * 1024,
        places={0: SMEM},
    )
    (by_place,) = call(
        own_kernel,
        [((288, 2 * PART), BF)],
        grads + (send(ahead, ("x", 1)), send(behind, ("x", -1)))
        + (out_own, out_ahead, out_behind, out_far, by_z),
        2 * 288 * TOK * 2 * PART,
        scratch=[pltpu.VMEM((288, 2 * PART), BF)],
        places={0: SMEM},
    )
    (down,) = call(
        down_kernel,
        [((TOK, D), F32)],
        (act, feed_w),
        2 * TOK * HALF * D,
        scratch=[pltpu.VMEM((TILE, 3 * D), BF), pltpu.SemaphoreType.DMA],
        places={0: FAR, 1: HERE},
    )
    down = down.reshape(2, ROWS, D)
    down_got = send(pick(down, 0, 1 - c).astype(BF), "c")
    own_kf = pick(kf.reshape(2, ROWS, 1), 0, c)
    mixed = pick(middle.reshape(2, ROWS, D), 0, c) + own_kf * (pick(down, 0, c) + down_got)

    attention_sum = reduce_direct(by_place.astype(F32).reshape(4, 72, 2 * PART), "z", z, 0)
    attention_sum = mm(by_y, attention_sum.astype(BF)).reshape(4, 24, 2 * PART)
    a24 = reduce_direct(attention_sum, "y", y, 0)
    a24, feed_sum = lax.optimization_barrier((a24, feed_sum))
    dn1 = pick(dn1_part, 0, c) + send(pick(dn1_part, 0, 1 - c).astype(BF), "c")
    hat_own, scale_own = normal(tokens.astype(F32))
    back_tokens = pick(dmiddle.reshape(2, ROWS, D), 0, c) + normal_pull(
        hat_own, scale_own, dn1 * g1
    )

    def swap(own, other):
        got = send(other.astype(BF), "c").astype(F32)
        return jnp.where(first_core, own, got), jnp.where(first_core, got, own)

    by_chip = feed_sum.reshape(4, 8, WIDE)
    mine, other_rows, back_down = call(
        unpack_kernel,
        [((9, FF), BF), ((9, FF), BF), ((24, D), F32)],
        (
            core,
            pick(by_chip, 0, x),
            send(pick(by_chip, 0, wrap(x, 1)), ("x", 1)),
            send(pick(by_chip, 0, wrap(x, -1)), ("x", -1)),
            send(pick(by_chip, 0, wrap(x, 2)), ("x", 2)),
        ),
        1,
        places={0: SMEM},
    )
    back_gate, back_up, back_two = call(
        join_kernel,
        [((9, FF), F32), ((9, FF), F32), ((9,), F32)],
        (core, mine, send(other_rows, "c"), wg, wu, both_gains),
        8 * 9 * 768 * 768 * 2,
        scratch=[pltpu.VMEM((128, 768), BF)],
        places={0: SMEM, 3: FAR, 4: FAR, 5: SMEM, 8: SMEM},
    )
    core0, core1 = a24[:9], a24[9:18]
    a0, a1 = swap(jnp.where(first_core, core0, core1), jnp.where(first_core, core1, core0))
    join = lambda low, high: jnp.concatenate([a0[:, low:high], a1[:, low:high]], axis=1)
    back_query = join(192, 768)
    back_key = join(0, 192)
    back_value = join(832, 1024)
    back_out = join(1024, 1600)
    dots = lambda weight, grad: jnp.sum(weight.astype(F32) * grad, axis=1)
    back_one = (
        dots(wq, back_query) + dots(wk, back_key) + dots(wv, back_value)
    ) / gain_one.astype(F32)
    return (
        mixed.astype(BF),
        back_tokens,
        back_one,
        back_query,
        back_key,
        back_value,
        back_out,
        back_two,
        back_gate,
        back_up,
        back_down,
    )


def solution(mesh):
    fine = Mesh(mesh.devices.reshape([SIZES[name] for name in AXES]), AXES)
    row, rows = P(AXES), P(AXES, None)
    in_specs = (rows, row, row, row, rows, rows, rows, rows, row, rows, rows, rows, rows)
    out_specs = (rows, rows, row, rows, rows, rows, rows, row, rows, rows, rows)
    return jax.shard_map(
        on_device, mesh=fine, in_specs=in_specs, out_specs=out_specs, check_vma=False
    )
```
